128 devices in a mesh: patch: 8 (over y, x_lo), hid: 16 (over x_hi, z, core).
Axes of the slice: x: 4 (x_hi: 2, x_lo: 2; x = x_hi * 2 + x_lo), y: 4, z: 4, core: 2. Of those that a mesh axis runs over, the one named last changes fastest.
Arguments:
- frames: bfloat16 [4, 2, 32, 64, 512], P(None, None, 'patch', None, 'hid'), may hold values from -6 to 6
- hidden_start: bfloat16 [2, 32, 64, 512], P(None, 'patch', None, 'hid'), may hold values from -4 to 4
- cell_start: float32 [2, 32, 64, 512], P(None, 'patch', None, 'hid'), may hold values from -6 to 6
- input_weight: bfloat16 [3, 3, 512, 4, 512], P(None, None, None, None, 'hid'), may hold values from -0.09375 to 0.09375
- hidden_weight: bfloat16 [3, 3, 512, 4, 512], P(None, None, None, None, 'hid'), may hold values from -0.09375 to 0.09375
- gate_bias: float32 [4, 512], P(None, 'hid'), may hold values from -3 to 3
- first_weight: bfloat16 [3, 3, 512, 512], replicated, may hold values from -0.09375 to 0.09375
- first_bias: float32 [512], replicated, may hold values from -3 to 3
- second_weight: bfloat16 [3, 3, 512, 512], replicated, may hold values from -0.09375 to 0.09375
- second_bias: float32 [512], replicated, may hold values from -3 to 3
Outputs:
- decoded: bfloat16 [2, 32, 64, 512], P(None, 'patch', 'hid')
- cell_final: float32 [2, 32, 64, 512], P(None, 'patch', None, 'hid')
The draws below stay inside these ranges and needn't reach their ends.
All inputs are finite; a program needn't handle non-finite values.
Results may differ from the reference program's by a relative error of at most 0.0045.
Values may be sent and summed in bfloat16 or wider, within the bound.
A program may use at most 128 MiB of HBM per device.

```python
import jax
import jax.numpy as jnp

C = 512
CIN = 512
W = 64
B = 2
STEPS = 4
H = 32


def shard_levels(stream_key, extent, pieces, low, top_value):
    loudness, own = 1.0, jax.random.fold_in(stream_key, 6)
    for dim, blocks in pieces:
        heights = jnp.exp(jax.random.uniform(jax.random.fold_in(own, dim), (blocks,), jnp.float32, low / len(pieces), top_value / len(pieces)))
        loudness = loudness * jnp.repeat(heights, extent[dim] // blocks).reshape([-1 if axis == dim else 1 for axis in range(len(extent))])
    return loudness


def normal_values(stream_key, shape, scale, limit, shards=(), dtype=jnp.bfloat16):
    level = shard_levels(stream_key, shape, shards, -0.22, 0.18) if shards else 1.0
    entries = jax.random.normal(stream_key, shape, jnp.float32) * scale * level
    return jnp.minimum(jnp.maximum(entries, -limit), limit).astype(dtype)


def setup_inputs(seed: int = 0) -> dict:
    keys = jax.random.split(jax.random.key(seed), 11)
    return {
        "frames": normal_values(keys[0], (STEPS, B, H, W, CIN), 1.0, 6.0, ((2, 8), (4, 16))),
        "hidden_start": normal_values(keys[1], (B, H, W, C), 0.5, 4.0, ((1, 8), (3, 16))),
        "cell_start": normal_values(keys[2], (B, H, W, C), 1.0, 6.0, ((1, 8), (3, 16)), jnp.float32),
        "input_weight": normal_values(keys[3], (3, 3, CIN, 4, C), (9 * CIN) ** -0.5, 0.09375, ((4, 16),)),
        "hidden_weight": normal_values(keys[4], (3, 3, C, 4, C), (9 * C) ** -0.5, 0.09375, ((4, 16),)),
        "gate_bias": normal_values(keys[5], (4, C), 0.5, 3.0, ((1, 16),), jnp.float32),
        "first_weight": normal_values(keys[6], (3, 3, C, C), (9 * C) ** -0.5, 0.09375),
        "first_bias": normal_values(keys[7], (C,), 0.5, 3.0, (), jnp.float32),
        "second_weight": normal_values(keys[8], (3, 3, C, C), (9 * C) ** -0.5, 0.09375),
        "second_bias": normal_values(keys[9], (C,), 0.5, 3.0, (), jnp.float32),
    }


FORGET_BIAS = 1.0


def conv_taps(padded, weight):
    batch_count, padded_rows, padded_cols, channel_count = padded.shape
    row_count = padded_rows - 2
    col_count = padded_cols - 2
    summed = jnp.zeros((batch_count * row_count * col_count, weight.shape[-1]), jnp.float32)
    for tap_row in range(3):
        for tap_col in range(3):
            window = padded[:, tap_row:tap_row + row_count, tap_col:tap_col + col_count, :]
            summed = summed + jnp.dot(window.reshape(-1, channel_count), weight[tap_row, tap_col], preferred_element_type=jnp.float32)
    return summed.reshape(batch_count, row_count, col_count, weight.shape[-1])


def lstm_update(gates, cell):
    shaped = gates.reshape(gates.shape[:-1] + (4, gates.shape[-1] // 4))
    input_gate = jax.nn.sigmoid(shaped[..., 0, :])
    forget_gate = jax.nn.sigmoid(shaped[..., 1, :] + FORGET_BIAS)
    candidate = jnp.tanh(shaped[..., 2, :])
    output_gate = jax.nn.sigmoid(shaped[..., 3, :])
    cell = forget_gate * cell + input_gate * candidate
    hidden = (output_gate * jnp.tanh(cell)).astype(jnp.bfloat16)
    return hidden, cell


def pad_both(image):
    return jnp.pad(image, ((0, 0), (1, 1), (1, 1), (0, 0)))


def reference(frames, hidden_start, cell_start, input_weight, hidden_weight, gate_bias, first_weight, first_bias, second_weight, second_bias):
    wide_input = input_weight.reshape(3, 3, CIN, 4 * C)
    wide_hidden = hidden_weight.reshape(3, 3, C, 4 * C)
    bias_row = gate_bias.reshape(-1)
    hidden = hidden_start
    cell = cell_start
    for time_index in range(STEPS):
        gates = conv_taps(pad_both(frames[time_index]), wide_input) + conv_taps(pad_both(hidden), wide_hidden) + bias_row
        hidden, cell = lstm_update(gates, cell)
    middle = jax.nn.silu(conv_taps(pad_both(hidden), first_weight) + first_bias).astype(jnp.bfloat16)
    decoded = (conv_taps(pad_both(middle), second_weight) + second_bias).astype(jnp.bfloat16)
    return decoded, cell
```

```python
import jax
import jax.numpy as jnp
from jax import lax
from jax.experimental import pallas as pl
from jax.experimental.pallas import tpu as pltpu
from jax.sharding import PartitionSpec as P

STEPS = 4
MESH = pl.DeviceIdType.MESH
F32 = jnp.float32
BF16 = jnp.bfloat16


def swap_halves(tile):
    return jnp.concatenate([tile[..., 64:], tile[..., :64]], axis=-1)


def kernel(
    frames, hidden, cell_in, gate_bias, bias1, bias2, w_in, w_hid, w_first, w_second,
    decoded, cell_out,
    packed, packed_cell, own, edge_top, edge_bot, image, halo_top, halo_bot,
    far_top_out, far_bot_out, far_top, far_bot,
    wi, wh, w1, w2, bias_col, cell, gin, dec_out, dec_in, cell_back,
    w_sem, wx_send, wx_recv, s1_send, s1_recv, c1_send, c1_recv, local_sem,
    x_send, x_recv, ht_send, ht_recv, hb_send, hb_recv, fin_send, fin_recv, c2_send, c2_recv, d_send, d_recv,
):
    patch = lax.axis_index("patch")
    hid = lax.axis_index("hid")
    core = lax.rem(hid, 2)
    grp = hid // 2
    x_hi = grp // 4
    y = patch // 2
    x_lo = lax.rem(patch, 2)
    flip = lax.rem(x_hi + y, 2)
    block = y * 2 + lax.rem(x_lo + flip, 2)

    def holder(blk, g, c):
        by = blk // 2
        lo = lax.rem(lax.rem(blk, 2) + g // 4 + by, 2)
        return (by * 2 + lo, g * 2 + c)

    def trade(c):
        return (y * 2 + lax.rem(x_lo + flip, 2), grp * 2 + c)

    has_up = block > 0
    has_down = block < 7
    sibling = (patch, grp * 2 + 1 - core)

    def peer(d):
        g = lax.rem(grp // 4 + d // 4, 2) * 4 + lax.rem(lax.rem(grp, 4) + lax.rem(d, 4), 4)
        return g

    barrier = pltpu.get_barrier_semaphore()

    def greet(device):
        pl.semaphore_signal(barrier, inc=1, device_id=device, device_id_type=MESH)

    greet(sibling)

    @pl.when(flip == 1)
    def _():
        greet(trade(0))
        greet(trade(1))

    @pl.loop(1, 8)
    def _(d):
        greet(holder(block, peer(d), core))

    @pl.loop(0, 8)
    def _(g):
        @pl.when(has_up)
        def _():
            greet(holder(block - 1, g, core))

        @pl.when(has_down)
        def _():
            greet(holder(block + 1, g, core))

    weight_copies = []
    for k, (src, dst) in enumerate(((w_in, wi), (w_hid, wh))):
        copy = pltpu.make_async_copy(src, dst.at[:, :, core], w_sem.at[k])
        copy.start()
        weight_copies.append(copy)
    for k, (src, dst) in enumerate(((w_first, w1), (w_second, w2))):
        copy = pltpu.make_async_copy(src, dst, w_sem.at[2 + k])
        copy.start()
        weight_copies.append(copy)

    for b in range(2):
        for t in range(STEPS):
            packed[b, t] = jnp.concatenate([frames[t, b, r] for r in (0, 2, 1, 3)], axis=-1)
        packed[b, STEPS] = jnp.concatenate([hidden[b, r] for r in (0, 2, 1, 3)], axis=-1)
        packed_cell[b] = jnp.concatenate([cell_in[b, r] for r in (0, 2, 1, 3)], axis=-1)
    eye = lax.broadcasted_iota(jnp.int32, (32, 32), 0) == lax.broadcasted_iota(jnp.int32, (32, 32), 1)
    for k in range(4):
        column = jnp.sum(jnp.where(eye, gate_bias[k : k + 1, :], 0.0), axis=1, keepdims=True)
        bias_col[core, k * 32 : (k + 1) * 32, :] = jnp.broadcast_to(column, (32, 128))

    @pl.when(block == 0)
    def _():
        halo_top[...] = jnp.zeros_like(halo_top)
        far_top[...] = jnp.zeros_like(far_top)

    @pl.when(block == 7)
    def _():
        halo_bot[...] = jnp.zeros_like(halo_bot)
        far_bot[...] = jnp.zeros_like(far_bot)

    greeted = 1 + 2 * flip + 7 + jnp.where(has_up, 8, 0) + jnp.where(has_down, 8, 0)
    pl.semaphore_wait(barrier, greeted)

    my_rows = pl.ds(pl.multiple_of(core * 32, 32), 32)

    def trade_copies(c, b, rows):
        return (
            pltpu.make_async_remote_copy(
                src_ref=packed.at[b], dst_ref=own.at[0 : STEPS + 1, rows, :],
                send_sem=s1_send.at[b], recv_sem=s1_recv.at[c],
                device_id=trade(b), device_id_type=MESH,
            ),
            pltpu.make_async_remote_copy(
                src_ref=packed_cell.at[b], dst_ref=cell.at[c],
                send_sem=c1_send.at[b], recv_sem=c1_recv.at[c],
                device_id=trade(b), device_id_type=MESH,
            ),
        )

    for b in range(2):
        stays = (flip == 0) & (core == b)

        @pl.when(jnp.logical_not(stays))
        def _(b=b):
            for copy in trade_copies(core, b, my_rows):
                copy.start()

        @pl.when(stays)
        def _(b=b):
            one = pltpu.make_async_copy(packed.at[b], own.at[0 : STEPS + 1, my_rows, :], local_sem.at[0])
            two = pltpu.make_async_copy(packed_cell.at[b], cell.at[core], local_sem.at[1])
            one.start()
            two.start()
            one.wait()
            two.wait()

    def weight_trade(k, src, dst):
        return pltpu.make_async_remote_copy(
            src_ref=src, dst_ref=dst, send_sem=wx_send.at[k], recv_sem=wx_recv.at[k],
            device_id=sibling, device_id_type=MESH,
        )

    trades = [
        weight_trade(0, w_in, wi.at[:, :, core]),
        weight_trade(1, w_hid, wh.at[:, :, core]),
        weight_trade(2, bias_col.at[core], bias_col.at[core]),
    ]
    for copy in trades:
        copy.start()

    for c in range(2):
        stays = (flip == 0) & (core == c)

        @pl.when(jnp.logical_not(stays))
        def _(c=c):
            for copy in trade_copies(c, 0, pl.ds(c * 32, 32)):
                copy.wait_recv()

    half = lax.broadcasted_iota(jnp.int32, (32, 128), 1) < 64
    my_tile = pl.ds(pl.multiple_of(grp * 64, 64), 64)
    my_edge = pl.ds(pl.multiple_of(grp * 32, 32), 32)

    def pack_edges(slot):
        a = own[slot, :, 0:128]
        b = own[slot, :, 128:256]
        edge_top[slot] = jnp.where(half, a[:32], swap_halves(a[32:]))
        edge_bot[slot] = jnp.where(half, swap_halves(b[:32]), b[32:])

    def tile_copy(slot, d):
        return pltpu.make_async_remote_copy(
            src_ref=own.at[slot], dst_ref=image.at[slot, my_tile, 128:384],
            send_sem=x_send.at[slot], recv_sem=x_recv.at[slot],
            device_id=holder(block, peer(d), core), device_id_type=MESH,
        )

    def up_copy(slot, g):
        return pltpu.make_async_remote_copy(
            src_ref=edge_top.at[slot], dst_ref=halo_bot.at[slot, my_edge, :],
            send_sem=ht_send.at[slot], recv_sem=hb_recv.at[slot],
            device_id=holder(block - 1, g, core), device_id_type=MESH,
        )

    def down_copy(slot, g):
        return pltpu.make_async_remote_copy(
            src_ref=edge_bot.at[slot], dst_ref=halo_top.at[slot, my_edge, :],
            send_sem=hb_send.at[slot], recv_sem=ht_recv.at[slot],
            device_id=holder(block + 1, g, core), device_id_type=MESH,
        )

    def send_tiles(slot):
        image[slot, my_tile, 128:384] = own[slot]

        @pl.loop(1, 8)
        def _(k):
            tile_copy(slot, 8 - k).start()

    def broadcast(slot):
        pack_edges(slot)

        @pl.loop(0, 8)
        def _(g):
            @pl.when(has_up)
            def _():
                up_copy(slot, g).start()

            @pl.when(has_down)
            def _():
                down_copy(slot, g).start()

        send_tiles(slot)

    def wait_bytes(ref, sem):
        pltpu.make_async_copy(ref, ref, sem).wait()

    def wait_tiles(slot):
        wait_bytes(image.at[slot, 0:448, 128:384], x_recv.at[slot])

    def wait_sent(slot):
        wait_bytes(image.at[slot, 0:448, 128:384], x_send.at[slot])

        @pl.when(has_up)
        def _():
            wait_bytes(halo_top.at[slot], ht_send.at[slot])

        @pl.when(has_down)
        def _():
            wait_bytes(halo_bot.at[slot], hb_send.at[slot])

    def wait_image(slot):
        wait_tiles(slot)

        @pl.when(has_up)
        def _():
            wait_bytes(halo_top.at[slot], ht_recv.at[slot])

        @pl.when(has_down)
        def _():
            wait_bytes(halo_bot.at[slot], hb_recv.at[slot])

        for g in range(8):
            a0 = image[slot, g * 64 : g * 64 + 32, 128:256]
            a1 = image[slot, g * 64 + 32 : g * 64 + 64, 128:256]
            b0 = image[slot, g * 64 : g * 64 + 32, 256:384]
            b1 = image[slot, g * 64 + 32 : g * 64 + 64, 256:384]
            top = halo_top[slot, g * 32 : g * 32 + 32, :]
            bot = halo_bot[slot, g * 32 : g * 32 + 32, :]
            image[slot, g * 64 : g * 64 + 32, 0:128] = jnp.where(half, top, swap_halves(b0))
            image[slot, g * 64 + 32 : g * 64 + 64, 0:128] = swap_halves(jnp.where(half, b1, top))
            image[slot, g * 64 : g * 64 + 32, 384:512] = swap_halves(jnp.where(half, bot, a0))
            image[slot, g * 64 + 32 : g * 64 + 64, 384:512] = jnp.where(half, swap_halves(a1), bot)

    place = lax.rem(lax.broadcasted_iota(jnp.int32, (256, 128), 1), 64)

    def conv(slot, weight, write):
        parts = []
        for q in range(3):
            total = None
            for p in range(3):
                lhs = weight[p, q].reshape(256, 512)
                term = jnp.dot(lhs, image[slot, :, p * 128 : p * 128 + 256], preferred_element_type=F32)
                total = term if total is None else total + term
            parts.append(total)
        for tile in range(2):
            lanes = slice(tile * 128, (tile + 1) * 128)
            left = jnp.where(place == 0, 0.0, pltpu.roll(parts[0][:, lanes], 1, 1))
            right = jnp.where(place == 63, 0.0, pltpu.roll(parts[2][:, lanes], 127, 1))
            write(lanes, parts[1][:, lanes] + left + right)

    broadcast(0)
    broadcast(STEPS)
    weight_copies[0].wait()
    weight_copies[1].wait()
    for k, copy in enumerate(trades):
        copy.wait_recv()

    def write_gin(lanes, value):
        for c in range(2):
            rows = slice(c * 128, (c + 1) * 128)
            gin[rows, lanes] = value[rows] + bias_col[c]

    def update(next_slot):
        def write(lanes, value):
            gates = value + gin[:, lanes]
            for c in range(2):
                z = [gates[c * 128 + k * 32 : c * 128 + (k + 1) * 32] for k in range(4)]
                new = jax.nn.sigmoid(z[1] + 1.0) * cell[c, :, lanes] + jax.nn.sigmoid(z[0]) * jnp.tanh(z[2])
                cell[c, :, lanes] = new
                own[next_slot, c * 32 : (c + 1) * 32, lanes] = (jax.nn.sigmoid(z[3]) * jnp.tanh(new)).astype(BF16)

        return write

    def step(t, carry):
        slot = STEPS + lax.rem(t, 2)
        following = STEPS + lax.rem(t + 1, 2)

        @pl.when(t < STEPS - 1)
        def _():
            broadcast(t + 1)

        wait_image(t)
        conv(t, wi, write_gin)
        wait_image(slot)

        @pl.when(t > 0)
        def _():
            wait_sent(following)

        conv(slot, wh, update(following))

        @pl.when(t < STEPS - 1)
        def _():
            broadcast(following)

        return carry

    lax.fori_loop(0, STEPS, step, 0)

    last = STEPS + STEPS % 2
    wide = lax.broadcasted_iota(jnp.int32, (64, 128), 1) < 64
    row_a = own[last, :, 0:128]
    row_b = own[last, :, 128:256]
    far_top_out[...] = jnp.where(wide, row_a, swap_halves(row_b))
    far_bot_out[...] = jnp.where(wide, swap_halves(row_a), row_b)

    def far_up_copy(g):
        return pltpu.make_async_remote_copy(
            src_ref=far_top_out, dst_ref=far_bot.at[my_tile, :],
            send_sem=fin_send.at[0], recv_sem=fin_recv.at[0],
            device_id=holder(block - 1, g, core), device_id_type=MESH,
        )

    def far_down_copy(g):
        return pltpu.make_async_remote_copy(
            src_ref=far_bot_out, dst_ref=far_top.at[my_tile, :],
            send_sem=fin_send.at[1], recv_sem=fin_recv.at[1],
            device_id=holder(block + 1, g, core), device_id_type=MESH,
        )

    @pl.loop(0, 8)
    def _(g):
        @pl.when(has_up)
        def _():
            far_up_copy(g).start()

        @pl.when(has_down)
        def _():
            far_down_copy(g).start()

    send_tiles(last)

    def cell_copy(c, b):
        return pltpu.make_async_remote_copy(
            src_ref=cell.at[c], dst_ref=cell_back.at[b],
            send_sem=c2_send.at[c], recv_sem=c2_recv.at[b],
            device_id=trade(c), device_id_type=MESH,
        )

    for c in range(2):
        stays = (flip == 0) & (core == c)

        @pl.when(jnp.logical_not(stays))
        def _(c=c):
            cell_copy(c, core).start()

        @pl.when(stays)
        def _(c=c):
            copy = pltpu.make_async_copy(cell.at[c], cell_back.at[core], local_sem.at[1])
            copy.start()
            copy.wait()

    weight_copies[2].wait()
    weight_copies[3].wait()
    wait_tiles(last)

    @pl.when(has_down)
    def _():
        wait_bytes(far_bot, fin_recv.at[0])

    @pl.when(has_up)
    def _():
        wait_bytes(far_top, fin_recv.at[1])

    sel_row = lax.broadcasted_iota(jnp.int32, (32, 128), 0)
    sel_lane = lax.broadcasted_iota(jnp.int32, (32, 128), 1)
    want = lax.rem(sel_row, 16) + grp * 8 - 2
    chosen = (want >= 0) & (want < 64) & (sel_lane == want + 64 * (sel_row // 16))
    pick = jnp.where(chosen, 1.0, 0.0).astype(BF16)

    def window(tile):
        return lax.dot_general(pick, tile, (((1,), (1,)), ((), ())), preferred_element_type=F32).astype(BF16)

    above = window(far_top[...])
    tile_a = window(image[last, :, 128:256])
    tile_b = window(image[last, :, 256:384])
    below = window(far_bot[...])
    pixels = jnp.concatenate([above, tile_a[:16], tile_b[:16], tile_a[16:], tile_b[16:], below], axis=0)

    def decode(source, rows, weight):
        parts = []
        for q in range(3):
            total = None
            for p in range(3):
                term = jnp.dot(source[p * 16 : p * 16 + rows * 16], weight[p, q], preferred_element_type=F32)
                total = term if total is None else total + term
            parts.append(total)
        return parts[1] + pltpu.roll(parts[0], 1, 0) + pltpu.roll(parts[2], rows * 16 - 1, 0)

    first = decode(pixels, 6, w1) + bias1[...]
    first = first / (1.0 + jnp.exp(-first))
    pixel = lax.broadcasted_iota(jnp.int32, (96, 512), 0)
    image_row = block * 4 - 1 + pixel // 16
    image_col = grp * 8 - 2 + lax.rem(pixel, 16)
    inside = (image_row >= 0) & (image_row < 32) & (image_col >= 0) & (image_col < 64)
    middle = jnp.where(inside, first, 0.0).astype(BF16)
    second = decode(middle, 4, w2) + bias2[...]
    shifted = second.reshape(4, 16, 512)
    for c in range(2):
        dec_out[c] = shifted[:, 2 + 4 * c : 6 + 4 * c, :].astype(BF16)

    def dec_copy(c, b):
        return pltpu.make_async_remote_copy(
            src_ref=dec_out.at[c], dst_ref=dec_in.at[b],
            send_sem=d_send.at[c], recv_sem=d_recv.at[b],
            device_id=trade(c), device_id_type=MESH,
        )

    for c in range(2):
        stays = (flip == 0) & (core == c)

        @pl.when(jnp.logical_not(stays))
        def _(c=c):
            dec_copy(c, core).start()

        @pl.when(stays)
        def _(c=c):
            dec_in[core] = dec_out[c]

    for b in range(2):
        stays = (flip == 0) & (core == b)

        @pl.when(jnp.logical_not(stays))
        def _(b=b):
            cell_copy(0, b).wait_recv()

        for r in range(4):
            start = (r % 2) * 128 + (r // 2) * 64
            cell_out[b, r] = cell_back[b, :, start : start + 64]

    for slot in range(STEPS):
        wait_sent(slot)
    wait_sent(STEPS + 1)
    wait_bytes(image.at[last, 0:448, 128:384], x_send.at[last])

    @pl.when(has_up)
    def _():
        wait_bytes(far_top, fin_send.at[0])

    @pl.when(has_down)
    def _():
        wait_bytes(far_bot, fin_send.at[1])

    for copy in trades:
        copy.wait_send()

    for b in range(2):
        stays = (flip == 0) & (core == b)

        @pl.when(jnp.logical_not(stays))
        def _(b=b):
            for copy in trade_copies(core, b, my_rows):
                copy.wait_send()
            cell_copy(b, core).wait_send()
            dec_copy(0, b).wait_recv()
            dec_copy(b, core).wait_send()

        decoded[b] = dec_in[b]


def per_device(
    frames, hidden_start, cell_start, input_weight, hidden_weight, gate_bias,
    first_weight, first_bias, second_weight, second_bias,
):
    vmem = pl.BlockSpec(memory_space=pltpu.VMEM)
    anywhere = pl.BlockSpec(memory_space=pl.ANY)
    dma = pltpu.SemaphoreType.DMA
    slots = STEPS + 2

    def gate_rows(weight):
        return weight.transpose(0, 1, 3, 4, 2).reshape(3, 3, 128, 512)

    decoded, cell = pl.pallas_call(
        kernel,
        name="convlstm",
        out_shape=(
            jax.ShapeDtypeStruct((2, 4, 4, 512), BF16),
            jax.ShapeDtypeStruct((2, 4, 32, 64), F32),
        ),
        in_specs=[vmem] * 6 + [anywhere] * 4,
        out_specs=(vmem, vmem),
        scratch_shapes=[
            pltpu.VMEM((2, STEPS + 1, 32, 256), BF16),
            pltpu.VMEM((2, 32, 256), F32),
            pltpu.VMEM((slots, 64, 256), BF16),
            pltpu.VMEM((slots, 32, 128), BF16),
            pltpu.VMEM((slots, 32, 128), BF16),
            pltpu.VMEM((slots, 512, 512), BF16),
            pltpu.VMEM((slots, 256, 128), BF16),
            pltpu.VMEM((slots, 256, 128), BF16),
            pltpu.VMEM((64, 128), BF16),
            pltpu.VMEM((64, 128), BF16),
            pltpu.VMEM((512, 128), BF16),
            pltpu.VMEM((512, 128), BF16),
            pltpu.VMEM((3, 3, 2, 128, 512), BF16),
            pltpu.VMEM((3, 3, 2, 128, 512), BF16),
            pltpu.VMEM((3, 3, 512, 512), BF16),
            pltpu.VMEM((3, 3, 512, 512), BF16),
            pltpu.VMEM((2, 128, 128), F32),
            pltpu.VMEM((2, 32, 256), F32),
            pltpu.VMEM((256, 256), F32),
            pltpu.VMEM((2, 4, 4, 512), BF16),
            pltpu.VMEM((2, 4, 4, 512), BF16),
            pltpu.VMEM((2, 32, 256), F32),
            dma((4,)), dma((3,)), dma((3,)), dma((2,)), dma((2,)), dma((2,)), dma((2,)), dma((2,)),
            dma((slots,)), dma((slots,)), dma((slots,)), dma((slots,)), dma((slots,)), dma((slots,)),
            dma((2,)), dma((2,)), dma((2,)), dma((2,)), dma((2,)), dma((2,)),
        ],
        compiler_params=pltpu.CompilerParams(
            collective_id=0, has_side_effects=True, vmem_limit_bytes=50 << 20
        ),
    )(
        frames.transpose(0, 1, 2, 4, 3),
        hidden_start.transpose(0, 1, 3, 2),
        cell_start.transpose(0, 1, 3, 2),
        gate_bias,
        first_bias.reshape(1, -1),
        second_bias.reshape(1, -1),
        gate_rows(input_weight),
        gate_rows(hidden_weight),
        first_weight,
        second_weight,
    )
    return decoded, cell.transpose(0, 1, 3, 2)


def solution(mesh):
    return jax.shard_map(
        per_device,
        mesh=mesh,
        in_specs=(
            P(None, None, "patch", None, "hid"),
            P(None, "patch", None, "hid"),
            P(None, "patch", None, "hid"),
            P(None, None, None, None, "hid"),
            P(None, None, None, None, "hid"),
            P(None, "hid"),
            P(),
            P(),
            P(),
            P(),
        ),
        out_specs=(P(None, "patch", "hid", None), P(None, "patch", None, "hid")),
        check_vma=False,
    )
```

```python
import jax
import jax.numpy as jnp
from jax import lax
from jax.experimental import pallas as pl
from jax.experimental.pallas import tpu as pltpu
from jax.sharding import PartitionSpec as P

STEPS = 4
FAR_FIRST = (6, 5, 7, 2, 4, 1, 3)
MESH = pl.DeviceIdType.MESH
F32 = jnp.float32
BF16 = jnp.bfloat16


def swap_halves(tile):
    return jnp.concatenate([tile[..., 64:], tile[..., :64]], axis=-1)


def kernel(
    frames_hbm, hidden_hbm, cell_hbm, gate_bias_hbm, bias1_hbm, bias2_hbm, w_in, w_hid, w_first, w_second,
    decoded, cell_out,
    frames, hidden, cell_in, gate_bias, bias1, bias2,
    packed, packed_cell, own, edge_top, edge_bot, image, halo_top, halo_bot,
    far_top_out, far_bot_out, far_top, far_bot, frame_top, frame_bot,
    wi, wh, w1, w2, bias_col, cell, gin, dec_out, dec_in, cell_back,
    in_sem, w_sem, wx_send, wx_recv, s_send, s_recv, f_send, f_recv,
    x_send, x_recv, ht_send, ht_recv, hb_send, hb_recv, fin_send, fin_recv, c2_send, c2_recv, d_send, d_recv,
):
    patch = lax.axis_index("patch")
    hid = lax.axis_index("hid")
    core = lax.rem(hid, 2)
    grp = hid // 2
    x_hi = grp // 4
    y = patch // 2
    x_lo = lax.rem(patch, 2)
    flip = lax.rem(x_hi + y, 2)
    block = y * 2 + lax.rem(x_lo + flip, 2)

    def holder(blk, g, c):
        by = blk // 2
        lo = lax.rem(lax.rem(blk, 2) + g // 4 + by, 2)
        return (by * 2 + lo, g * 2 + c)

    def trade(c):
        return (y * 2 + lax.rem(x_lo + flip, 2), grp * 2 + c)

    has_up = block > 0
    has_down = block < 7
    sibling = (patch, grp * 2 + 1 - core)
    z = lax.rem(grp, 4)
    group_patch = [holder(block, g, 0)[0] for g in (0, 4)]
    up_patch = [holder(block - 1, g, 0)[0] for g in (0, 4)]
    down_patch = [holder(block + 1, g, 0)[0] for g in (0, 4)]
    cross_patch = jnp.where(x_hi == 0, group_patch[1], group_patch[0])

    def peer(d):
        hi = 1 - x_hi if d >= 4 else x_hi
        return (cross_patch if d >= 4 else patch, (hi * 4 + lax.rem(z + d % 4, 4)) * 2 + core)

    above_same = (jnp.where(x_hi == 0, up_patch[0], up_patch[1]), hid)
    below_same = (jnp.where(x_hi == 0, down_patch[0], down_patch[1]), hid)

    def above(g):
        return (up_patch[g // 4], g * 2 + core)

    def below(g):
        return (down_patch[g // 4], g * 2 + core)

    in_copies = []
    loads = (
        (frames_hbm, frames), (hidden_hbm, hidden), (cell_hbm, cell_in),
        (gate_bias_hbm, gate_bias), (bias1_hbm, bias1), (bias2_hbm, bias2),
    )
    for k, (src, dst) in enumerate(loads):
        copy = pltpu.make_async_copy(src, dst, in_sem.at[k])
        copy.start()
        in_copies.append(copy)

    barrier = pltpu.get_barrier_semaphore()

    def greet(device):
        pl.semaphore_signal(barrier, inc=1, device_id=device, device_id_type=MESH)

    greet(sibling)

    @pl.when(flip == 1)
    def _():
        greet(trade(0))
        greet(trade(1))

    for d in FAR_FIRST:
        greet(peer(d))

    @pl.when(has_up)
    def _():
        for g in range(8):
            greet(above(g))

    @pl.when(has_down)
    def _():
        for g in range(8):
            greet(below(g))

    weight_copies = []
    for k, (src, dst) in enumerate(((w_in, wi), (w_hid, wh))):
        copy = pltpu.make_async_copy(src, dst.at[:, :, core], w_sem.at[k])
        copy.start()
        weight_copies.append(copy)
    for k, (src, dst) in enumerate(((w_first, w1), (w_second, w2))):
        copy = pltpu.make_async_copy(src, dst, w_sem.at[2 + k])
        copy.start()
        weight_copies.append(copy)

    for copy in in_copies:
        copy.wait()
    for b in range(2):
        packed[b, 0] = jnp.concatenate([hidden[b, r] for r in (0, 2, 1, 3)], axis=-1)
        for t in range(STEPS):
            packed[b, 1 + t] = jnp.concatenate([frames[t, b, r] for r in (0, 2, 1, 3)], axis=-1)
        packed_cell[b] = jnp.concatenate([cell_in[b, r] for r in (0, 2, 1, 3)], axis=-1)
    eye = lax.broadcasted_iota(jnp.int32, (32, 32), 0) == lax.broadcasted_iota(jnp.int32, (32, 32), 1)
    for k in range(4):
        column = jnp.sum(jnp.where(eye, gate_bias[k : k + 1, :], 0.0), axis=1, keepdims=True)
        bias_col[core, k * 32 : (k + 1) * 32, :] = jnp.broadcast_to(column, (32, 128))

    @pl.when(block == 0)
    def _():
        halo_top[...] = jnp.zeros_like(halo_top)
        far_top[...] = jnp.zeros_like(far_top)

    @pl.when(block == 7)
    def _():
        halo_bot[...] = jnp.zeros_like(halo_bot)
        far_bot[...] = jnp.zeros_like(far_bot)

    greeted = 1 + 2 * flip + 7 + jnp.where(has_up, 8, 0) + jnp.where(has_down, 8, 0)
    pl.semaphore_wait(barrier, greeted)

    my_rows = pl.ds(pl.multiple_of(core * 32, 32), 32)

    def trade_copy(k, c, b, rows):
        src, dst = (
            (lambda: (packed.at[b, 0:2], own.at[1:3, rows, :])),
            (lambda: (packed.at[b, 2:5], own.at[3:6, rows, :])),
            (lambda: (packed_cell.at[b], cell.at[c])),
        )[k]()
        return pltpu.make_async_remote_copy(
            src_ref=src, dst_ref=dst, send_sem=s_send.at[k, b], recv_sem=s_recv.at[k, c],
            device_id=trade(b), device_id_type=MESH,
        )

    def start_trades(kinds):
        for b in range(2):
            stays = (flip == 0) & (core == b)

            @pl.when(jnp.logical_not(stays))
            def _(b=b):
                for k in kinds:
                    trade_copy(k, core, b, my_rows).start()

    def wait_trades(kinds):
        for c in range(2):
            stays = (flip == 0) & (core == c)

            @pl.when(jnp.logical_not(stays))
            def _(c=c):
                for k in kinds:
                    trade_copy(k, c, 0, pl.ds(c * 32, 32)).wait_recv()

    start_trades((0,))

    @pl.when(flip == 0)
    def _():
        own[1:6, my_rows, :] = packed[core]
        cell[core] = packed_cell[core]

    def weight_trade(k, src, dst):
        return pltpu.make_async_remote_copy(
            src_ref=src, dst_ref=dst, send_sem=wx_send.at[k], recv_sem=wx_recv.at[k],
            device_id=sibling, device_id_type=MESH,
        )

    trades = [
        weight_trade(0, w_in, wi.at[:, :, core]),
        weight_trade(1, w_hid, wh.at[:, :, core]),
        weight_trade(2, bias_col.at[core], bias_col.at[core]),
    ]
    for copy in trades:
        copy.start()
    wait_trades((0,))

    half = lax.broadcasted_iota(jnp.int32, (32, 128), 1) < 64
    my_tile = pl.ds(pl.multiple_of(grp * 64, 64), 64)
    my_edge = pl.ds(pl.multiple_of(grp * 32, 32), 32)

    def pack_edges(slot):
        a = own[slot, :, 0:128]
        b = own[slot, :, 128:256]
        edge_top[slot] = jnp.where(half, a[:32], swap_halves(a[32:]))
        edge_bot[slot] = jnp.where(half, swap_halves(b[:32]), b[32:])

    def wait_bytes(ref, sem):
        pltpu.make_async_copy(ref, ref, sem).wait()

    def send(src, dst, send_sem, recv_sem, device):
        pltpu.make_async_remote_copy(
            src_ref=src, dst_ref=dst, send_sem=send_sem, recv_sem=recv_sem, device_id=device, device_id_type=MESH
        ).start()

    def send_tiles(slot, distances):
        for d in distances:
            send(own.at[slot], image.at[slot, my_tile, 128:384], x_send.at[slot], x_recv.at[slot], peer(d))
        image[slot, my_tile, 128:384] = own[slot]

    def broadcast(slot):
        pack_edges(slot)

        @pl.when(has_up)
        def _():
            for g in range(8):
                send(edge_top.at[slot], halo_bot.at[slot, my_edge, :], ht_send.at[slot], hb_recv.at[slot], above(g))

        @pl.when(has_down)
        def _():
            for g in range(8):
                send(edge_bot.at[slot], halo_top.at[slot, my_edge, :], hb_send.at[slot], ht_recv.at[slot], below(g))

        send_tiles(slot, FAR_FIRST)

    def wait_tiles(slot):
        wait_bytes(image.at[slot, 0:448, 128:384], x_recv.at[slot])

    def wait_edges_sent(slot):
        @pl.when(has_up)
        def _():
            wait_bytes(halo_top.at[slot], ht_send.at[slot])

        @pl.when(has_down)
        def _():
            wait_bytes(halo_bot.at[slot], hb_send.at[slot])

    def wait_sent(slot):
        wait_bytes(image.at[slot, 0:448, 128:384], x_send.at[slot])
        wait_edges_sent(slot)

    my_half = pl.ds(pl.multiple_of(x_hi * 256, 256), 256)

    def frame_along_z(t):
        send_tiles(2 + t, (2, 1, 3))

    def frame_along_x(t):
        slot = 2 + t
        wait_bytes(image.at[slot, 0:192, 128:384], x_recv.at[slot])
        block_ref = image.at[slot, my_half, 128:384]
        send(block_ref, block_ref, f_send.at[t], f_recv.at[t], peer(4))

    def frame_edges(t):
        slot = 2 + t
        wait_bytes(image.at[slot, 0:256, 128:384], f_recv.at[t])
        for g in range(8):
            first = slice(g * 64, g * 64 + 32)
            later = slice(g * 64 + 32, g * 64 + 64)
            packed_rows = slice(g * 32, g * 32 + 32)
            frame_top[t, packed_rows] = jnp.where(
                half, image[slot, first, 128:256], swap_halves(image[slot, later, 128:256])
            )
            frame_bot[t, packed_rows] = jnp.where(
                half, swap_halves(image[slot, first, 256:384]), image[slot, later, 256:384]
            )

        @pl.when(has_up)
        def _():
            send(frame_top.at[t], halo_bot.at[slot], ht_send.at[slot], hb_recv.at[slot], above_same)

        @pl.when(has_down)
        def _():
            send(frame_bot.at[t], halo_top.at[slot], hb_send.at[slot], ht_recv.at[slot], below_same)

    def wait_halos(slot):
        @pl.when(has_up)
        def _():
            wait_bytes(halo_top.at[slot], ht_recv.at[slot])

        @pl.when(has_down)
        def _():
            wait_bytes(halo_bot.at[slot], hb_recv.at[slot])

        for g in range(8):
            a0 = image[slot, g * 64 : g * 64 + 32, 128:256]
            a1 = image[slot, g * 64 + 32 : g * 64 + 64, 128:256]
            b0 = image[slot, g * 64 : g * 64 + 32, 256:384]
            b1 = image[slot, g * 64 + 32 : g * 64 + 64, 256:384]
            top = halo_top[slot, g * 32 : g * 32 + 32, :]
            bot = halo_bot[slot, g * 32 : g * 32 + 32, :]
            image[slot, g * 64 : g * 64 + 32, 0:128] = jnp.where(half, top, swap_halves(b0))
            image[slot, g * 64 + 32 : g * 64 + 64, 0:128] = swap_halves(jnp.where(half, b1, top))
            image[slot, g * 64 : g * 64 + 32, 384:512] = swap_halves(jnp.where(half, bot, a0))
            image[slot, g * 64 + 32 : g * 64 + 64, 384:512] = jnp.where(half, swap_halves(a1), bot)

    place = lax.rem(lax.broadcasted_iota(jnp.int32, (256, 128), 1), 64)

    def conv(slot, weight, write):
        def tap(p, q):
            lhs = weight[p, q].reshape(256, 512)
            return jnp.dot(lhs, image[slot, :, p * 128 : p * 128 + 256], preferred_element_type=F32)

        parts = [tap(1, q) for q in range(3)]
        wait_halos(slot)
        parts = [parts[q] + tap(0, q) + tap(2, q) for q in range(3)]
        for tile in range(2):
            lanes = slice(tile * 128, (tile + 1) * 128)
            left = jnp.where(place == 0, 0.0, pltpu.roll(parts[0][:, lanes], 1, 1))
            right = jnp.where(place == 63, 0.0, pltpu.roll(parts[2][:, lanes], 127, 1))
            write(lanes, parts[1][:, lanes] + left + right)

    broadcast(1)
    frame_along_z(0)
    start_trades((1, 2))
    frame_along_x(0)
    wait_trades((1, 2))
    frame_along_z(1)
    frame_edges(0)
    frame_along_z(2)
    frame_along_x(1)
    weight_copies[0].wait()
    weight_copies[1].wait()
    for copy in trades:
        copy.wait_recv()

    def write_gin(lanes, value):
        for c in range(2):
            rows = slice(c * 128, (c + 1) * 128)
            gin[rows, lanes] = value[rows] + bias_col[c]

    def update(next_slot):
        def write(lanes, value):
            gates = value + gin[:, lanes]
            for c in range(2):
                z = [gates[c * 128 + k * 32 : c * 128 + (k + 1) * 32] for k in range(4)]
                new = jax.nn.sigmoid(z[1] + 1.0) * cell[c, :, lanes] + jax.nn.sigmoid(z[0]) * jnp.tanh(z[2])
                cell[c, :, lanes] = new
                own[next_slot, c * 32 : (c + 1) * 32, lanes] = (jax.nn.sigmoid(z[3]) * jnp.tanh(new)).astype(BF16)

        return write

    def step(t, carry):
        slot = lax.rem(t + 1, 2)
        following = lax.rem(t, 2)

        @pl.when(t < STEPS - 3)
        def _():
            frame_along_z(t + 3)

        @pl.when(t < STEPS - 2)
        def _():
            frame_along_x(t + 2)

        @pl.when(t < STEPS - 1)
        def _():
            frame_edges(t + 1)

        conv(2 + t, wi, write_gin)

        @pl.when(t > 0)
        def _():
            wait_sent(following)

        wait_tiles(slot)
        conv(slot, wh, update(following))

        @pl.when(t < STEPS - 1)
        def _():
            broadcast(following)

        return carry

    lax.fori_loop(0, STEPS, step, 0)

    last = (STEPS + 1) % 2
    wide = lax.broadcasted_iota(jnp.int32, (64, 128), 1) < 64
    row_a = own[last, :, 0:128]
    row_b = own[last, :, 128:256]
    far_top_out[...] = jnp.where(wide, row_a, swap_halves(row_b))
    far_bot_out[...] = jnp.where(wide, swap_halves(row_a), row_b)

    @pl.when(has_up)
    def _():
        for g in range(8):
            send(far_top_out, far_bot.at[my_tile, :], fin_send.at[0], fin_recv.at[0], above(g))

    @pl.when(has_down)
    def _():
        for g in range(8):
            send(far_bot_out, far_top.at[my_tile, :], fin_send.at[1], fin_recv.at[1], below(g))

    send_tiles(last, FAR_FIRST)

    def cell_copy(c, b):
        return pltpu.make_async_remote_copy(
            src_ref=cell.at[c], dst_ref=cell_back.at[b],
            send_sem=c2_send.at[c], recv_sem=c2_recv.at[b],
            device_id=trade(c), device_id_type=MESH,
        )

    for c in range(2):
        stays = (flip == 0) & (core == c)

        @pl.when(jnp.logical_not(stays))
        def _(c=c):
            cell_copy(c, core).start()

        @pl.when(stays)
        def _(c=c):
            cell_back[core] = cell[c]

    weight_copies[2].wait()
    weight_copies[3].wait()
    wait_tiles(last)

    @pl.when(has_down)
    def _():
        wait_bytes(far_bot, fin_recv.at[0])

    @pl.when(has_up)
    def _():
        wait_bytes(far_top, fin_recv.at[1])

    sel_row = lax.broadcasted_iota(jnp.int32, (32, 128), 0)
    sel_lane = lax.broadcasted_iota(jnp.int32, (32, 128), 1)
    want = lax.rem(sel_row, 16) + grp * 8 - 2
    chosen = (want >= 0) & (want < 64) & (sel_lane == want + 64 * (sel_row // 16))
    pick = jnp.where(chosen, 1.0, 0.0).astype(BF16)

    def window(tile):
        return lax.dot_general(pick, tile, (((1,), (1,)), ((), ())), preferred_element_type=F32).astype(BF16)

    above = window(far_top[...])
    tile_a = window(image[last, :, 128:256])
    tile_b = window(image[last, :, 256:384])
    below = window(far_bot[...])
    pixels = jnp.concatenate([above, tile_a[:16], tile_b[:16], tile_a[16:], tile_b[16:], below], axis=0)

    def decode(source, rows, weight):
        parts = []
        for q in range(3):
            total = None
            for p in range(3):
                term = jnp.dot(source[p * 16 : p * 16 + rows * 16], weight[p, q], preferred_element_type=F32)
                total = term if total is None else total + term
            parts.append(total)
        return parts[1] + pltpu.roll(parts[0], 1, 0) + pltpu.roll(parts[2], rows * 16 - 1, 0)

    first = decode(pixels, 6, w1) + bias1[...]
    first = first / (1.0 + jnp.exp(-first))
    pixel = lax.broadcasted_iota(jnp.int32, (96, 512), 0)
    image_row = block * 4 - 1 + pixel // 16
    image_col = grp * 8 - 2 + lax.rem(pixel, 16)
    inside = (image_row >= 0) & (image_row < 32) & (image_col >= 0) & (image_col < 64)
    middle = jnp.where(inside, first, 0.0).astype(BF16)
    second = decode(middle, 4, w2) + bias2[...]
    shifted = second.reshape(4, 16, 512)
    for c in range(2):
        dec_out[c] = shifted[:, 2 + 4 * c : 6 + 4 * c, :].astype(BF16)

    def dec_copy(c, b):
        return pltpu.make_async_remote_copy(
            src_ref=dec_out.at[c], dst_ref=dec_in.at[b],
            send_sem=d_send.at[c], recv_sem=d_recv.at[b],
            device_id=trade(c), device_id_type=MESH,
        )

    for c in range(2):
        stays = (flip == 0) & (core == c)

        @pl.when(jnp.logical_not(stays))
        def _(c=c):
            dec_copy(c, core).start()

        @pl.when(stays)
        def _(c=c):
            dec_in[core] = dec_out[c]

    for b in range(2):
        stays = (flip == 0) & (core == b)

        @pl.when(jnp.logical_not(stays))
        def _(b=b):
            cell_copy(0, b).wait_recv()

        for r in range(4):
            start = (r % 2) * 128 + (r // 2) * 64
            cell_out[b, r] = cell_back[b, :, start : start + 64]

    for t in range(STEPS):
        wait_bytes(image.at[2 + t, 0:192, 128:384], x_send.at[2 + t])
        wait_bytes(image.at[2 + t, 0:256, 128:384], f_send.at[t])
        wait_edges_sent(2 + t)
    wait_sent(1 - last)
    wait_bytes(image.at[last, 0:448, 128:384], x_send.at[last])

    @pl.when(has_up)
    def _():
        wait_bytes(far_top, fin_send.at[0])

    @pl.when(has_down)
    def _():
        wait_bytes(far_bot, fin_send.at[1])

    for copy in trades:
        copy.wait_send()

    for b in range(2):
        stays = (flip == 0) & (core == b)

        @pl.when(jnp.logical_not(stays))
        def _(b=b):
            for k in range(3):
                trade_copy(k, core, b, my_rows).wait_send()
            cell_copy(b, core).wait_send()
            dec_copy(0, b).wait_recv()
            dec_copy(b, core).wait_send()

        decoded[b] = dec_in[b]


def per_device(
    frames, hidden_start, cell_start, input_weight, hidden_weight, gate_bias,
    first_weight, first_bias, second_weight, second_bias,
):
    vmem = pl.BlockSpec(memory_space=pltpu.VMEM)
    hbm = pl.BlockSpec(memory_space=pltpu.HBM)
    dma = pltpu.SemaphoreType.DMA
    slots = STEPS + 2

    def gate_rows(weight):
        return weight.transpose(0, 1, 3, 4, 2).reshape(3, 3, 128, 512)

    operands = (
        frames.transpose(0, 1, 2, 4, 3),
        hidden_start.transpose(0, 1, 3, 2),
        cell_start.transpose(0, 1, 3, 2),
        gate_bias,
        first_bias.reshape(1, -1),
        second_bias.reshape(1, -1),
        gate_rows(input_weight),
        gate_rows(hidden_weight),
        first_weight,
        second_weight,
    )
    decoded, cell = pl.pallas_call(
        kernel,
        name="convlstm",
        out_shape=(
            jax.ShapeDtypeStruct((2, 4, 4, 512), BF16),
            jax.ShapeDtypeStruct((2, 4, 32, 64), F32),
        ),
        in_specs=[hbm] * 10,
        out_specs=(vmem, vmem),
        scratch_shapes=[
            pltpu.VMEM((STEPS, 2, 4, 32, 64), BF16),
            pltpu.VMEM((2, 4, 32, 64), BF16),
            pltpu.VMEM((2, 4, 32, 64), F32),
            pltpu.VMEM((4, 32), F32),
            pltpu.VMEM((1, 512), F32),
            pltpu.VMEM((1, 512), F32),
            pltpu.VMEM((2, STEPS + 1, 32, 256), BF16),
            pltpu.VMEM((2, 32, 256), F32),
            pltpu.VMEM((slots, 64, 256), BF16),
            pltpu.VMEM((2, 32, 128), BF16),
            pltpu.VMEM((2, 32, 128), BF16),
            pltpu.VMEM((slots, 512, 512), BF16),
            pltpu.VMEM((slots, 256, 128), BF16),
            pltpu.VMEM((slots, 256, 128), BF16),
            pltpu.VMEM((64, 128), BF16),
            pltpu.VMEM((64, 128), BF16),
            pltpu.VMEM((512, 128), BF16),
            pltpu.VMEM((512, 128), BF16),
            pltpu.VMEM((STEPS, 256, 128), BF16),
            pltpu.VMEM((STEPS, 256, 128), BF16),
            pltpu.VMEM((3, 3, 2, 128, 512), BF16),
            pltpu.VMEM((3, 3, 2, 128, 512), BF16),
            pltpu.VMEM((3, 3, 512, 512), BF16),
            pltpu.VMEM((3, 3, 512, 512), BF16),
            pltpu.VMEM((2, 128, 128), F32),
            pltpu.VMEM((2, 32, 256), F32),
            pltpu.VMEM((256, 256), F32),
            pltpu.VMEM((2, 4, 4, 512), BF16),
            pltpu.VMEM((2, 4, 4, 512), BF16),
            pltpu.VMEM((2, 32, 256), F32),
            dma((6,)), dma((4,)), dma((3,)), dma((3,)), dma((3, 2)), dma((3, 2)), dma((STEPS,)), dma((STEPS,)),
            dma((slots,)), dma((slots,)), dma((slots,)), dma((slots,)), dma((slots,)), dma((slots,)),
            dma((2,)), dma((2,)), dma((2,)), dma((2,)), dma((2,)), dma((2,)),
        ],
        compiler_params=pltpu.CompilerParams(
            collective_id=0, has_side_effects=True, vmem_limit_bytes=50 << 20
        ),
    )(
        *(pltpu.with_memory_space_constraint(array, pltpu.HBM) for array in operands)
    )
    return decoded, cell.transpose(0, 1, 3, 2)


def solution(mesh):
    return jax.shard_map(
        per_device,
        mesh=mesh,
        in_specs=(
            P(None, None, "patch", None, "hid"),
            P(None, "patch", None, "hid"),
            P(None, "patch", None, "hid"),
            P(None, None, None, None, "hid"),
            P(None, None, None, None, "hid"),
            P(None, "hid"),
            P(),
            P(),
            P(),
            P(),
        ),
        out_specs=(P(None, "patch", "hid", None), P(None, "patch", None, "hid")),
        check_vma=False,
    )
```

```python
import jax
import jax.numpy as jnp
from jax import lax
from jax.experimental import pallas as pl
from jax.experimental.pallas import tpu as pltpu
from jax.sharding import PartitionSpec as P

STEPS = 4
FAR_FIRST = (6, 5, 7, 2, 4, 1, 3)
FAR_Z = (2, 1, 3, 0)
MESH = pl.DeviceIdType.MESH
F32 = jnp.float32
BF16 = jnp.bfloat16


def swap_halves(tile):
    return jnp.concatenate([tile[..., 64:], tile[..., :64]], axis=-1)


def kernel(
    frames_hbm, hidden_hbm, cell_hbm, gate_bias_hbm, bias1_hbm, bias2_hbm, w_in, w_hid, w_first, w_second,
    decoded, cell_out,
    frames, hidden, cell_in, gate_bias, bias1, bias2,
    packed, packed_cell, own, edge_top, edge_bot, image, halo_top, halo_bot,
    far_top_out, far_bot_out, far_top, far_bot, frame_top, frame_bot,
    wi, wh, w1, w2, bias_col, cell, gin, dec_out, dec_in, cell_back,
    in_sem, w_sem, wx_send, wx_recv, s_send, s_recv, f_send, f_recv,
    x_send, x_recv, ht_send, ht_recv, hb_send, hb_recv, fin_send, fin_recv, c2_send, c2_recv, d_send, d_recv,
):
    patch = lax.axis_index("patch")
    hid = lax.axis_index("hid")
    core = lax.rem(hid, 2)
    grp = hid // 2
    x_hi = grp // 4
    y = patch // 2
    x_lo = lax.rem(patch, 2)
    flip = lax.rem(x_hi + y, 2)
    block = y * 2 + lax.rem(x_lo + flip, 2)

    def holder(blk, g, c):
        by = blk // 2
        lo = lax.rem(lax.rem(blk, 2) + g // 4 + by, 2)
        return (by * 2 + lo, g * 2 + c)

    def trade(c):
        return (y * 2 + lax.rem(x_lo + flip, 2), grp * 2 + c)

    has_up = block > 0
    has_down = block < 7
    sibling = (patch, grp * 2 + 1 - core)
    z = lax.rem(grp, 4)
    group_patch = [holder(block, g, 0)[0] for g in (0, 4)]
    up_patch = [holder(block - 1, g, 0)[0] for g in (0, 4)]
    down_patch = [holder(block + 1, g, 0)[0] for g in (0, 4)]
    cross_patch = jnp.where(x_hi == 0, group_patch[1], group_patch[0])

    def peer(d):
        hi = 1 - x_hi if d >= 4 else x_hi
        return (cross_patch if d >= 4 else patch, (hi * 4 + lax.rem(z + d % 4, 4)) * 2 + core)

    def above(k):
        return (up_patch[k % 2], (k % 2 * 4 + lax.rem(z + FAR_Z[k // 2], 4)) * 2 + core)

    def below(k):
        return (down_patch[k % 2], (k % 2 * 4 + lax.rem(z + FAR_Z[k // 2], 4)) * 2 + core)

    in_copies = []
    loads = (
        (frames_hbm, frames), (hidden_hbm, hidden), (cell_hbm, cell_in),
        (gate_bias_hbm, gate_bias), (bias1_hbm, bias1), (bias2_hbm, bias2),
    )
    for k, (src, dst) in enumerate(loads):
        copy = pltpu.make_async_copy(src, dst, in_sem.at[k])
        copy.start()
        in_copies.append(copy)

    barrier = pltpu.get_barrier_semaphore()

    def greet(device):
        pl.semaphore_signal(barrier, inc=1, device_id=device, device_id_type=MESH)

    greet(sibling)

    @pl.when(flip == 1)
    def _():
        greet(trade(0))
        greet(trade(1))

    for d in FAR_FIRST:
        greet(peer(d))

    @pl.when(has_up)
    def _():
        for g in range(8):
            greet(above(g))

    @pl.when(has_down)
    def _():
        for g in range(8):
            greet(below(g))

    weight_copies = []
    for k, (src, dst) in enumerate(((w_in, wi), (w_hid, wh))):
        copy = pltpu.make_async_copy(src, dst.at[:, :, core], w_sem.at[k])
        copy.start()
        weight_copies.append(copy)
    for k, (src, dst) in enumerate(((w_first, w1), (w_second, w2))):
        copy = pltpu.make_async_copy(src, dst, w_sem.at[2 + k])
        copy.start()
        weight_copies.append(copy)

    for copy in in_copies:
        copy.wait()
    for b in range(2):
        packed[b, 0] = jnp.concatenate([hidden[b, r] for r in (0, 2, 1, 3)], axis=-1)
        for t in range(STEPS):
            packed[b, 1 + t] = jnp.concatenate([frames[t, b, r] for r in (0, 2, 1, 3)], axis=-1)
        packed_cell[b] = jnp.concatenate([cell_in[b, r] for r in (0, 2, 1, 3)], axis=-1)
    eye = lax.broadcasted_iota(jnp.int32, (32, 32), 0) == lax.broadcasted_iota(jnp.int32, (32, 32), 1)
    for k in range(4):
        column = jnp.sum(jnp.where(eye, gate_bias[k : k + 1, :], 0.0), axis=1, keepdims=True)
        bias_col[core, k * 32 : (k + 1) * 32, :] = jnp.broadcast_to(column, (32, 128))

    @pl.when(block == 0)
    def _():
        halo_top[...] = jnp.zeros_like(halo_top)
        far_top[...] = jnp.zeros_like(far_top)

    @pl.when(block == 7)
    def _():
        halo_bot[...] = jnp.zeros_like(halo_bot)
        far_bot[...] = jnp.zeros_like(far_bot)

    greeted = 1 + 2 * flip + 7 + jnp.where(has_up, 8, 0) + jnp.where(has_down, 8, 0)
    pl.semaphore_wait(barrier, greeted)

    my_rows = pl.ds(pl.multiple_of(core * 32, 32), 32)

    def trade_copy(k, c, b, rows):
        src, dst = (
            (lambda: (packed.at[b, 0:2], own.at[1:3, rows, :])),
            (lambda: (packed.at[b, 2:5], own.at[3:6, rows, :])),
            (lambda: (packed_cell.at[b], cell.at[c])),
        )[k]()
        return pltpu.make_async_remote_copy(
            src_ref=src, dst_ref=dst, send_sem=s_send.at[k, b], recv_sem=s_recv.at[k, c],
            device_id=trade(b), device_id_type=MESH,
        )

    def start_trades(kinds):
        for b in range(2):
            stays = (flip == 0) & (core == b)

            @pl.when(jnp.logical_not(stays))
            def _(b=b):
                for k in kinds:
                    trade_copy(k, core, b, my_rows).start()

    def wait_trades(kinds):
        for c in range(2):
            stays = (flip == 0) & (core == c)

            @pl.when(jnp.logical_not(stays))
            def _(c=c):
                for k in kinds:
                    trade_copy(k, c, 0, pl.ds(c * 32, 32)).wait_recv()

    start_trades((0,))

    @pl.when(flip == 0)
    def _():
        own[1:6, my_rows, :] = packed[core]
        cell[core] = packed_cell[core]

    def weight_trade(k, src, dst):
        return pltpu.make_async_remote_copy(
            src_ref=src, dst_ref=dst, send_sem=wx_send.at[k], recv_sem=wx_recv.at[k],
            device_id=sibling, device_id_type=MESH,
        )

    trades = [
        weight_trade(0, w_in, wi.at[:, :, core]),
        weight_trade(1, w_hid, wh.at[:, :, core]),
        weight_trade(2, bias_col.at[core], bias_col.at[core]),
    ]
    for copy in trades:
        copy.start()
    wait_trades((0,))

    half = lax.broadcasted_iota(jnp.int32, (32, 128), 1) < 64
    my_tile = pl.ds(pl.multiple_of(grp * 64, 64), 64)
    my_edge = pl.ds(pl.multiple_of(grp * 32, 32), 32)

    def pack_edges(slot):
        a = own[slot, :, 0:128]
        b = own[slot, :, 128:256]
        edge_top[slot] = jnp.where(half, a[:32], swap_halves(a[32:]))
        edge_bot[slot] = jnp.where(half, swap_halves(b[:32]), b[32:])

    def wait_bytes(ref, sem):
        pltpu.make_async_copy(ref, ref, sem).wait()

    def send(src, dst, send_sem, recv_sem, device):
        pltpu.make_async_remote_copy(
            src_ref=src, dst_ref=dst, send_sem=send_sem, recv_sem=recv_sem, device_id=device, device_id_type=MESH
        ).start()

    def send_tiles(slot, distances):
        for d in distances:
            send(own.at[slot], image.at[slot, my_tile, 128:384], x_send.at[slot], x_recv.at[slot], peer(d))
        image[slot, my_tile, 128:384] = own[slot]

    def broadcast(slot):
        pack_edges(slot)

        @pl.when(has_up)
        def _():
            for g in range(8):
                send(edge_top.at[slot], halo_bot.at[slot, my_edge, :], ht_send.at[slot], hb_recv.at[slot], above(g))

        @pl.when(has_down)
        def _():
            for g in range(8):
                send(edge_bot.at[slot], halo_top.at[slot, my_edge, :], hb_send.at[slot], ht_recv.at[slot], below(g))

        send_tiles(slot, FAR_FIRST)

    def wait_tiles(slot):
        wait_bytes(image.at[slot, 0:448, 128:384], x_recv.at[slot])

    def wait_edges_sent(slot):
        @pl.when(has_up)
        def _():
            wait_bytes(halo_top.at[slot], ht_send.at[slot])

        @pl.when(has_down)
        def _():
            wait_bytes(halo_bot.at[slot], hb_send.at[slot])

    def wait_sent(slot):
        wait_bytes(image.at[slot, 0:448, 128:384], x_send.at[slot])
        wait_edges_sent(slot)

    my_half = pl.ds(pl.multiple_of(x_hi * 256, 256), 256)
    my_edges = pl.ds(pl.multiple_of(x_hi * 128, 128), 128)

    def frame_along_z(t):
        send_tiles(2 + t, (2, 1, 3))

    def frame_onward(t):
        slot = 2 + t
        wait_bytes(image.at[slot, 0:192, 128:384], x_recv.at[slot])
        block_ref = image.at[slot, my_half, 128:384]
        send(block_ref, block_ref, f_send.at[t], f_recv.at[t], peer(4))
        for k in range(4):
            first = pl.ds(pl.multiple_of(x_hi * 256 + k * 64, 64), 32)
            later = pl.ds(pl.multiple_of(x_hi * 256 + k * 64 + 32, 32), 32)
            rows = slice(k * 32, k * 32 + 32)
            frame_top[t, rows] = jnp.where(half, image[slot, first, 128:256], swap_halves(image[slot, later, 128:256]))
            frame_bot[t, rows] = jnp.where(half, swap_halves(image[slot, first, 256:384]), image[slot, later, 256:384])

        @pl.when(has_up)
        def _():
            for k in (6, 7):
                send(frame_top.at[t], halo_bot.at[slot, my_edges, :], ht_send.at[slot], hb_recv.at[slot], above(k))

        @pl.when(has_down)
        def _():
            for k in (6, 7):
                send(frame_bot.at[t], halo_top.at[slot, my_edges, :], hb_send.at[slot], ht_recv.at[slot], below(k))

    def wait_halos(slot):
        @pl.when(has_up)
        def _():
            wait_bytes(halo_top.at[slot], ht_recv.at[slot])

        @pl.when(has_down)
        def _():
            wait_bytes(halo_bot.at[slot], hb_recv.at[slot])

        for g in range(8):
            a0 = image[slot, g * 64 : g * 64 + 32, 128:256]
            a1 = image[slot, g * 64 + 32 : g * 64 + 64, 128:256]
            b0 = image[slot, g * 64 : g * 64 + 32, 256:384]
            b1 = image[slot, g * 64 + 32 : g * 64 + 64, 256:384]
            top = halo_top[slot, g * 32 : g * 32 + 32, :]
            bot = halo_bot[slot, g * 32 : g * 32 + 32, :]
            image[slot, g * 64 : g * 64 + 32, 0:128] = jnp.where(half, top, swap_halves(b0))
            image[slot, g * 64 + 32 : g * 64 + 64, 0:128] = swap_halves(jnp.where(half, b1, top))
            image[slot, g * 64 : g * 64 + 32, 384:512] = swap_halves(jnp.where(half, bot, a0))
            image[slot, g * 64 + 32 : g * 64 + 64, 384:512] = jnp.where(half, swap_halves(a1), bot)

    place = lax.rem(lax.broadcasted_iota(jnp.int32, (256, 128), 1), 64)

    def conv(slot, weight, write):
        def tap(p, q):
            lhs = weight[p, q].reshape(256, 512)
            return jnp.dot(lhs, image[slot, :, p * 128 : p * 128 + 256], preferred_element_type=F32)

        parts = [tap(1, q) for q in range(3)]
        wait_halos(slot)
        parts = [parts[q] + tap(0, q) + tap(2, q) for q in range(3)]
        for tile in range(2):
            lanes = slice(tile * 128, (tile + 1) * 128)
            left = jnp.where(place == 0, 0.0, pltpu.roll(parts[0][:, lanes], 1, 1))
            right = jnp.where(place == 63, 0.0, pltpu.roll(parts[2][:, lanes], 127, 1))
            write(lanes, parts[1][:, lanes] + left + right)

    frame_along_z(0)
    broadcast(1)
    start_trades((1, 2))
    frame_onward(0)
    wait_trades((1, 2))
    frame_along_z(1)
    weight_copies[0].wait()
    weight_copies[1].wait()
    for copy in trades:
        copy.wait_recv()

    def write_gin(lanes, value):
        for c in range(2):
            rows = slice(c * 128, (c + 1) * 128)
            gin[rows, lanes] = value[rows] + bias_col[c]

    def update(next_slot):
        def write(lanes, value):
            gates = value + gin[:, lanes]
            for c in range(2):
                z = [gates[c * 128 + k * 32 : c * 128 + (k + 1) * 32] for k in range(4)]
                new = jax.nn.sigmoid(z[1] + 1.0) * cell[c, :, lanes] + jax.nn.sigmoid(z[0]) * jnp.tanh(z[2])
                cell[c, :, lanes] = new
                own[next_slot, c * 32 : (c + 1) * 32, lanes] = (jax.nn.sigmoid(z[3]) * jnp.tanh(new)).astype(BF16)

        return write

    def step(t, carry):
        slot = lax.rem(t + 1, 2)
        following = lax.rem(t, 2)

        wait_bytes(image.at[2 + t, 0:256, 128:384], f_recv.at[t])
        conv(2 + t, wi, write_gin)

        @pl.when(t > 0)
        def _():
            wait_sent(following)

        wait_tiles(slot)
        conv(slot, wh, update(following))

        @pl.when(t < STEPS - 1)
        def _():
            broadcast(following)
            frame_onward(t + 1)

        @pl.when(t < STEPS - 2)
        def _():
            frame_along_z(t + 2)

        return carry

    lax.fori_loop(0, STEPS, step, 0)

    last = (STEPS + 1) % 2
    wide = lax.broadcasted_iota(jnp.int32, (64, 128), 1) < 64
    row_a = own[last, :, 0:128]
    row_b = own[last, :, 128:256]
    far_top_out[...] = jnp.where(wide, row_a, swap_halves(row_b))
    far_bot_out[...] = jnp.where(wide, swap_halves(row_a), row_b)

    @pl.when(has_up)
    def _():
        for g in range(8):
            send(far_top_out, far_bot.at[my_tile, :], fin_send.at[0], fin_recv.at[0], above(g))

    @pl.when(has_down)
    def _():
        for g in range(8):
            send(far_bot_out, far_top.at[my_tile, :], fin_send.at[1], fin_recv.at[1], below(g))

    send_tiles(last, FAR_FIRST)

    def cell_copy(c, b):
        return pltpu.make_async_remote_copy(
            src_ref=cell.at[c], dst_ref=cell_back.at[b],
            send_sem=c2_send.at[c], recv_sem=c2_recv.at[b],
            device_id=trade(c), device_id_type=MESH,
        )

    for c in range(2):
        stays = (flip == 0) & (core == c)

        @pl.when(jnp.logical_not(stays))
        def _(c=c):
            cell_copy(c, core).start()

        @pl.when(stays)
        def _(c=c):
            cell_back[core] = cell[c]

    weight_copies[2].wait()
    weight_copies[3].wait()
    wait_tiles(last)

    @pl.when(has_down)
    def _():
        wait_bytes(far_bot, fin_recv.at[0])

    @pl.when(has_up)
    def _():
        wait_bytes(far_top, fin_recv.at[1])

    sel_row = lax.broadcasted_iota(jnp.int32, (32, 128), 0)
    sel_lane = lax.broadcasted_iota(jnp.int32, (32, 128), 1)
    want = lax.rem(sel_row, 16) + grp * 8 - 2
    chosen = (want >= 0) & (want < 64) & (sel_lane == want + 64 * (sel_row // 16))
    pick = jnp.where(chosen, 1.0, 0.0).astype(BF16)

    def window(tile):
        return lax.dot_general(pick, tile, (((1,), (1,)), ((), ())), preferred_element_type=F32).astype(BF16)

    above = window(far_top[...])
    tile_a = window(image[last, :, 128:256])
    tile_b = window(image[last, :, 256:384])
    below = window(far_bot[...])
    pixels = jnp.concatenate([above, tile_a[:16], tile_b[:16], tile_a[16:], tile_b[16:], below], axis=0)

    def decode(source, rows, weight):
        parts = []
        for q in range(3):
            total = None
            for p in range(3):
                term = jnp.dot(source[p * 16 : p * 16 + rows * 16], weight[p, q], preferred_element_type=F32)
                total = term if total is None else total + term
            parts.append(total)
        return parts[1] + pltpu.roll(parts[0], 1, 0) + pltpu.roll(parts[2], rows * 16 - 1, 0)

    first = decode(pixels, 6, w1) + bias1[...]
    first = first / (1.0 + jnp.exp(-first))
    pixel = lax.broadcasted_iota(jnp.int32, (96, 512), 0)
    image_row = block * 4 - 1 + pixel // 16
    image_col = grp * 8 - 2 + lax.rem(pixel, 16)
    inside = (image_row >= 0) & (image_row < 32) & (image_col >= 0) & (image_col < 64)
    middle = jnp.where(inside, first, 0.0).astype(BF16)
    second = decode(middle, 4, w2) + bias2[...]
    shifted = second.reshape(4, 16, 512)
    for c in range(2):
        dec_out[c] = shifted[:, 2 + 4 * c : 6 + 4 * c, :].astype(BF16)

    def dec_copy(c, b):
        return pltpu.make_async_remote_copy(
            src_ref=dec_out.at[c], dst_ref=dec_in.at[b],
            send_sem=d_send.at[c], recv_sem=d_recv.at[b],
            device_id=trade(c), device_id_type=MESH,
        )

    for c in range(2):
        stays = (flip == 0) & (core == c)

        @pl.when(jnp.logical_not(stays))
        def _(c=c):
            dec_copy(c, core).start()

        @pl.when(stays)
        def _(c=c):
            dec_in[core] = dec_out[c]

    for b in range(2):
        stays = (flip == 0) & (core == b)

        @pl.when(jnp.logical_not(stays))
        def _(b=b):
            cell_copy(0, b).wait_recv()

        for r in range(4):
            start = (r % 2) * 128 + (r // 2) * 64
            cell_out[b, r] = cell_back[b, :, start : start + 64]

    for t in range(STEPS):
        wait_bytes(image.at[2 + t, 0:192, 128:384], x_send.at[2 + t])
        wait_bytes(image.at[2 + t, 0:256, 128:384], f_send.at[t])
        wait_edges_sent(2 + t)
    wait_sent(1 - last)
    wait_bytes(image.at[last, 0:448, 128:384], x_send.at[last])

    @pl.when(has_up)
    def _():
        wait_bytes(far_top, fin_send.at[0])

    @pl.when(has_down)
    def _():
        wait_bytes(far_bot, fin_send.at[1])

    for copy in trades:
        copy.wait_send()

    for b in range(2):
        stays = (flip == 0) & (core == b)

        @pl.when(jnp.logical_not(stays))
        def _(b=b):
            for k in range(3):
                trade_copy(k, core, b, my_rows).wait_send()
            cell_copy(b, core).wait_send()
            dec_copy(0, b).wait_recv()
            dec_copy(b, core).wait_send()

        decoded[b] = dec_in[b]


def per_device(
    frames, hidden_start, cell_start, input_weight, hidden_weight, gate_bias,
    first_weight, first_bias, second_weight, second_bias,
):
    vmem = pl.BlockSpec(memory_space=pltpu.VMEM)
    hbm = pl.BlockSpec(memory_space=pltpu.HBM)
    dma = pltpu.SemaphoreType.DMA
    slots = STEPS + 2

    def gate_rows(weight):
        return weight.transpose(0, 1, 3, 4, 2).reshape(3, 3, 128, 512)

    operands = (
        frames.transpose(0, 1, 2, 4, 3),
        hidden_start.transpose(0, 1, 3, 2),
        cell_start.transpose(0, 1, 3, 2),
        gate_bias,
        first_bias.reshape(1, -1),
        second_bias.reshape(1, -1),
        gate_rows(input_weight),
        gate_rows(hidden_weight),
        first_weight,
        second_weight,
    )
    decoded, cell = pl.pallas_call(
        kernel,
        name="convlstm",
        out_shape=(
            jax.ShapeDtypeStruct((2, 4, 4, 512), BF16),
            jax.ShapeDtypeStruct((2, 4, 32, 64), F32),
        ),
        in_specs=[hbm] * 10,
        out_specs=(vmem, vmem),
        scratch_shapes=[
            pltpu.VMEM((STEPS, 2, 4, 32, 64), BF16),
            pltpu.VMEM((2, 4, 32, 64), BF16),
            pltpu.VMEM((2, 4, 32, 64), F32),
            pltpu.VMEM((4, 32), F32),
            pltpu.VMEM((1, 512), F32),
            pltpu.VMEM((1, 512), F32),
            pltpu.VMEM((2, STEPS + 1, 32, 256), BF16),
            pltpu.VMEM((2, 32, 256), F32),
            pltpu.VMEM((slots, 64, 256), BF16),
            pltpu.VMEM((2, 32, 128), BF16),
            pltpu.VMEM((2, 32, 128), BF16),
            pltpu.VMEM((slots, 512, 512), BF16),
            pltpu.VMEM((slots, 256, 128), BF16),
            pltpu.VMEM((slots, 256, 128), BF16),
            pltpu.VMEM((64, 128), BF16),
            pltpu.VMEM((64, 128), BF16),
            pltpu.VMEM((512, 128), BF16),
            pltpu.VMEM((512, 128), BF16),
            pltpu.VMEM((STEPS, 128, 128), BF16),
            pltpu.VMEM((STEPS, 128, 128), BF16),
            pltpu.VMEM((3, 3, 2, 128, 512), BF16),
            pltpu.VMEM((3, 3, 2, 128, 512), BF16),
            pltpu.VMEM((3, 3, 512, 512), BF16),
            pltpu.VMEM((3, 3, 512, 512), BF16),
            pltpu.VMEM((2, 128, 128), F32),
            pltpu.VMEM((2, 32, 256), F32),
            pltpu.VMEM((256, 256), F32),
            pltpu.VMEM((2, 4, 4, 512), BF16),
            pltpu.VMEM((2, 4, 4, 512), BF16),
            pltpu.VMEM((2, 32, 256), F32),
            dma((6,)), dma((4,)), dma((3,)), dma((3,)), dma((3, 2)), dma((3, 2)), dma((STEPS,)), dma((STEPS,)),
            dma((slots,)), dma((slots,)), dma((slots,)), dma((slots,)), dma((slots,)), dma((slots,)),
            dma((2,)), dma((2,)), dma((2,)), dma((2,)), dma((2,)), dma((2,)),
        ],
        compiler_params=pltpu.CompilerParams(
            collective_id=0, has_side_effects=True, vmem_limit_bytes=50 << 20
        ),
    )(
        *(pltpu.with_memory_space_constraint(array, pltpu.HBM) for array in operands)
    )
    return decoded, cell.transpose(0, 1, 3, 2)


def solution(mesh):
    return jax.shard_map(
        per_device,
        mesh=mesh,
        in_specs=(
            P(None, None, "patch", None, "hid"),
            P(None, "patch", None, "hid"),
            P(None, "patch", None, "hid"),
            P(None, None, None, None, "hid"),
            P(None, None, None, None, "hid"),
            P(None, "hid"),
            P(),
            P(),
            P(),
            P(),
        ),
        out_specs=(P(None, "patch", "hid", None), P(None, "patch", None, "hid")),
        check_vma=False,
    )
```

```python
import jax
import jax.numpy as jnp
from jax import lax
from jax.experimental import pallas as pl
from jax.experimental.pallas import tpu as pltpu
from jax.sharding import PartitionSpec as P

STEPS = 4
FAR_FIRST = (6, 5, 7, 2, 4, 1, 3)
FAR_Z = (2, 1, 3, 0)
MESH = pl.DeviceIdType.MESH
F32 = jnp.float32
BF16 = jnp.bfloat16


def swap_halves(tile):
    return jnp.concatenate([tile[..., 64:], tile[..., :64]], axis=-1)


def kernel(
    frames_hbm, hidden_hbm, cell_hbm, gate_bias_hbm, bias1_hbm, bias2_hbm, w_in, w_hid, w_first, w_second,
    decoded, cell_out,
    frames, hidden, cell_in, gate_bias, bias1, bias2,
    packed, packed_cell, own, edge_top, edge_bot, image, halo_top, halo_bot,
    far_top_out, far_bot_out, far_top, far_bot, frame_top, frame_bot,
    wi, wh, w1, w2, bias_col, cell, gin, dec_out, dec_in, cell_back,
    in_sem, w_sem, wx_send, wx_recv, s_send, s_recv, f_send, f_recv,
    x_send, x_recv, ht_send, ht_recv, hb_send, hb_recv, fin_send, fin_recv, c2_send, c2_recv, d_send, d_recv,
):
    patch = lax.axis_index("patch")
    hid = lax.axis_index("hid")
    core = lax.rem(hid, 2)
    grp = hid // 2
    x_hi = grp // 4
    y = patch // 2
    x_lo = lax.rem(patch, 2)
    flip = lax.rem(x_hi + y, 2)
    block = y * 2 + lax.rem(x_lo + flip, 2)

    def holder(blk, g, c):
        by = blk // 2
        lo = lax.rem(lax.rem(blk, 2) + g // 4 + by, 2)
        return (by * 2 + lo, g * 2 + c)

    def trade(c):
        return (y * 2 + lax.rem(x_lo + flip, 2), grp * 2 + c)

    has_up = block > 0
    has_down = block < 7
    sibling = (patch, grp * 2 + 1 - core)
    z = lax.rem(grp, 4)
    group_patch = [holder(block, g, 0)[0] for g in (0, 4)]
    up_patch = [holder(block - 1, g, 0)[0] for g in (0, 4)]
    down_patch = [holder(block + 1, g, 0)[0] for g in (0, 4)]
    cross_patch = jnp.where(x_hi == 0, group_patch[1], group_patch[0])

    def peer(d):
        hi = 1 - x_hi if d >= 4 else x_hi
        return (cross_patch if d >= 4 else patch, (hi * 4 + lax.rem(z + d % 4, 4)) * 2 + core)

    above_same = (jnp.where(x_hi == 0, up_patch[0], up_patch[1]), hid)
    below_same = (jnp.where(x_hi == 0, down_patch[0], down_patch[1]), hid)

    def above(k):
        return (up_patch[k % 2], (k % 2 * 4 + lax.rem(z + FAR_Z[k // 2], 4)) * 2 + core)

    def below(k):
        return (down_patch[k % 2], (k % 2 * 4 + lax.rem(z + FAR_Z[k // 2], 4)) * 2 + core)

    in_copies = []
    loads = (
        (frames_hbm, frames), (hidden_hbm, hidden), (cell_hbm, cell_in),
        (gate_bias_hbm, gate_bias), (bias1_hbm, bias1), (bias2_hbm, bias2),
    )
    for k, (src, dst) in enumerate(loads):
        copy = pltpu.make_async_copy(src, dst, in_sem.at[k])
        copy.start()
        in_copies.append(copy)

    barrier = pltpu.get_barrier_semaphore()

    def greet(device):
        pl.semaphore_signal(barrier, inc=1, device_id=device, device_id_type=MESH)

    greet(sibling)

    @pl.when(flip == 1)
    def _():
        greet(trade(0))
        greet(trade(1))

    for d in FAR_FIRST:
        greet(peer(d))

    @pl.when(has_up)
    def _():
        for g in range(8):
            greet(above(g))

    @pl.when(has_down)
    def _():
        for g in range(8):
            greet(below(g))

    weight_copies = []
    for k, (src, dst) in enumerate(((w_in, wi), (w_hid, wh))):
        copy = pltpu.make_async_copy(src, dst.at[:, :, core], w_sem.at[k])
        copy.start()
        weight_copies.append(copy)
    for k, (src, dst) in enumerate(((w_first, w1), (w_second, w2))):
        copy = pltpu.make_async_copy(src, dst, w_sem.at[2 + k])
        copy.start()
        weight_copies.append(copy)

    for copy in in_copies:
        copy.wait()
    for b in range(2):
        for i in range(2):
            packed[b, 0, i] = jnp.concatenate([hidden[b, i], hidden[b, i + 2]], axis=-1)
            for t in range(STEPS):
                packed[b, 1 + t, i] = jnp.concatenate([frames[t, b, i], frames[t, b, i + 2]], axis=-1)
        packed_cell[b] = jnp.concatenate([cell_in[b, r] for r in (0, 2, 1, 3)], axis=-1)
    eye = lax.broadcasted_iota(jnp.int32, (32, 32), 0) == lax.broadcasted_iota(jnp.int32, (32, 32), 1)
    for k in range(4):
        column = jnp.sum(jnp.where(eye, gate_bias[k : k + 1, :], 0.0), axis=1, keepdims=True)
        bias_col[core, k * 32 : (k + 1) * 32, :] = jnp.broadcast_to(column, (32, 128))

    @pl.when(block == 0)
    def _():
        halo_top[...] = jnp.zeros_like(halo_top)
        far_top[...] = jnp.zeros_like(far_top)

    @pl.when(block == 7)
    def _():
        halo_bot[...] = jnp.zeros_like(halo_bot)
        far_bot[...] = jnp.zeros_like(far_bot)

    greeted = 1 + 2 * flip + 7 + jnp.where(has_up, 8, 0) + jnp.where(has_down, 8, 0)
    pl.semaphore_wait(barrier, greeted)

    my_rows = pl.ds(pl.multiple_of(core * 32, 32), 32)

    def trade_copy(k, c, b, rows):
        src, dst = (
            (lambda: (packed.at[b, 0:2], own.at[1:3, :, rows, :])),
            (lambda: (packed.at[b, 2:5], own.at[3:6, :, rows, :])),
            (lambda: (packed_cell.at[b], cell.at[c])),
        )[k]()
        return pltpu.make_async_remote_copy(
            src_ref=src, dst_ref=dst, send_sem=s_send.at[k, b], recv_sem=s_recv.at[k, c],
            device_id=trade(b), device_id_type=MESH,
        )

    def start_trades(kinds):
        for b in range(2):
            stays = (flip == 0) & (core == b)

            @pl.when(jnp.logical_not(stays))
            def _(b=b):
                for k in kinds:
                    trade_copy(k, core, b, my_rows).start()

    def wait_trades(kinds):
        for c in range(2):
            stays = (flip == 0) & (core == c)

            @pl.when(jnp.logical_not(stays))
            def _(c=c):
                for k in kinds:
                    trade_copy(k, c, 0, pl.ds(c * 32, 32)).wait_recv()

    start_trades((0,))

    @pl.when(flip == 0)
    def _():
        own[1:6, :, my_rows, :] = packed[core]
        cell[core] = packed_cell[core]

    def weight_trade(k, src, dst):
        return pltpu.make_async_remote_copy(
            src_ref=src, dst_ref=dst, send_sem=wx_send.at[k], recv_sem=wx_recv.at[k],
            device_id=sibling, device_id_type=MESH,
        )

    trades = [
        weight_trade(0, w_in, wi.at[:, :, core]),
        weight_trade(1, w_hid, wh.at[:, :, core]),
        weight_trade(2, bias_col.at[core], bias_col.at[core]),
    ]
    for copy in trades:
        copy.start()
    wait_trades((0,))

    half = lax.broadcasted_iota(jnp.int32, (32, 128), 1) < 64
    my_tile = pl.ds(pl.multiple_of(grp * 64, 64), 64)
    my_edge = pl.ds(pl.multiple_of(grp * 32, 32), 32)

    def pack_edges(slot):
        a = own[slot, 0]
        b = own[slot, 1]
        edge_top[slot] = jnp.where(half, a[:32], swap_halves(a[32:]))
        edge_bot[slot] = jnp.where(half, swap_halves(b[:32]), b[32:])

    def wait_bytes(ref, sem):
        pltpu.make_async_copy(ref, ref, sem).wait()

    def send(src, dst, send_sem, recv_sem, device):
        pltpu.make_async_remote_copy(
            src_ref=src, dst_ref=dst, send_sem=send_sem, recv_sem=recv_sem, device_id=device, device_id_type=MESH
        ).start()

    def send_tiles(slot, distances):
        for d in distances:
            send(own.at[slot], image.at[slot, 1:3, my_tile, :], x_send.at[slot], x_recv.at[slot], peer(d))
        image[slot, 1:3, my_tile, :] = own[slot]

    def send_edges(slot):
        pack_edges(slot)

        @pl.when(has_up)
        def _():
            for g in range(8):
                send(edge_top.at[slot], halo_bot.at[slot, my_edge, :], ht_send.at[slot], hb_recv.at[slot], above(g))

        @pl.when(has_down)
        def _():
            for g in range(8):
                send(edge_bot.at[slot], halo_top.at[slot, my_edge, :], hb_send.at[slot], ht_recv.at[slot], below(g))

    def broadcast(slot):
        send_edges(slot)
        send_tiles(slot, FAR_FIRST)

    def wait_tiles(slot):
        wait_bytes(image.at[slot, 1:3, 0:448, :], x_recv.at[slot])

    def wait_edges_sent(slot):
        @pl.when(has_up)
        def _():
            wait_bytes(halo_top.at[slot], ht_send.at[slot])

        @pl.when(has_down)
        def _():
            wait_bytes(halo_bot.at[slot], hb_send.at[slot])

    def wait_sent(slot):
        wait_bytes(image.at[slot, 1:3, 0:448, :], x_send.at[slot])
        wait_edges_sent(slot)

    my_half = pl.ds(pl.multiple_of(x_hi * 256, 256), 256)
    cross_tile = pl.ds(pl.multiple_of((1 - x_hi) * 256 + z * 64, 64), 64)

    def frame_first(t):
        slot = 2 + t
        send(
            own.at[slot, 1], image.at[slot, 2, my_tile, :], f_send.at[0, t], f_recv.at[0, t], peer(4)
        )
        send_tiles(slot, (2, 1, 3))

    def frame_second(t):
        slot = 2 + t
        wait_bytes(image.at[slot, 2, 0:64, :], f_recv.at[0, t])
        cross = image.at[slot, 2, cross_tile, :]
        for d in (2, 1, 3):
            send(cross, cross, f_send.at[1, t], f_recv.at[1, t], peer(d))
        wait_bytes(image.at[slot, 1:3, 0:192, :], x_recv.at[slot])
        half_ref = image.at[slot, 1, my_half, :]
        send(half_ref, half_ref, f_send.at[2, t], f_recv.at[2, t], peer(4))

    def frame_wait(t):
        slot = 2 + t
        wait_bytes(image.at[slot, 2, 0:192, :], f_recv.at[1, t])
        wait_bytes(image.at[slot, 1, 0:256, :], f_recv.at[2, t])

    def frame_edges(t):
        slot = 2 + t
        for g in range(8):
            first = slice(g * 64, g * 64 + 32)
            later = slice(g * 64 + 32, g * 64 + 64)
            rows = slice(g * 32, g * 32 + 32)
            frame_top[t, rows] = jnp.where(half, image[slot, 1, first], swap_halves(image[slot, 1, later]))
            frame_bot[t, rows] = jnp.where(half, swap_halves(image[slot, 2, first]), image[slot, 2, later])

        @pl.when(has_up)
        def _():
            send(frame_top.at[t], halo_bot.at[slot], ht_send.at[slot], hb_recv.at[slot], above_same)

        @pl.when(has_down)
        def _():
            send(frame_bot.at[t], halo_top.at[slot], hb_send.at[slot], ht_recv.at[slot], below_same)

    def wait_halos(slot):
        @pl.when(has_up)
        def _():
            wait_bytes(halo_top.at[slot], ht_recv.at[slot])

        @pl.when(has_down)
        def _():
            wait_bytes(halo_bot.at[slot], hb_recv.at[slot])

        for g in range(8):
            a0 = image[slot, 1, g * 64 : g * 64 + 32]
            a1 = image[slot, 1, g * 64 + 32 : g * 64 + 64]
            b0 = image[slot, 2, g * 64 : g * 64 + 32]
            b1 = image[slot, 2, g * 64 + 32 : g * 64 + 64]
            top = halo_top[slot, g * 32 : g * 32 + 32, :]
            bot = halo_bot[slot, g * 32 : g * 32 + 32, :]
            image[slot, 0, g * 64 : g * 64 + 32] = jnp.where(half, top, swap_halves(b0))
            image[slot, 0, g * 64 + 32 : g * 64 + 64] = swap_halves(jnp.where(half, b1, top))
            image[slot, 3, g * 64 : g * 64 + 32] = swap_halves(jnp.where(half, bot, a0))
            image[slot, 3, g * 64 + 32 : g * 64 + 64] = jnp.where(half, swap_halves(a1), bot)

    place = lax.rem(lax.broadcasted_iota(jnp.int32, (256, 128), 1), 64)

    def conv(slot, weight, write):
        def tap(p, q):
            lhs = weight[p, q].reshape(256, 512)
            rhs = jnp.concatenate([image[slot, p], image[slot, p + 1]], axis=1)
            return jnp.dot(lhs, rhs, preferred_element_type=F32)

        parts = [tap(1, q) for q in range(3)]
        wait_halos(slot)
        parts = [parts[q] + tap(0, q) + tap(2, q) for q in range(3)]
        for tile in range(2):
            lanes = slice(tile * 128, (tile + 1) * 128)
            left = jnp.where(place == 0, 0.0, pltpu.roll(parts[0][:, lanes], 1, 1))
            right = jnp.where(place == 63, 0.0, pltpu.roll(parts[2][:, lanes], 127, 1))
            write(tile, lanes, parts[1][:, lanes] + left + right)

    frame_first(0)
    broadcast(1)
    send_edges(2)
    start_trades((1, 2))
    frame_second(0)
    wait_trades((1, 2))
    frame_first(1)
    send_edges(3)
    weight_copies[0].wait()
    weight_copies[1].wait()
    for copy in trades:
        copy.wait_recv()

    def write_gin(tile, lanes, value):
        for c in range(2):
            rows = slice(c * 128, (c + 1) * 128)
            gin[rows, lanes] = value[rows] + bias_col[c]

    def update(next_slot):
        def write(tile, lanes, value):
            gates = value + gin[:, lanes]
            for c in range(2):
                z = [gates[c * 128 + k * 32 : c * 128 + (k + 1) * 32] for k in range(4)]
                new = jax.nn.sigmoid(z[1] + 1.0) * cell[c, :, lanes] + jax.nn.sigmoid(z[0]) * jnp.tanh(z[2])
                cell[c, :, lanes] = new
                own[next_slot, tile, c * 32 : (c + 1) * 32] = (jax.nn.sigmoid(z[3]) * jnp.tanh(new)).astype(BF16)

        return write

    def step(t, carry):
        slot = lax.rem(t + 1, 2)
        following = lax.rem(t, 2)

        frame_wait(t)

        @pl.when(t > 1)
        def _():
            frame_edges(t)

        @pl.when((t > 0) & (t < STEPS - 1))
        def _():
            frame_second(t + 1)

        @pl.when(t < STEPS - 2)
        def _():
            frame_first(t + 2)

        conv(2 + t, wi, write_gin)

        @pl.when(t == 0)
        def _():
            frame_second(t + 1)

        @pl.when(t > 0)
        def _():
            wait_sent(following)

        wait_tiles(slot)
        conv(slot, wh, update(following))

        @pl.when(t < STEPS - 1)
        def _():
            broadcast(following)

        return carry

    lax.fori_loop(0, STEPS, step, 0)

    last = (STEPS + 1) % 2
    wide = lax.broadcasted_iota(jnp.int32, (64, 128), 1) < 64
    row_a = own[last, 0]
    row_b = own[last, 1]
    far_top_out[...] = jnp.where(wide, row_a, swap_halves(row_b))
    far_bot_out[...] = jnp.where(wide, swap_halves(row_a), row_b)

    @pl.when(has_up)
    def _():
        for g in range(8):
            send(far_top_out, far_bot.at[my_tile, :], fin_send.at[0], fin_recv.at[0], above(g))

    @pl.when(has_down)
    def _():
        for g in range(8):
            send(far_bot_out, far_top.at[my_tile, :], fin_send.at[1], fin_recv.at[1], below(g))

    send_tiles(last, FAR_FIRST)

    def cell_copy(c, b):
        return pltpu.make_async_remote_copy(
            src_ref=cell.at[c], dst_ref=cell_back.at[b],
            send_sem=c2_send.at[c], recv_sem=c2_recv.at[b],
            device_id=trade(c), device_id_type=MESH,
        )

    for c in range(2):
        stays = (flip == 0) & (core == c)

        @pl.when(jnp.logical_not(stays))
        def _(c=c):
            cell_copy(c, core).start()

        @pl.when(stays)
        def _(c=c):
            cell_back[core] = cell[c]

    weight_copies[2].wait()
    weight_copies[3].wait()
    wait_tiles(last)

    @pl.when(has_down)
    def _():
        wait_bytes(far_bot, fin_recv.at[0])

    @pl.when(has_up)
    def _():
        wait_bytes(far_top, fin_recv.at[1])

    sel_row = lax.broadcasted_iota(jnp.int32, (32, 128), 0)
    sel_lane = lax.broadcasted_iota(jnp.int32, (32, 128), 1)
    want = lax.rem(sel_row, 16) + grp * 8 - 2
    chosen = (want >= 0) & (want < 64) & (sel_lane == want + 64 * (sel_row // 16))
    pick = jnp.where(chosen, 1.0, 0.0).astype(BF16)

    def window(tile):
        return lax.dot_general(pick, tile, (((1,), (1,)), ((), ())), preferred_element_type=F32).astype(BF16)

    above = window(far_top[...])
    tile_a = window(image[last, 1])
    tile_b = window(image[last, 2])
    below = window(far_bot[...])
    pixels = jnp.concatenate([above, tile_a[:16], tile_b[:16], tile_a[16:], tile_b[16:], below], axis=0)

    def decode(source, rows, weight):
        parts = []
        for q in range(3):
            total = None
            for p in range(3):
                term = jnp.dot(source[p * 16 : p * 16 + rows * 16], weight[p, q], preferred_element_type=F32)
                total = term if total is None else total + term
            parts.append(total)
        return parts[1] + pltpu.roll(parts[0], 1, 0) + pltpu.roll(parts[2], rows * 16 - 1, 0)

    first = decode(pixels, 6, w1) + bias1[...]
    first = first / (1.0 + jnp.exp(-first))
    pixel = lax.broadcasted_iota(jnp.int32, (96, 512), 0)
    image_row = block * 4 - 1 + pixel // 16
    image_col = grp * 8 - 2 + lax.rem(pixel, 16)
    inside = (image_row >= 0) & (image_row < 32) & (image_col >= 0) & (image_col < 64)
    middle = jnp.where(inside, first, 0.0).astype(BF16)
    second = decode(middle, 4, w2) + bias2[...]
    shifted = second.reshape(4, 16, 512)
    for c in range(2):
        dec_out[c] = shifted[:, 2 + 4 * c : 6 + 4 * c, :].astype(BF16)

    def dec_copy(c, b):
        return pltpu.make_async_remote_copy(
            src_ref=dec_out.at[c], dst_ref=dec_in.at[b],
            send_sem=d_send.at[c], recv_sem=d_recv.at[b],
            device_id=trade(c), device_id_type=MESH,
        )

    for c in range(2):
        stays = (flip == 0) & (core == c)

        @pl.when(jnp.logical_not(stays))
        def _(c=c):
            dec_copy(c, core).start()

        @pl.when(stays)
        def _(c=c):
            dec_in[core] = dec_out[c]

    for b in range(2):
        stays = (flip == 0) & (core == b)

        @pl.when(jnp.logical_not(stays))
        def _(b=b):
            cell_copy(0, b).wait_recv()

        for r in range(4):
            start = (r % 2) * 128 + (r // 2) * 64
            cell_out[b, r] = cell_back[b, :, start : start + 64]

    for t in range(STEPS):
        wait_bytes(image.at[2 + t, 1:3, 0:192, :], x_send.at[2 + t])
        wait_bytes(image.at[2 + t, 2, 0:64, :], f_send.at[0, t])
        wait_bytes(image.at[2 + t, 2, 0:192, :], f_send.at[1, t])
        wait_bytes(image.at[2 + t, 1, 0:256, :], f_send.at[2, t])
        wait_edges_sent(2 + t)
    wait_sent(1 - last)
    wait_bytes(image.at[last, 1:3, 0:448, :], x_send.at[last])

    @pl.when(has_up)
    def _():
        wait_bytes(far_top, fin_send.at[0])

    @pl.when(has_down)
    def _():
        wait_bytes(far_bot, fin_send.at[1])

    for copy in trades:
        copy.wait_send()

    for b in range(2):
        stays = (flip == 0) & (core == b)

        @pl.when(jnp.logical_not(stays))
        def _(b=b):
            for k in range(3):
                trade_copy(k, core, b, my_rows).wait_send()
            cell_copy(b, core).wait_send()
            dec_copy(0, b).wait_recv()
            dec_copy(b, core).wait_send()

        decoded[b] = dec_in[b]


def per_device(
    frames, hidden_start, cell_start, input_weight, hidden_weight, gate_bias,
    first_weight, first_bias, second_weight, second_bias,
):
    vmem = pl.BlockSpec(memory_space=pltpu.VMEM)
    hbm = pl.BlockSpec(memory_space=pltpu.HBM)
    dma = pltpu.SemaphoreType.DMA
    slots = STEPS + 2

    def gate_rows(weight):
        return weight.transpose(0, 1, 3, 4, 2).reshape(3, 3, 128, 512)

    operands = (
        frames.transpose(0, 1, 2, 4, 3),
        hidden_start.transpose(0, 1, 3, 2),
        cell_start.transpose(0, 1, 3, 2),
        gate_bias,
        first_bias.reshape(1, -1),
        second_bias.reshape(1, -1),
        gate_rows(input_weight),
        gate_rows(hidden_weight),
        first_weight,
        second_weight,
    )
    decoded, cell = pl.pallas_call(
        kernel,
        name="convlstm",
        out_shape=(
            jax.ShapeDtypeStruct((2, 4, 4, 512), BF16),
            jax.ShapeDtypeStruct((2, 4, 32, 64), F32),
        ),
        in_specs=[hbm] * 10,
        out_specs=(vmem, vmem),
        scratch_shapes=[
            pltpu.VMEM((STEPS, 2, 4, 32, 64), BF16),
            pltpu.VMEM((2, 4, 32, 64), BF16),
            pltpu.VMEM((2, 4, 32, 64), F32),
            pltpu.VMEM((4, 32), F32),
            pltpu.VMEM((1, 512), F32),
            pltpu.VMEM((1, 512), F32),
            pltpu.VMEM((2, STEPS + 1, 2, 32, 128), BF16),
            pltpu.VMEM((2, 32, 256), F32),
            pltpu.VMEM((slots, 2, 64, 128), BF16),
            pltpu.VMEM((4, 32, 128), BF16),
            pltpu.VMEM((4, 32, 128), BF16),
            pltpu.VMEM((slots, 4, 512, 128), BF16),
            pltpu.VMEM((slots, 256, 128), BF16),
            pltpu.VMEM((slots, 256, 128), BF16),
            pltpu.VMEM((64, 128), BF16),
            pltpu.VMEM((64, 128), BF16),
            pltpu.VMEM((512, 128), BF16),
            pltpu.VMEM((512, 128), BF16),
            pltpu.VMEM((STEPS, 256, 128), BF16),
            pltpu.VMEM((STEPS, 256, 128), BF16),
            pltpu.VMEM((3, 3, 2, 128, 512), BF16),
            pltpu.VMEM((3, 3, 2, 128, 512), BF16),
            pltpu.VMEM((3, 3, 512, 512), BF16),
            pltpu.VMEM((3, 3, 512, 512), BF16),
            pltpu.VMEM((2, 128, 128), F32),
            pltpu.VMEM((2, 32, 256), F32),
            pltpu.VMEM((256, 256), F32),
            pltpu.VMEM((2, 4, 4, 512), BF16),
            pltpu.VMEM((2, 4, 4, 512), BF16),
            pltpu.VMEM((2, 32, 256), F32),
            dma((6,)), dma((4,)), dma((3,)), dma((3,)), dma((3, 2)), dma((3, 2)), dma((3, STEPS)), dma((3, STEPS)),
            dma((slots,)), dma((slots,)), dma((slots,)), dma((slots,)), dma((slots,)), dma((slots,)),
            dma((2,)), dma((2,)), dma((2,)), dma((2,)), dma((2,)), dma((2,)),
        ],
        compiler_params=pltpu.CompilerParams(
            collective_id=0, has_side_effects=True, vmem_limit_bytes=50 << 20
        ),
    )(
        *(pltpu.with_memory_space_constraint(array, pltpu.HBM) for array in operands)
    )
    return decoded, cell.transpose(0, 1, 3, 2)


def solution(mesh):
    return jax.shard_map(
        per_device,
        mesh=mesh,
        in_specs=(
            P(None, None, "patch", None, "hid"),
            P(None, "patch", None, "hid"),
            P(None, "patch", None, "hid"),
            P(None, None, None, None, "hid"),
            P(None, None, None, None, "hid"),
            P(None, "hid"),
            P(),
            P(),
            P(),
            P(),
        ),
        out_specs=(P(None, "patch", "hid", None), P(None, "patch", None, "hid")),
        check_vma=False,
    )
```

```python
import jax
import jax.numpy as jnp
from jax import lax
from jax.experimental import pallas as pl
from jax.experimental.pallas import tpu as pltpu
from jax.sharding import PartitionSpec as P

STEPS = 4
FAR_FIRST = (6, 5, 7, 2, 4, 1, 3)
FAR_Z = (2, 1, 3, 0)
MESH = pl.DeviceIdType.MESH
F32 = jnp.float32
BF16 = jnp.bfloat16


def swap_halves(tile):
    return jnp.concatenate([tile[..., 64:], tile[..., :64]], axis=-1)


def kernel(
    frames_hbm, hidden_hbm, cell_hbm, gate_bias_hbm, bias1_hbm, bias2_hbm, w_in, w_hid, w_first, w_second,
    decoded, cell_out,
    frames, hidden, cell_in, gate_bias, bias1, bias2,
    packed, packed_cell, own, edge_top, edge_bot, image, halo_top, halo_bot,
    spread, win_out, win_in, frame_top, frame_bot,
    wi, wh, w1, w2, bias_col, cell, gin, dec_out, dec_in, cell_back,
    in_sem, w_sem, wx_send, wx_recv, s_send, s_recv, f_send, f_recv,
    x_send, x_recv, ht_send, ht_recv, hb_send, hb_recv, fin_send, fin_recv, c2_send, c2_recv, d_send, d_recv,
):
    patch = lax.axis_index("patch")
    hid = lax.axis_index("hid")
    core = lax.rem(hid, 2)
    grp = hid // 2
    x_hi = grp // 4
    y = patch // 2
    x_lo = lax.rem(patch, 2)
    flip = lax.rem(x_hi + y, 2)
    block = y * 2 + lax.rem(x_lo + flip, 2)

    def holder(blk, g, c):
        by = blk // 2
        lo = lax.rem(lax.rem(blk, 2) + g // 4 + by, 2)
        return (by * 2 + lo, g * 2 + c)

    def trade(c):
        return (y * 2 + lax.rem(x_lo + flip, 2), grp * 2 + c)

    has_up = block > 0
    has_down = block < 7
    sibling = (patch, grp * 2 + 1 - core)
    z = lax.rem(grp, 4)
    group_patch = [holder(block, g, 0)[0] for g in (0, 4)]
    up_patch = [holder(block - 1, g, 0)[0] for g in (0, 4)]
    down_patch = [holder(block + 1, g, 0)[0] for g in (0, 4)]
    cross_patch = jnp.where(x_hi == 0, group_patch[1], group_patch[0])

    def peer(d):
        hi = 1 - x_hi if d >= 4 else x_hi
        return (cross_patch if d >= 4 else patch, (hi * 4 + lax.rem(z + d % 4, 4)) * 2 + core)

    above_same = (jnp.where(x_hi == 0, up_patch[0], up_patch[1]), hid)
    below_same = (jnp.where(x_hi == 0, down_patch[0], down_patch[1]), hid)

    def above(k):
        return (up_patch[k % 2], (k % 2 * 4 + lax.rem(z + FAR_Z[k // 2], 4)) * 2 + core)

    def below(k):
        return (down_patch[k % 2], (k % 2 * 4 + lax.rem(z + FAR_Z[k // 2], 4)) * 2 + core)

    in_copies = []
    loads = (
        (frames_hbm, frames), (hidden_hbm, hidden), (cell_hbm, cell_in),
        (gate_bias_hbm, gate_bias), (bias1_hbm, bias1), (bias2_hbm, bias2),
    )
    for k, (src, dst) in enumerate(loads):
        copy = pltpu.make_async_copy(src, dst, in_sem.at[k])
        copy.start()
        in_copies.append(copy)

    barrier = pltpu.get_barrier_semaphore()

    def greet(device):
        pl.semaphore_signal(barrier, inc=1, device_id=device, device_id_type=MESH)

    greet(sibling)

    @pl.when(flip == 1)
    def _():
        greet(trade(0))
        greet(trade(1))

    for d in FAR_FIRST:
        greet(peer(d))

    @pl.when(has_up)
    def _():
        for g in range(8):
            greet(above(g))

    @pl.when(has_down)
    def _():
        for g in range(8):
            greet(below(g))

    weight_copies = []
    for k, (src, dst) in enumerate(((w_in, wi), (w_hid, wh))):
        copy = pltpu.make_async_copy(src, dst.at[:, :, core], w_sem.at[k])
        copy.start()
        weight_copies.append(copy)
    first_parts = [(w_first.at[:, :, :, k], w1.at[:, :, k]) for k in range(2)]
    for k, (src, dst) in enumerate((*first_parts, (w_second, w2))):
        copy = pltpu.make_async_copy(src, dst, w_sem.at[2 + k])
        copy.start()
        weight_copies.append(copy)

    for copy in in_copies:
        copy.wait()
    for b in range(2):
        for i in range(2):
            packed[b, 0, i] = jnp.concatenate([hidden[b, i], hidden[b, i + 2]], axis=-1)
            for t in range(STEPS):
                packed[b, 1 + t, i] = jnp.concatenate([frames[t, b, i], frames[t, b, i + 2]], axis=-1)
        packed_cell[b] = jnp.concatenate([cell_in[b, r] for r in (0, 2, 1, 3)], axis=-1)
    eye = lax.broadcasted_iota(jnp.int32, (32, 32), 0) == lax.broadcasted_iota(jnp.int32, (32, 32), 1)
    for k in range(4):
        column = jnp.sum(jnp.where(eye, gate_bias[k : k + 1, :], 0.0), axis=1, keepdims=True)
        bias_col[core, k * 32 : (k + 1) * 32, :] = jnp.broadcast_to(column, (32, 128))

    @pl.when(block == 0)
    def _():
        halo_top[...] = jnp.zeros_like(halo_top)
        win_in[0] = jnp.zeros_like(win_in[0])

    @pl.when(block == 7)
    def _():
        halo_bot[...] = jnp.zeros_like(halo_bot)
        win_in[2] = jnp.zeros_like(win_in[2])

    lane_in = lax.broadcasted_iota(jnp.int32, (256, 512), 0)
    lane_out = lax.broadcasted_iota(jnp.int32, (256, 512), 1)
    row_in = lane_in // 128 + 2 * (lax.rem(lane_in, 128) // 64)
    row_out = lax.rem(lane_out, 64) // 16
    col_out = lane_out // 64 * 8 - 2 + lax.rem(lane_out, 16)
    taken = (row_in == row_out) & (lax.rem(lane_in, 64) == col_out)
    spread[...] = jnp.where(taken, 1.0, 0.0).astype(BF16)

    greeted = 1 + 2 * flip + 7 + jnp.where(has_up, 8, 0) + jnp.where(has_down, 8, 0)
    pl.semaphore_wait(barrier, greeted)

    my_rows = pl.ds(pl.multiple_of(core * 32, 32), 32)

    def trade_copy(k, c, b, rows):
        src, dst = (
            (lambda: (packed.at[b, 0:2], own.at[1:3, :, rows, :])),
            (lambda: (packed.at[b, 2:5], own.at[3:6, :, rows, :])),
            (lambda: (packed_cell.at[b], cell.at[c])),
        )[k]()
        return pltpu.make_async_remote_copy(
            src_ref=src, dst_ref=dst, send_sem=s_send.at[k, b], recv_sem=s_recv.at[k, c],
            device_id=trade(b), device_id_type=MESH,
        )

    def start_trades(kinds):
        for b in range(2):
            stays = (flip == 0) & (core == b)

            @pl.when(jnp.logical_not(stays))
            def _(b=b):
                for k in kinds:
                    trade_copy(k, core, b, my_rows).start()

    def wait_trades(kinds):
        for c in range(2):
            stays = (flip == 0) & (core == c)

            @pl.when(jnp.logical_not(stays))
            def _(c=c):
                for k in kinds:
                    trade_copy(k, c, 0, pl.ds(c * 32, 32)).wait_recv()

    start_trades((0,))

    @pl.when(flip == 0)
    def _():
        own[1:6, :, my_rows, :] = packed[core]
        cell[core] = packed_cell[core]

    def weight_trade(k, src, dst):
        return pltpu.make_async_remote_copy(
            src_ref=src, dst_ref=dst, send_sem=wx_send.at[k], recv_sem=wx_recv.at[k],
            device_id=sibling, device_id_type=MESH,
        )

    trades = [
        weight_trade(0, w_in, wi.at[:, :, core]),
        weight_trade(1, w_hid, wh.at[:, :, core]),
        weight_trade(2, bias_col.at[core], bias_col.at[core]),
    ]
    for copy in trades:
        copy.start()
    wait_trades((0,))

    half = lax.broadcasted_iota(jnp.int32, (32, 128), 1) < 64
    my_tile = pl.ds(pl.multiple_of(grp * 64, 64), 64)
    my_edge = pl.ds(pl.multiple_of(grp * 32, 32), 32)

    def pack_edges(slot):
        a = own[slot, 0]
        b = own[slot, 1]
        edge_top[slot] = jnp.where(half, a[:32], swap_halves(a[32:]))
        edge_bot[slot] = jnp.where(half, swap_halves(b[:32]), b[32:])

    def wait_bytes(ref, sem):
        pltpu.make_async_copy(ref, ref, sem).wait()

    def send(src, dst, send_sem, recv_sem, device):
        pltpu.make_async_remote_copy(
            src_ref=src, dst_ref=dst, send_sem=send_sem, recv_sem=recv_sem, device_id=device, device_id_type=MESH
        ).start()

    def send_tiles(slot, distances):
        for d in distances:
            send(own.at[slot], image.at[slot, 1:3, my_tile, :], x_send.at[slot], x_recv.at[slot], peer(d))
        image[slot, 1:3, my_tile, :] = own[slot]

    def send_edges(slot):
        pack_edges(slot)

        @pl.when(has_up)
        def _():
            for g in range(8):
                send(edge_top.at[slot], halo_bot.at[slot, my_edge, :], ht_send.at[slot], hb_recv.at[slot], above(g))

        @pl.when(has_down)
        def _():
            for g in range(8):
                send(edge_bot.at[slot], halo_top.at[slot, my_edge, :], hb_send.at[slot], ht_recv.at[slot], below(g))

    def broadcast(slot):
        send_edges(slot)
        send_tiles(slot, FAR_FIRST)

    def wait_tiles(slot):
        wait_bytes(image.at[slot, 1:3, 0:448, :], x_recv.at[slot])

    def wait_edges_sent(slot):
        @pl.when(has_up)
        def _():
            wait_bytes(halo_top.at[slot], ht_send.at[slot])

        @pl.when(has_down)
        def _():
            wait_bytes(halo_bot.at[slot], hb_send.at[slot])

    def wait_sent(slot):
        wait_bytes(image.at[slot, 1:3, 0:448, :], x_send.at[slot])
        wait_edges_sent(slot)

    my_half = pl.ds(pl.multiple_of(x_hi * 256, 256), 256)
    cross_tile = pl.ds(pl.multiple_of((1 - x_hi) * 256 + z * 64, 64), 64)

    def frame_first(t):
        slot = 2 + t
        send(
            own.at[slot, 1], image.at[slot, 2, my_tile, :], f_send.at[0, t], f_recv.at[0, t], peer(4)
        )
        send_tiles(slot, (2, 1, 3))

    def frame_second(t):
        slot = 2 + t
        wait_bytes(image.at[slot, 2, 0:64, :], f_recv.at[0, t])
        cross = image.at[slot, 2, cross_tile, :]
        for d in (2, 1, 3):
            send(cross, cross, f_send.at[1, t], f_recv.at[1, t], peer(d))
        wait_bytes(image.at[slot, 1:3, 0:192, :], x_recv.at[slot])
        half_ref = image.at[slot, 1, my_half, :]
        send(half_ref, half_ref, f_send.at[2, t], f_recv.at[2, t], peer(4))

    def frame_wait(t):
        slot = 2 + t
        wait_bytes(image.at[slot, 2, 0:192, :], f_recv.at[1, t])
        wait_bytes(image.at[slot, 1, 0:256, :], f_recv.at[2, t])

    def frame_edges(t):
        slot = 2 + t
        for g in range(8):
            first = slice(g * 64, g * 64 + 32)
            later = slice(g * 64 + 32, g * 64 + 64)
            rows = slice(g * 32, g * 32 + 32)
            frame_top[t, rows] = jnp.where(half, image[slot, 1, first], swap_halves(image[slot, 1, later]))
            frame_bot[t, rows] = jnp.where(half, swap_halves(image[slot, 2, first]), image[slot, 2, later])

        @pl.when(has_up)
        def _():
            send(frame_top.at[t], halo_bot.at[slot], ht_send.at[slot], hb_recv.at[slot], above_same)

        @pl.when(has_down)
        def _():
            send(frame_bot.at[t], halo_top.at[slot], hb_send.at[slot], ht_recv.at[slot], below_same)

    def wait_halos(slot):
        @pl.when(has_up)
        def _():
            wait_bytes(halo_top.at[slot], ht_recv.at[slot])

        @pl.when(has_down)
        def _():
            wait_bytes(halo_bot.at[slot], hb_recv.at[slot])

        for g in range(8):
            a0 = image[slot, 1, g * 64 : g * 64 + 32]
            a1 = image[slot, 1, g * 64 + 32 : g * 64 + 64]
            b0 = image[slot, 2, g * 64 : g * 64 + 32]
            b1 = image[slot, 2, g * 64 + 32 : g * 64 + 64]
            top = halo_top[slot, g * 32 : g * 32 + 32, :]
            bot = halo_bot[slot, g * 32 : g * 32 + 32, :]
            image[slot, 0, g * 64 : g * 64 + 32] = jnp.where(half, top, swap_halves(b0))
            image[slot, 0, g * 64 + 32 : g * 64 + 64] = swap_halves(jnp.where(half, b1, top))
            image[slot, 3, g * 64 : g * 64 + 32] = swap_halves(jnp.where(half, bot, a0))
            image[slot, 3, g * 64 + 32 : g * 64 + 64] = jnp.where(half, swap_halves(a1), bot)

    place = lax.rem(lax.broadcasted_iota(jnp.int32, (256, 128), 1), 64)

    def conv(slot, weight, write):
        def tap(p, q):
            lhs = weight[p, q].reshape(256, 512)
            rhs = jnp.concatenate([image[slot, p], image[slot, p + 1]], axis=1)
            return jnp.dot(lhs, rhs, preferred_element_type=F32)

        parts = [tap(1, q) for q in range(3)]
        wait_halos(slot)
        parts = [parts[q] + tap(0, q) + tap(2, q) for q in range(3)]
        for tile in range(2):
            lanes = slice(tile * 128, (tile + 1) * 128)
            left = jnp.where(place == 0, 0.0, pltpu.roll(parts[0][:, lanes], 1, 1))
            right = jnp.where(place == 63, 0.0, pltpu.roll(parts[2][:, lanes], 127, 1))
            write(tile, lanes, parts[1][:, lanes] + left + right)

    frame_first(0)
    broadcast(1)
    send_edges(2)
    start_trades((1, 2))
    frame_second(0)
    wait_trades((1, 2))
    frame_first(1)
    send_edges(3)
    weight_copies[0].wait()
    weight_copies[1].wait()
    for copy in trades:
        copy.wait_recv()

    def write_gin(tile, lanes, value):
        for c in range(2):
            rows = slice(c * 128, (c + 1) * 128)
            gin[rows, lanes] = value[rows] + bias_col[c]

    def update(next_slot):
        def write(tile, lanes, value):
            gates = value + gin[:, lanes]
            for c in range(2):
                z = [gates[c * 128 + k * 32 : c * 128 + (k + 1) * 32] for k in range(4)]
                new = jax.nn.sigmoid(z[1] + 1.0) * cell[c, :, lanes] + jax.nn.sigmoid(z[0]) * jnp.tanh(z[2])
                cell[c, :, lanes] = new
                own[next_slot, tile, c * 32 : (c + 1) * 32] = (jax.nn.sigmoid(z[3]) * jnp.tanh(new)).astype(BF16)

        return write

    def step(t, carry):
        slot = lax.rem(t + 1, 2)
        following = lax.rem(t, 2)

        frame_wait(t)

        @pl.when(t > 1)
        def _():
            frame_edges(t)

        @pl.when((t > 0) & (t < STEPS - 1))
        def _():
            frame_second(t + 1)

        @pl.when(t < STEPS - 2)
        def _():
            frame_first(t + 2)

        conv(2 + t, wi, write_gin)

        @pl.when(t == 0)
        def _():
            frame_second(t + 1)

        @pl.when(t > 0)
        def _():
            wait_sent(following)

        wait_tiles(slot)
        conv(slot, wh, update(following))

        @pl.when(t < STEPS - 1)
        def _():
            broadcast(following)

        return carry

    lax.fori_loop(0, STEPS, step, 0)

    last = (STEPS + 1) % 2
    windows = jnp.dot(own[last, 0], spread[0:128, :], preferred_element_type=F32)
    windows = (windows + jnp.dot(own[last, 1], spread[128:256, :], preferred_element_type=F32)).astype(BF16)
    for k in range(4):
        low = windows[:32, k * 128 : (k + 1) * 128]
        high = windows[32:, k * 128 : (k + 1) * 128]
        win_out[2 * k] = jnp.where(half, low, swap_halves(high))
        win_out[2 * k + 1] = jnp.where(half, swap_halves(low), high)

    @pl.when(has_up)
    def _():
        for k in range(8):
            device = above(k)
            send(win_out.at[device[1] // 2], win_in.at[2, my_edge, :], fin_send.at[0], fin_recv.at[0], device)

    @pl.when(has_down)
    def _():
        for k in range(8):
            device = below(k)
            send(win_out.at[device[1] // 2], win_in.at[0, my_edge, :], fin_send.at[1], fin_recv.at[1], device)

    for d in FAR_FIRST:
        device = peer(d)
        send(win_out.at[device[1] // 2], win_in.at[1, my_edge, :], fin_send.at[2], fin_recv.at[2], device)
    win_in[1, my_edge, :] = win_out[grp]

    def cell_copy(c, b):
        return pltpu.make_async_remote_copy(
            src_ref=cell.at[c], dst_ref=cell_back.at[b],
            send_sem=c2_send.at[c], recv_sem=c2_recv.at[b],
            device_id=trade(c), device_id_type=MESH,
        )

    for c in range(2):
        stays = (flip == 0) & (core == c)

        @pl.when(jnp.logical_not(stays))
        def _(c=c):
            cell_copy(c, core).start()

        @pl.when(stays)
        def _(c=c):
            cell_back[core] = cell[c]

    for copy in weight_copies[2:]:
        copy.wait()
    wait_bytes(win_in.at[1, 0:224, :], fin_recv.at[2])

    @pl.when(has_down)
    def _():
        wait_bytes(win_in.at[2], fin_recv.at[0])

    @pl.when(has_up)
    def _():
        wait_bytes(win_in.at[0], fin_recv.at[1])

    unit = lax.broadcasted_iota(jnp.int32, (128, 128), 0) == lax.broadcasted_iota(jnp.int32, (128, 128), 1)
    unit = jnp.where(unit, 1.0, 0.0).astype(BF16)

    def window(k, first, stop):
        turned = lax.dot_general(unit, win_in[k], (((1,), (1,)), ((), ())), preferred_element_type=F32).astype(BF16)
        return jnp.concatenate([turned[first:stop], turned[64 + first : 64 + stop]], axis=1)

    pixels = jnp.concatenate([window(0, 32, 64), window(1, 0, 64), window(2, 0, 32)], axis=0)

    def decode(source, rows, weight):
        parts = []
        for q in range(3):
            total = None
            for p in range(3):
                term = jnp.dot(source[p * 16 : p * 16 + rows * 16], weight(p, q), preferred_element_type=F32)
                total = term if total is None else total + term
            parts.append(total)
        return parts[1] + pltpu.roll(parts[0], 1, 0) + pltpu.roll(parts[2], rows * 16 - 1, 0)

    first = decode(pixels, 6, lambda p, q: w1[p, q].reshape(512, 512)) + bias1[...]
    first = first / (1.0 + jnp.exp(-first))
    pixel = lax.broadcasted_iota(jnp.int32, (96, 512), 0)
    image_row = block * 4 - 1 + pixel // 16
    image_col = grp * 8 - 2 + lax.rem(pixel, 16)
    inside = (image_row >= 0) & (image_row < 32) & (image_col >= 0) & (image_col < 64)
    middle = jnp.where(inside, first, 0.0).astype(BF16)
    second = decode(middle, 4, lambda p, q: w2[p, q]) + bias2[...]
    shifted = second.reshape(4, 16, 512)
    for c in range(2):
        dec_out[c] = shifted[:, 2 + 4 * c : 6 + 4 * c, :].astype(BF16)

    def dec_copy(c, b):
        return pltpu.make_async_remote_copy(
            src_ref=dec_out.at[c], dst_ref=dec_in.at[b],
            send_sem=d_send.at[c], recv_sem=d_recv.at[b],
            device_id=trade(c), device_id_type=MESH,
        )

    for c in range(2):
        stays = (flip == 0) & (core == c)

        @pl.when(jnp.logical_not(stays))
        def _(c=c):
            dec_copy(c, core).start()

        @pl.when(stays)
        def _(c=c):
            dec_in[core] = dec_out[c]

    for b in range(2):
        stays = (flip == 0) & (core == b)

        @pl.when(jnp.logical_not(stays))
        def _(b=b):
            cell_copy(0, b).wait_recv()

        for r in range(4):
            start = (r % 2) * 128 + (r // 2) * 64
            cell_out[b, r] = cell_back[b, :, start : start + 64]

    for t in range(STEPS):
        wait_bytes(image.at[2 + t, 1:3, 0:192, :], x_send.at[2 + t])
        wait_bytes(image.at[2 + t, 2, 0:64, :], f_send.at[0, t])
        wait_bytes(image.at[2 + t, 2, 0:192, :], f_send.at[1, t])
        wait_bytes(image.at[2 + t, 1, 0:256, :], f_send.at[2, t])
        wait_edges_sent(2 + t)
    wait_sent(1 - last)
    wait_bytes(win_in.at[1, 0:224, :], fin_send.at[2])

    @pl.when(has_up)
    def _():
        wait_bytes(win_in.at[0], fin_send.at[0])

    @pl.when(has_down)
    def _():
        wait_bytes(win_in.at[2], fin_send.at[1])

    for copy in trades:
        copy.wait_send()

    for b in range(2):
        stays = (flip == 0) & (core == b)

        @pl.when(jnp.logical_not(stays))
        def _(b=b):
            for k in range(3):
                trade_copy(k, core, b, my_rows).wait_send()
            cell_copy(b, core).wait_send()
            dec_copy(0, b).wait_recv()
            dec_copy(b, core).wait_send()

        decoded[b] = dec_in[b]


def per_device(
    frames, hidden_start, cell_start, input_weight, hidden_weight, gate_bias,
    first_weight, first_bias, second_weight, second_bias,
):
    vmem = pl.BlockSpec(memory_space=pltpu.VMEM)
    hbm = pl.BlockSpec(memory_space=pltpu.HBM)
    dma = pltpu.SemaphoreType.DMA
    slots = STEPS + 2

    def gate_rows(weight):
        return weight.transpose(0, 1, 3, 4, 2).reshape(3, 3, 128, 512)

    operands = (
        frames.transpose(0, 1, 2, 4, 3),
        hidden_start.transpose(0, 1, 3, 2),
        cell_start.transpose(0, 1, 3, 2),
        gate_bias,
        first_bias.reshape(1, -1),
        second_bias.reshape(1, -1),
        gate_rows(input_weight),
        gate_rows(hidden_weight),
        first_weight.reshape(3, 3, 8, 2, 32, 512),
        second_weight,
    )
    decoded, cell = pl.pallas_call(
        kernel,
        name="convlstm",
        out_shape=(
            jax.ShapeDtypeStruct((2, 4, 4, 512), BF16),
            jax.ShapeDtypeStruct((2, 4, 32, 64), F32),
        ),
        in_specs=[hbm] * 10,
        out_specs=(vmem, vmem),
        scratch_shapes=[
            pltpu.VMEM((STEPS, 2, 4, 32, 64), BF16),
            pltpu.VMEM((2, 4, 32, 64), BF16),
            pltpu.VMEM((2, 4, 32, 64), F32),
            pltpu.VMEM((4, 32), F32),
            pltpu.VMEM((1, 512), F32),
            pltpu.VMEM((1, 512), F32),
            pltpu.VMEM((2, STEPS + 1, 2, 32, 128), BF16),
            pltpu.VMEM((2, 32, 256), F32),
            pltpu.VMEM((slots, 2, 64, 128), BF16),
            pltpu.VMEM((4, 32, 128), BF16),
            pltpu.VMEM((4, 32, 128), BF16),
            pltpu.VMEM((slots, 4, 512, 128), BF16),
            pltpu.VMEM((slots, 256, 128), BF16),
            pltpu.VMEM((slots, 256, 128), BF16),
            pltpu.VMEM((256, 512), BF16),
            pltpu.VMEM((8, 32, 128), BF16),
            pltpu.VMEM((3, 256, 128), BF16),
            pltpu.VMEM((STEPS, 256, 128), BF16),
            pltpu.VMEM((STEPS, 256, 128), BF16),
            pltpu.VMEM((3, 3, 2, 128, 512), BF16),
            pltpu.VMEM((3, 3, 2, 128, 512), BF16),
            pltpu.VMEM((3, 3, 2, 8, 32, 512), BF16),
            pltpu.VMEM((3, 3, 512, 512), BF16),
            pltpu.VMEM((2, 128, 128), F32),
            pltpu.VMEM((2, 32, 256), F32),
            pltpu.VMEM((256, 256), F32),
            pltpu.VMEM((2, 4, 4, 512), BF16),
            pltpu.VMEM((2, 4, 4, 512), BF16),
            pltpu.VMEM((2, 32, 256), F32),
            dma((6,)), dma((5,)), dma((3,)), dma((3,)), dma((3, 2)), dma((3, 2)), dma((3, STEPS)), dma((3, STEPS)),
            dma((slots,)), dma((slots,)), dma((slots,)), dma((slots,)), dma((slots,)), dma((slots,)),
            dma((3,)), dma((3,)), dma((2,)), dma((2,)), dma((2,)), dma((2,)),
        ],
        compiler_params=pltpu.CompilerParams(
            collective_id=0, has_side_effects=True, vmem_limit_bytes=50 << 20
        ),
    )(
        *(pltpu.with_memory_space_constraint(array, pltpu.HBM) for array in operands)
    )
    return decoded, cell.transpose(0, 1, 3, 2)


def solution(mesh):
    return jax.shard_map(
        per_device,
        mesh=mesh,
        in_specs=(
            P(None, None, "patch", None, "hid"),
            P(None, "patch", None, "hid"),
            P(None, "patch", None, "hid"),
            P(None, None, None, None, "hid"),
            P(None, None, None, None, "hid"),
            P(None, "hid"),
            P(),
            P(),
            P(),
            P(),
        ),
        out_specs=(P(None, "patch", "hid", None), P(None, "patch", None, "hid")),
        check_vma=False,
    )
```

```python
import jax
import jax.numpy as jnp
from jax import lax
from jax.experimental import pallas as pl
from jax.experimental.pallas import tpu as pltpu
from jax.sharding import PartitionSpec as P

STEPS = 4
FAR_FIRST = (6, 5, 7, 2, 4, 1, 3)
FAR_Z = (2, 1, 3, 0)
MESH = pl.DeviceIdType.MESH
F32 = jnp.float32
BF16 = jnp.bfloat16


def swap_halves(tile):
    return jnp.concatenate([tile[..., 64:], tile[..., :64]], axis=-1)


def kernel(
    frames_hbm, hidden_hbm, cell_hbm, gate_bias_hbm, bias1_hbm, bias2_hbm, w_in, w_hid, w_first, w_second,
    decoded, cell_out,
    frames, hidden, cell_in, gate_bias, bias1, bias2,
    packed, packed_cell, own, edge_top, edge_bot, image, halo_top, halo_bot,
    spread, win_out, win_in, frame_top, frame_bot,
    wi, wh, w1, w2, bias_col, cell, gin, dec_out, dec_in, cell_back,
    in_sem, w_sem, wx_send, wx_recv, s_send, s_recv, f_send, f_recv,
    x_send, x_recv, ht_send, ht_recv, hb_send, hb_recv, fin_send, fin_recv, c2_send, c2_recv, d_send, d_recv,
):
    patch = lax.axis_index("patch")
    hid = lax.axis_index("hid")
    core = lax.rem(hid, 2)
    grp = hid // 2
    x_hi = grp // 4
    y = patch // 2
    x_lo = lax.rem(patch, 2)
    flip = lax.rem(x_hi + y, 2)
    block = y * 2 + lax.rem(x_lo + flip, 2)

    def holder(blk, g, c):
        by = blk // 2
        lo = lax.rem(lax.rem(blk, 2) + g // 4 + by, 2)
        return (by * 2 + lo, g * 2 + c)

    def trade(c):
        return (y * 2 + lax.rem(x_lo + flip, 2), grp * 2 + c)

    has_up = block > 0
    has_down = block < 7
    sibling = (patch, grp * 2 + 1 - core)
    z = lax.rem(grp, 4)
    group_patch = [holder(block, g, 0)[0] for g in (0, 4)]
    up_patch = [holder(block - 1, g, 0)[0] for g in (0, 4)]
    down_patch = [holder(block + 1, g, 0)[0] for g in (0, 4)]
    cross_patch = jnp.where(x_hi == 0, group_patch[1], group_patch[0])

    def peer(d):
        hi = 1 - x_hi if d >= 4 else x_hi
        return (cross_patch if d >= 4 else patch, (hi * 4 + lax.rem(z + d % 4, 4)) * 2 + core)

    above_same = (jnp.where(x_hi == 0, up_patch[0], up_patch[1]), hid)
    below_same = (jnp.where(x_hi == 0, down_patch[0], down_patch[1]), hid)

    def above(k):
        return (up_patch[k % 2], (k % 2 * 4 + lax.rem(z + FAR_Z[k // 2], 4)) * 2 + core)

    def below(k):
        return (down_patch[k % 2], (k % 2 * 4 + lax.rem(z + FAR_Z[k // 2], 4)) * 2 + core)

    in_copies = []
    loads = (
        (frames_hbm, frames), (hidden_hbm, hidden), (cell_hbm, cell_in),
        (gate_bias_hbm, gate_bias), (bias1_hbm, bias1), (bias2_hbm, bias2),
    )
    for k, (src, dst) in enumerate(loads):
        copy = pltpu.make_async_copy(src, dst, in_sem.at[k])
        copy.start()
        in_copies.append(copy)

    barrier = pltpu.get_barrier_semaphore()

    def greet(device):
        pl.semaphore_signal(barrier, inc=1, device_id=device, device_id_type=MESH)

    greet(sibling)

    @pl.when(flip == 1)
    def _():
        greet(trade(0))
        greet(trade(1))

    for d in FAR_FIRST:
        greet(peer(d))

    @pl.when(has_up)
    def _():
        for g in range(8):
            greet(above(g))

    @pl.when(has_down)
    def _():
        for g in range(8):
            greet(below(g))

    weight_copies = []
    for k, (src, dst) in enumerate(((w_in, wi), (w_hid, wh))):
        copy = pltpu.make_async_copy(src, dst.at[:, :, core], w_sem.at[k])
        copy.start()
        weight_copies.append(copy)
    first_parts = [(w_first.at[:, :, :, k], w1.at[:, :, k]) for k in range(2)]
    for k, (src, dst) in enumerate((*first_parts, (w_second, w2))):
        copy = pltpu.make_async_copy(src, dst, w_sem.at[2 + k])
        copy.start()
        weight_copies.append(copy)

    for copy in in_copies:
        copy.wait()
    for b in range(2):
        for i in range(2):
            packed[b, 0, i] = jnp.concatenate([hidden[b, i], hidden[b, i + 2]], axis=-1)
            for t in range(STEPS):
                packed[b, 1 + t, i] = jnp.concatenate([frames[t, b, i], frames[t, b, i + 2]], axis=-1)
        packed_cell[b] = jnp.concatenate([cell_in[b, r] for r in (0, 2, 1, 3)], axis=-1)
    eye = lax.broadcasted_iota(jnp.int32, (32, 32), 0) == lax.broadcasted_iota(jnp.int32, (32, 32), 1)
    for k in range(4):
        column = jnp.sum(jnp.where(eye, gate_bias[k : k + 1, :], 0.0), axis=1, keepdims=True)
        bias_col[core, k * 32 : (k + 1) * 32, :] = jnp.broadcast_to(column, (32, 128))

    @pl.when(block == 0)
    def _():
        halo_top[...] = jnp.zeros_like(halo_top)
        win_in[0] = jnp.zeros_like(win_in[0])

    @pl.when(block == 7)
    def _():
        halo_bot[...] = jnp.zeros_like(halo_bot)
        win_in[2] = jnp.zeros_like(win_in[2])

    lane_in = lax.broadcasted_iota(jnp.int32, (256, 512), 0)
    lane_out = lax.broadcasted_iota(jnp.int32, (256, 512), 1)
    row_in = lane_in // 128 + 2 * (lax.rem(lane_in, 128) // 64)
    row_out = lax.rem(lane_out, 64) // 16
    col_out = lane_out // 64 * 8 - 2 + lax.rem(lane_out, 16)
    taken = (row_in == row_out) & (lax.rem(lane_in, 64) == col_out)
    spread[...] = jnp.where(taken, 1.0, 0.0).astype(BF16)

    greeted = 1 + 2 * flip + 7 + jnp.where(has_up, 8, 0) + jnp.where(has_down, 8, 0)
    pl.semaphore_wait(barrier, greeted)

    my_rows = pl.ds(pl.multiple_of(core * 32, 32), 32)

    def trade_copy(k, c, b, rows):
        src, dst = (
            (lambda: (packed.at[b, 0:2], own.at[1:3, :, rows, :])),
            (lambda: (packed.at[b, 2:5], own.at[3:6, :, rows, :])),
            (lambda: (packed_cell.at[b], cell.at[c])),
        )[k]()
        return pltpu.make_async_remote_copy(
            src_ref=src, dst_ref=dst, send_sem=s_send.at[k, b], recv_sem=s_recv.at[k, c],
            device_id=trade(b), device_id_type=MESH,
        )

    def start_trades(kinds):
        for b in range(2):
            stays = (flip == 0) & (core == b)

            @pl.when(jnp.logical_not(stays))
            def _(b=b):
                for k in kinds:
                    trade_copy(k, core, b, my_rows).start()

    def wait_trades(kinds):
        for c in range(2):
            stays = (flip == 0) & (core == c)

            @pl.when(jnp.logical_not(stays))
            def _(c=c):
                for k in kinds:
                    trade_copy(k, c, 0, pl.ds(c * 32, 32)).wait_recv()

    start_trades((0,))

    @pl.when(flip == 0)
    def _():
        own[1:6, :, my_rows, :] = packed[core]
        cell[core] = packed_cell[core]

    def weight_trade(k, src, dst):
        return pltpu.make_async_remote_copy(
            src_ref=src, dst_ref=dst, send_sem=wx_send.at[k], recv_sem=wx_recv.at[k],
            device_id=sibling, device_id_type=MESH,
        )

    trades = [
        weight_trade(0, w_in, wi.at[:, :, core]),
        weight_trade(1, w_hid, wh.at[:, :, core]),
        weight_trade(2, bias_col.at[core], bias_col.at[core]),
    ]
    wait_trades((0,))

    half = lax.broadcasted_iota(jnp.int32, (32, 128), 1) < 64
    my_tile = pl.ds(pl.multiple_of(grp * 64, 64), 64)
    my_edge = pl.ds(pl.multiple_of(grp * 32, 32), 32)

    def pack_edges(slot):
        a = own[slot, 0]
        b = own[slot, 1]
        edge_top[slot] = jnp.where(half, a[:32], swap_halves(a[32:]))
        edge_bot[slot] = jnp.where(half, swap_halves(b[:32]), b[32:])

    def wait_bytes(ref, sem):
        pltpu.make_async_copy(ref, ref, sem).wait()

    def send(src, dst, send_sem, recv_sem, device):
        pltpu.make_async_remote_copy(
            src_ref=src, dst_ref=dst, send_sem=send_sem, recv_sem=recv_sem, device_id=device, device_id_type=MESH
        ).start()

    def send_tiles(slot, distances):
        for d in distances:
            send(own.at[slot], image.at[slot, 1:3, my_tile, :], x_send.at[slot], x_recv.at[slot], peer(d))
        image[slot, 1:3, my_tile, :] = own[slot]

    def send_edges(slot):
        pack_edges(slot)

        @pl.when(has_up)
        def _():
            for g in range(8):
                send(edge_top.at[slot], halo_bot.at[slot, my_edge, :], ht_send.at[slot], hb_recv.at[slot], above(g))

        @pl.when(has_down)
        def _():
            for g in range(8):
                send(edge_bot.at[slot], halo_top.at[slot, my_edge, :], hb_send.at[slot], ht_recv.at[slot], below(g))

    def broadcast(slot):
        send_edges(slot)
        send_tiles(slot, FAR_FIRST)

    def wait_tiles(slot):
        wait_bytes(image.at[slot, 1:3, 0:448, :], x_recv.at[slot])

    def wait_edges_sent(slot):
        @pl.when(has_up)
        def _():
            wait_bytes(halo_top.at[slot], ht_send.at[slot])

        @pl.when(has_down)
        def _():
            wait_bytes(halo_bot.at[slot], hb_send.at[slot])

    def wait_sent(slot):
        wait_bytes(image.at[slot, 1:3, 0:448, :], x_send.at[slot])
        wait_edges_sent(slot)

    my_half = pl.ds(pl.multiple_of(x_hi * 256, 256), 256)
    cross_tile = pl.ds(pl.multiple_of((1 - x_hi) * 256 + z * 64, 64), 64)

    def frame_first(t):
        slot = 2 + t
        send(
            own.at[slot, 1], image.at[slot, 2, my_tile, :], f_send.at[0, t], f_recv.at[0, t], peer(4)
        )
        send_tiles(slot, (2, 1, 3))

    def frame_second(t):
        slot = 2 + t
        wait_bytes(image.at[slot, 2, 0:64, :], f_recv.at[0, t])
        cross = image.at[slot, 2, cross_tile, :]
        for d in (2, 1, 3):
            send(cross, cross, f_send.at[1, t], f_recv.at[1, t], peer(d))
        wait_bytes(image.at[slot, 1:3, 0:192, :], x_recv.at[slot])
        half_ref = image.at[slot, 1, my_half, :]
        send(half_ref, half_ref, f_send.at[2, t], f_recv.at[2, t], peer(4))

    def frame_wait(t):
        slot = 2 + t
        wait_bytes(image.at[slot, 2, 0:192, :], f_recv.at[1, t])
        wait_bytes(image.at[slot, 1, 0:256, :], f_recv.at[2, t])

    def frame_edges(t):
        slot = 2 + t
        for g in range(8):
            first = slice(g * 64, g * 64 + 32)
            later = slice(g * 64 + 32, g * 64 + 64)
            rows = slice(g * 32, g * 32 + 32)
            frame_top[t, rows] = jnp.where(half, image[slot, 1, first], swap_halves(image[slot, 1, later]))
            frame_bot[t, rows] = jnp.where(half, swap_halves(image[slot, 2, first]), image[slot, 2, later])

        @pl.when(has_up)
        def _():
            send(frame_top.at[t], halo_bot.at[slot], ht_send.at[slot], hb_recv.at[slot], above_same)

        @pl.when(has_down)
        def _():
            send(frame_bot.at[t], halo_top.at[slot], hb_send.at[slot], ht_recv.at[slot], below_same)

    def wait_halos(slot):
        @pl.when(has_up)
        def _():
            wait_bytes(halo_top.at[slot], ht_recv.at[slot])

        @pl.when(has_down)
        def _():
            wait_bytes(halo_bot.at[slot], hb_recv.at[slot])

        for g in range(8):
            a0 = image[slot, 1, g * 64 : g * 64 + 32]
            a1 = image[slot, 1, g * 64 + 32 : g * 64 + 64]
            b0 = image[slot, 2, g * 64 : g * 64 + 32]
            b1 = image[slot, 2, g * 64 + 32 : g * 64 + 64]
            top = halo_top[slot, g * 32 : g * 32 + 32, :]
            bot = halo_bot[slot, g * 32 : g * 32 + 32, :]
            image[slot, 0, g * 64 : g * 64 + 32] = jnp.where(half, top, swap_halves(b0))
            image[slot, 0, g * 64 + 32 : g * 64 + 64] = swap_halves(jnp.where(half, b1, top))
            image[slot, 3, g * 64 : g * 64 + 32] = swap_halves(jnp.where(half, bot, a0))
            image[slot, 3, g * 64 + 32 : g * 64 + 64] = jnp.where(half, swap_halves(a1), bot)

    place = lax.rem(lax.broadcasted_iota(jnp.int32, (256, 128), 1), 64)

    def conv(slot, weight, write):
        def tap(p, q):
            lhs = weight[p, q].reshape(256, 512)
            rhs = jnp.concatenate([image[slot, p], image[slot, p + 1]], axis=1)
            return jnp.dot(lhs, rhs, preferred_element_type=F32)

        parts = [tap(1, q) for q in range(3)]
        wait_halos(slot)
        parts = [parts[q] + tap(0, q) + tap(2, q) for q in range(3)]
        for tile in range(2):
            lanes = slice(tile * 128, (tile + 1) * 128)
            left = jnp.where(place == 0, 0.0, pltpu.roll(parts[0][:, lanes], 1, 1))
            right = jnp.where(place == 63, 0.0, pltpu.roll(parts[2][:, lanes], 127, 1))
            write(tile, lanes, parts[1][:, lanes] + left + right)

    frame_first(0)
    broadcast(1)
    send_edges(2)
    start_trades((1, 2))
    for copy in trades:
        copy.start()
    frame_second(0)
    wait_trades((1, 2))
    frame_first(1)
    send_edges(3)
    weight_copies[0].wait()
    weight_copies[1].wait()
    for copy in trades:
        copy.wait_recv()

    def write_gin(tile, lanes, value):
        for c in range(2):
            rows = slice(c * 128, (c + 1) * 128)
            gin[rows, lanes] = value[rows] + bias_col[c]

    def update(next_slot):
        def write(tile, lanes, value):
            gates = value + gin[:, lanes]
            for c in range(2):
                z = [gates[c * 128 + k * 32 : c * 128 + (k + 1) * 32] for k in range(4)]
                new = jax.nn.sigmoid(z[1] + 1.0) * cell[c, :, lanes] + jax.nn.sigmoid(z[0]) * jnp.tanh(z[2])
                cell[c, :, lanes] = new
                own[next_slot, tile, c * 32 : (c + 1) * 32] = (jax.nn.sigmoid(z[3]) * jnp.tanh(new)).astype(BF16)

        return write

    def step(t, carry):
        slot = lax.rem(t + 1, 2)
        following = lax.rem(t, 2)

        frame_wait(t)

        @pl.when(t > 1)
        def _():
            frame_edges(t)

        @pl.when((t > 0) & (t < STEPS - 1))
        def _():
            frame_second(t + 1)

        @pl.when(t < STEPS - 2)
        def _():
            frame_first(t + 2)

        conv(2 + t, wi, write_gin)

        @pl.when(t == 0)
        def _():
            frame_second(t + 1)

        @pl.when(t > 0)
        def _():
            wait_sent(following)

        wait_tiles(slot)
        conv(slot, wh, update(following))

        @pl.when(t < STEPS - 1)
        def _():
            broadcast(following)

        return carry

    lax.fori_loop(0, STEPS, step, 0)

    last = (STEPS + 1) % 2
    windows = jnp.dot(own[last, 0], spread[0:128, :], preferred_element_type=F32)
    windows = (windows + jnp.dot(own[last, 1], spread[128:256, :], preferred_element_type=F32)).astype(BF16)
    for k in range(4):
        low = windows[:32, k * 128 : (k + 1) * 128]
        high = windows[32:, k * 128 : (k + 1) * 128]
        win_out[2 * k] = jnp.where(half, low, swap_halves(high))
        win_out[2 * k + 1] = jnp.where(half, swap_halves(low), high)

    @pl.when(has_up)
    def _():
        for k in range(8):
            device = above(k)
            send(win_out.at[device[1] // 2], win_in.at[2, my_edge, :], fin_send.at[0], fin_recv.at[0], device)

    @pl.when(has_down)
    def _():
        for k in range(8):
            device = below(k)
            send(win_out.at[device[1] // 2], win_in.at[0, my_edge, :], fin_send.at[1], fin_recv.at[1], device)

    for d in FAR_FIRST:
        device = peer(d)
        send(win_out.at[device[1] // 2], win_in.at[1, my_edge, :], fin_send.at[2], fin_recv.at[2], device)
    win_in[1, my_edge, :] = win_out[grp]

    def cell_copy(c, b):
        return pltpu.make_async_remote_copy(
            src_ref=cell.at[c], dst_ref=cell_back.at[b],
            send_sem=c2_send.at[c], recv_sem=c2_recv.at[b],
            device_id=trade(c), device_id_type=MESH,
        )

    for c in range(2):
        stays = (flip == 0) & (core == c)

        @pl.when(jnp.logical_not(stays))
        def _(c=c):
            cell_copy(c, core).start()

        @pl.when(stays)
        def _(c=c):
            cell_back[core] = cell[c]

    for copy in weight_copies[2:]:
        copy.wait()
    wait_bytes(win_in.at[1, 0:224, :], fin_recv.at[2])

    @pl.when(has_down)
    def _():
        wait_bytes(win_in.at[2], fin_recv.at[0])

    @pl.when(has_up)
    def _():
        wait_bytes(win_in.at[0], fin_recv.at[1])

    unit = lax.broadcasted_iota(jnp.int32, (128, 128), 0) == lax.broadcasted_iota(jnp.int32, (128, 128), 1)
    unit = jnp.where(unit, 1.0, 0.0).astype(BF16)

    def window(k, first, stop):
        turned = lax.dot_general(unit, win_in[k], (((1,), (1,)), ((), ())), preferred_element_type=F32).astype(BF16)
        return jnp.concatenate([turned[first:stop], turned[64 + first : 64 + stop]], axis=1)

    pixels = jnp.concatenate([window(0, 32, 64), window(1, 0, 64), window(2, 0, 32)], axis=0)

    def decode(source, rows, weight):
        parts = []
        for q in range(3):
            total = None
            for p in range(3):
                term = jnp.dot(source[p * 16 : p * 16 + rows * 16], weight(p, q), preferred_element_type=F32)
                total = term if total is None else total + term
            parts.append(total)
        return parts[1] + pltpu.roll(parts[0], 1, 0) + pltpu.roll(parts[2], rows * 16 - 1, 0)

    first = decode(pixels, 6, lambda p, q: w1[p, q].reshape(512, 512)) + bias1[...]
    first = first / (1.0 + jnp.exp(-first))
    pixel = lax.broadcasted_iota(jnp.int32, (96, 512), 0)
    image_row = block * 4 - 1 + pixel // 16
    image_col = grp * 8 - 2 + lax.rem(pixel, 16)
    inside = (image_row >= 0) & (image_row < 32) & (image_col >= 0) & (image_col < 64)
    middle = jnp.where(inside, first, 0.0).astype(BF16)
    second = decode(middle, 4, lambda p, q: w2[p, q]) + bias2[...]
    shifted = second.reshape(4, 16, 512)
    for c in range(2):
        dec_out[c] = shifted[:, 2 + 4 * c : 6 + 4 * c, :].astype(BF16)

    def dec_copy(c, b):
        return pltpu.make_async_remote_copy(
            src_ref=dec_out.at[c], dst_ref=dec_in.at[b],
            send_sem=d_send.at[c], recv_sem=d_recv.at[b],
            device_id=trade(c), device_id_type=MESH,
        )

    for c in range(2):
        stays = (flip == 0) & (core == c)

        @pl.when(jnp.logical_not(stays))
        def _(c=c):
            dec_copy(c, core).start()

        @pl.when(stays)
        def _(c=c):
            dec_in[core] = dec_out[c]

    for b in range(2):
        stays = (flip == 0) & (core == b)

        @pl.when(jnp.logical_not(stays))
        def _(b=b):
            cell_copy(0, b).wait_recv()

        for r in range(4):
            start = (r % 2) * 128 + (r // 2) * 64
            cell_out[b, r] = cell_back[b, :, start : start + 64]

    for t in range(STEPS):
        wait_bytes(image.at[2 + t, 1:3, 0:192, :], x_send.at[2 + t])
        wait_bytes(image.at[2 + t, 2, 0:64, :], f_send.at[0, t])
        wait_bytes(image.at[2 + t, 2, 0:192, :], f_send.at[1, t])
        wait_bytes(image.at[2 + t, 1, 0:256, :], f_send.at[2, t])
        wait_edges_sent(2 + t)
    wait_sent(1 - last)
    wait_bytes(win_in.at[1, 0:224, :], fin_send.at[2])

    @pl.when(has_up)
    def _():
        wait_bytes(win_in.at[0], fin_send.at[0])

    @pl.when(has_down)
    def _():
        wait_bytes(win_in.at[2], fin_send.at[1])

    for copy in trades:
        copy.wait_send()

    for b in range(2):
        stays = (flip == 0) & (core == b)

        @pl.when(jnp.logical_not(stays))
        def _(b=b):
            for k in range(3):
                trade_copy(k, core, b, my_rows).wait_send()
            cell_copy(b, core).wait_send()
            dec_copy(0, b).wait_recv()
            dec_copy(b, core).wait_send()

        decoded[b] = dec_in[b]


def give_out(decoded, cell, decoded_out, cell_out, sem):
    copies = [
        pltpu.make_async_copy(decoded, decoded_out, sem.at[0]),
        pltpu.make_async_copy(cell, cell_out, sem.at[1]),
    ]
    for copy in copies:
        copy.start()
    for copy in copies:
        copy.wait()


def per_device(
    frames, hidden_start, cell_start, input_weight, hidden_weight, gate_bias,
    first_weight, first_bias, second_weight, second_bias,
):
    vmem = pl.BlockSpec(memory_space=pltpu.VMEM)
    hbm = pl.BlockSpec(memory_space=pltpu.HBM)
    dma = pltpu.SemaphoreType.DMA
    slots = STEPS + 2

    def gate_rows(weight):
        return weight.transpose(0, 1, 3, 4, 2).reshape(3, 3, 128, 512)

    operands = (
        frames.transpose(0, 1, 2, 4, 3),
        hidden_start.transpose(0, 1, 3, 2),
        cell_start.transpose(0, 1, 3, 2),
        gate_bias,
        first_bias.reshape(1, -1),
        second_bias.reshape(1, -1),
        gate_rows(input_weight),
        gate_rows(hidden_weight),
        first_weight.reshape(3, 3, 8, 2, 32, 512),
        second_weight,
    )
    decoded, cell = pl.pallas_call(
        kernel,
        name="convlstm",
        out_shape=(
            jax.ShapeDtypeStruct((2, 4, 4, 512), BF16),
            jax.ShapeDtypeStruct((2, 4, 32, 64), F32),
        ),
        in_specs=[hbm] * 10,
        out_specs=(vmem, vmem),
        scratch_shapes=[
            pltpu.VMEM((STEPS, 2, 4, 32, 64), BF16),
            pltpu.VMEM((2, 4, 32, 64), BF16),
            pltpu.VMEM((2, 4, 32, 64), F32),
            pltpu.VMEM((4, 32), F32),
            pltpu.VMEM((1, 512), F32),
            pltpu.VMEM((1, 512), F32),
            pltpu.VMEM((2, STEPS + 1, 2, 32, 128), BF16),
            pltpu.VMEM((2, 32, 256), F32),
            pltpu.VMEM((slots, 2, 64, 128), BF16),
            pltpu.VMEM((4, 32, 128), BF16),
            pltpu.VMEM((4, 32, 128), BF16),
            pltpu.VMEM((slots, 4, 512, 128), BF16),
            pltpu.VMEM((slots, 256, 128), BF16),
            pltpu.VMEM((slots, 256, 128), BF16),
            pltpu.VMEM((256, 512), BF16),
            pltpu.VMEM((8, 32, 128), BF16),
            pltpu.VMEM((3, 256, 128), BF16),
            pltpu.VMEM((STEPS, 256, 128), BF16),
            pltpu.VMEM((STEPS, 256, 128), BF16),
            pltpu.VMEM((3, 3, 2, 128, 512), BF16),
            pltpu.VMEM((3, 3, 2, 128, 512), BF16),
            pltpu.VMEM((3, 3, 2, 8, 32, 512), BF16),
            pltpu.VMEM((3, 3, 512, 512), BF16),
            pltpu.VMEM((2, 128, 128), F32),
            pltpu.VMEM((2, 32, 256), F32),
            pltpu.VMEM((256, 256), F32),
            pltpu.VMEM((2, 4, 4, 512), BF16),
            pltpu.VMEM((2, 4, 4, 512), BF16),
            pltpu.VMEM((2, 32, 256), F32),
            dma((6,)), dma((5,)), dma((3,)), dma((3,)), dma((3, 2)), dma((3, 2)), dma((3, STEPS)), dma((3, STEPS)),
            dma((slots,)), dma((slots,)), dma((slots,)), dma((slots,)), dma((slots,)), dma((slots,)),
            dma((3,)), dma((3,)), dma((2,)), dma((2,)), dma((2,)), dma((2,)),
        ],
        compiler_params=pltpu.CompilerParams(
            collective_id=0, has_side_effects=True, vmem_limit_bytes=50 << 20
        ),
    )(
        *(pltpu.with_memory_space_constraint(array, pltpu.HBM) for array in operands)
    )
    decoded, cell = pl.pallas_call(
        give_out,
        name="give_out",
        out_shape=(
            jax.ShapeDtypeStruct((2, 4, 4, 512), BF16),
            jax.ShapeDtypeStruct((2, 4, 32, 64), F32),
        ),
        in_specs=[vmem, vmem],
        out_specs=(hbm, hbm),
        scratch_shapes=[dma((2,))],
        compiler_params=pltpu.CompilerParams(vmem_limit_bytes=1 << 20),
    )(decoded, cell)
    return decoded, cell.transpose(0, 1, 3, 2)


def solution(mesh):
    return jax.shard_map(
        per_device,
        mesh=mesh,
        in_specs=(
            P(None, None, "patch", None, "hid"),
            P(None, "patch", None, "hid"),
            P(None, "patch", None, "hid"),
            P(None, None, None, None, "hid"),
            P(None, None, None, None, "hid"),
            P(None, "hid"),
            P(),
            P(),
            P(),
            P(),
        ),
        out_specs=(P(None, "patch", "hid", None), P(None, "patch", None, "hid")),
        check_vma=False,
    )
```

```python
import jax
import jax.numpy as jnp
from jax import lax
from jax.experimental import pallas as pl
from jax.experimental.pallas import tpu as pltpu
from jax.sharding import PartitionSpec as P

STEPS = 4
FAR_FIRST = (6, 5, 7, 2, 4, 1, 3)
FAR_Z = (2, 1, 3, 0)
MESH = pl.DeviceIdType.MESH
F32 = jnp.float32
BF16 = jnp.bfloat16


def swap_halves(tile):
    return jnp.concatenate([tile[..., 64:], tile[..., :64]], axis=-1)


def kernel(
    frames_hbm, hidden_hbm, cell_hbm, gate_bias_hbm, bias1_hbm, bias2_hbm, w_in, w_hid, w_first, w_second,
    decoded, cell_out,
    frames, hidden, cell_in, gate_bias, bias1, bias2,
    packed, packed_cell, own, edge_top, edge_bot, image, halo_top, halo_bot,
    spread, win_out, win_in, frame_top, frame_bot,
    wi, wh, w1, w2, bias_col, cell, gin, dec_out, dec_in, cell_back,
    in_sem, w_sem, wx_send, wx_recv, s_send, s_recv, f_send, f_recv,
    x_send, x_recv, ht_send, ht_recv, hb_send, hb_recv, fin_send, fin_recv, c2_send, c2_recv, d_send, d_recv,
):
    patch = lax.axis_index("patch")
    hid = lax.axis_index("hid")
    core = lax.rem(hid, 2)
    grp = hid // 2
    x_hi = grp // 4
    y = patch // 2
    x_lo = lax.rem(patch, 2)
    flip = lax.rem(x_hi + y, 2)
    block = y * 2 + lax.rem(x_lo + flip, 2)

    def holder(blk, g, c):
        by = blk // 2
        lo = lax.rem(lax.rem(blk, 2) + g // 4 + by, 2)
        return (by * 2 + lo, g * 2 + c)

    def trade(c):
        return (y * 2 + lax.rem(x_lo + flip, 2), grp * 2 + c)

    has_up = block > 0
    has_down = block < 7
    sibling = (patch, grp * 2 + 1 - core)
    z = lax.rem(grp, 4)
    group_patch = [holder(block, g, 0)[0] for g in (0, 4)]
    up_patch = [holder(block - 1, g, 0)[0] for g in (0, 4)]
    down_patch = [holder(block + 1, g, 0)[0] for g in (0, 4)]
    cross_patch = jnp.where(x_hi == 0, group_patch[1], group_patch[0])

    def peer(d):
        hi = 1 - x_hi if d >= 4 else x_hi
        return (cross_patch if d >= 4 else patch, (hi * 4 + lax.rem(z + d % 4, 4)) * 2 + core)

    above_same = (jnp.where(x_hi == 0, up_patch[0], up_patch[1]), hid)
    below_same = (jnp.where(x_hi == 0, down_patch[0], down_patch[1]), hid)

    def above(k):
        return (up_patch[k % 2], (k % 2 * 4 + lax.rem(z + FAR_Z[k // 2], 4)) * 2 + core)

    def below(k):
        return (down_patch[k % 2], (k % 2 * 4 + lax.rem(z + FAR_Z[k // 2], 4)) * 2 + core)

    in_copies = []
    loads = (
        (frames_hbm, frames), (hidden_hbm, hidden), (cell_hbm, cell_in),
        (gate_bias_hbm, gate_bias), (bias1_hbm, bias1), (bias2_hbm, bias2),
    )
    for k, (src, dst) in enumerate(loads):
        copy = pltpu.make_async_copy(src, dst, in_sem.at[k])
        copy.start()
        in_copies.append(copy)

    barrier = pltpu.get_barrier_semaphore()

    def greet(device):
        pl.semaphore_signal(barrier, inc=1, device_id=device, device_id_type=MESH)

    @pl.when(has_up)
    def _():
        for g in range(8):
            greet(above(g))

    @pl.when(has_down)
    def _():
        for g in range(8):
            greet(below(g))

    for d in FAR_FIRST:
        greet(peer(d))

    greet(sibling)

    @pl.when(flip == 1)
    def _():
        greet(trade(0))
        greet(trade(1))

    weight_copies = []
    for k, (src, dst) in enumerate(((w_in, wi), (w_hid, wh))):
        copy = pltpu.make_async_copy(src, dst.at[:, :, core], w_sem.at[k])
        copy.start()
        weight_copies.append(copy)
    first_parts = [(w_first.at[:, :, :, k], w1.at[:, :, k]) for k in range(2)]
    for k, (src, dst) in enumerate((*first_parts, (w_second, w2))):
        copy = pltpu.make_async_copy(src, dst, w_sem.at[2 + k])
        copy.start()
        weight_copies.append(copy)

    for copy in in_copies:
        copy.wait()
    for b in range(2):
        for i in range(2):
            packed[b, 0, i] = jnp.concatenate([hidden[b, i], hidden[b, i + 2]], axis=-1)
            for t in range(STEPS):
                packed[b, 1 + t, i] = jnp.concatenate([frames[t, b, i], frames[t, b, i + 2]], axis=-1)
        packed_cell[b] = jnp.concatenate([cell_in[b, r] for r in (0, 2, 1, 3)], axis=-1)
    eye = lax.broadcasted_iota(jnp.int32, (32, 32), 0) == lax.broadcasted_iota(jnp.int32, (32, 32), 1)
    for k in range(4):
        column = jnp.sum(jnp.where(eye, gate_bias[k : k + 1, :], 0.0), axis=1, keepdims=True)
        bias_col[core, k * 32 : (k + 1) * 32, :] = jnp.broadcast_to(column, (32, 128))

    @pl.when(block == 0)
    def _():
        halo_top[...] = jnp.zeros_like(halo_top)
        win_in[0] = jnp.zeros_like(win_in[0])

    @pl.when(block == 7)
    def _():
        halo_bot[...] = jnp.zeros_like(halo_bot)
        win_in[2] = jnp.zeros_like(win_in[2])

    lane_in = lax.broadcasted_iota(jnp.int32, (256, 512), 0)
    lane_out = lax.broadcasted_iota(jnp.int32, (256, 512), 1)
    row_in = lane_in // 128 + 2 * (lax.rem(lane_in, 128) // 64)
    row_out = lax.rem(lane_out, 64) // 16
    col_out = lane_out // 64 * 8 - 2 + lax.rem(lane_out, 16)
    taken = (row_in == row_out) & (lax.rem(lane_in, 64) == col_out)
    spread[...] = jnp.where(taken, 1.0, 0.0).astype(BF16)

    greeted = 1 + 2 * flip + 7 + jnp.where(has_up, 8, 0) + jnp.where(has_down, 8, 0)
    pl.semaphore_wait(barrier, greeted)

    my_rows = pl.ds(pl.multiple_of(core * 32, 32), 32)

    def trade_copy(k, c, b, rows):
        src, dst = (
            (lambda: (packed.at[b, 0:2], own.at[1:3, :, rows, :])),
            (lambda: (packed.at[b, 2:5], own.at[3:6, :, rows, :])),
            (lambda: (packed_cell.at[b], cell.at[c])),
        )[k]()
        return pltpu.make_async_remote_copy(
            src_ref=src, dst_ref=dst, send_sem=s_send.at[k, b], recv_sem=s_recv.at[k, c],
            device_id=trade(b), device_id_type=MESH,
        )

    def start_trades(kinds):
        for b in range(2):
            stays = (flip == 0) & (core == b)

            @pl.when(jnp.logical_not(stays))
            def _(b=b):
                for k in kinds:
                    trade_copy(k, core, b, my_rows).start()

    def wait_trades(kinds):
        for c in range(2):
            stays = (flip == 0) & (core == c)

            @pl.when(jnp.logical_not(stays))
            def _(c=c):
                for k in kinds:
                    trade_copy(k, c, 0, pl.ds(c * 32, 32)).wait_recv()

    start_trades((0,))

    @pl.when(flip == 0)
    def _():
        own[1:6, :, my_rows, :] = packed[core]
        cell[core] = packed_cell[core]

    def weight_trade(k, src, dst):
        return pltpu.make_async_remote_copy(
            src_ref=src, dst_ref=dst, send_sem=wx_send.at[k], recv_sem=wx_recv.at[k],
            device_id=sibling, device_id_type=MESH,
        )

    trades = [
        weight_trade(0, w_in, wi.at[:, :, core]),
        weight_trade(1, w_hid, wh.at[:, :, core]),
        weight_trade(2, bias_col.at[core], bias_col.at[core]),
    ]
    wait_trades((0,))

    half = lax.broadcasted_iota(jnp.int32, (32, 128), 1) < 64
    my_tile = pl.ds(pl.multiple_of(grp * 64, 64), 64)
    my_edge = pl.ds(pl.multiple_of(grp * 32, 32), 32)

    def pack_edges(slot):
        a = own[slot, 0]
        b = own[slot, 1]
        edge_top[slot] = jnp.where(half, a[:32], swap_halves(a[32:]))
        edge_bot[slot] = jnp.where(half, swap_halves(b[:32]), b[32:])

    def wait_bytes(ref, sem):
        pltpu.make_async_copy(ref, ref, sem).wait()

    def send(src, dst, send_sem, recv_sem, device):
        pltpu.make_async_remote_copy(
            src_ref=src, dst_ref=dst, send_sem=send_sem, recv_sem=recv_sem, device_id=device, device_id_type=MESH
        ).start()

    def send_tiles(slot, distances):
        for d in distances:
            send(own.at[slot], image.at[slot, 1:3, my_tile, :], x_send.at[slot], x_recv.at[slot], peer(d))
        image[slot, 1:3, my_tile, :] = own[slot]

    def send_edges(slot):
        pack_edges(slot)

        @pl.when(has_up)
        def _():
            for g in range(8):
                send(edge_top.at[slot], halo_bot.at[slot, my_edge, :], ht_send.at[slot], hb_recv.at[slot], above(g))

        @pl.when(has_down)
        def _():
            for g in range(8):
                send(edge_bot.at[slot], halo_top.at[slot, my_edge, :], hb_send.at[slot], ht_recv.at[slot], below(g))

    def broadcast(slot):
        send_edges(slot)
        send_tiles(slot, FAR_FIRST)

    def wait_tiles(slot):
        wait_bytes(image.at[slot, 1:3, 0:448, :], x_recv.at[slot])

    def wait_edges_sent(slot):
        @pl.when(has_up)
        def _():
            wait_bytes(halo_top.at[slot], ht_send.at[slot])

        @pl.when(has_down)
        def _():
            wait_bytes(halo_bot.at[slot], hb_send.at[slot])

    def wait_sent(slot):
        wait_bytes(image.at[slot, 1:3, 0:448, :], x_send.at[slot])
        wait_edges_sent(slot)

    my_half = pl.ds(pl.multiple_of(x_hi * 256, 256), 256)
    cross_tile = pl.ds(pl.multiple_of((1 - x_hi) * 256 + z * 64, 64), 64)

    def frame_first(t):
        slot = 2 + t
        send(
            own.at[slot, 1], image.at[slot, 2, my_tile, :], f_send.at[0, t], f_recv.at[0, t], peer(4)
        )
        send_tiles(slot, (2, 1, 3))

    def frame_second(t):
        slot = 2 + t
        wait_bytes(image.at[slot, 2, 0:64, :], f_recv.at[0, t])
        cross = image.at[slot, 2, cross_tile, :]
        for d in (2, 1, 3):
            send(cross, cross, f_send.at[1, t], f_recv.at[1, t], peer(d))
        wait_bytes(image.at[slot, 1:3, 0:192, :], x_recv.at[slot])
        half_ref = image.at[slot, 1, my_half, :]
        send(half_ref, half_ref, f_send.at[2, t], f_recv.at[2, t], peer(4))

    def frame_wait(t):
        slot = 2 + t
        wait_bytes(image.at[slot, 2, 0:192, :], f_recv.at[1, t])
        wait_bytes(image.at[slot, 1, 0:256, :], f_recv.at[2, t])

    def frame_edges(t):
        slot = 2 + t
        for g in range(8):
            first = slice(g * 64, g * 64 + 32)
            later = slice(g * 64 + 32, g * 64 + 64)
            rows = slice(g * 32, g * 32 + 32)
            frame_top[t, rows] = jnp.where(half, image[slot, 1, first], swap_halves(image[slot, 1, later]))
            frame_bot[t, rows] = jnp.where(half, swap_halves(image[slot, 2, first]), image[slot, 2, later])

        @pl.when(has_up)
        def _():
            send(frame_top.at[t], halo_bot.at[slot], ht_send.at[slot], hb_recv.at[slot], above_same)

        @pl.when(has_down)
        def _():
            send(frame_bot.at[t], halo_top.at[slot], hb_send.at[slot], ht_recv.at[slot], below_same)

    def wait_halos(slot):
        @pl.when(has_up)
        def _():
            wait_bytes(halo_top.at[slot], ht_recv.at[slot])

        @pl.when(has_down)
        def _():
            wait_bytes(halo_bot.at[slot], hb_recv.at[slot])

        for g in range(8):
            a0 = image[slot, 1, g * 64 : g * 64 + 32]
            a1 = image[slot, 1, g * 64 + 32 : g * 64 + 64]
            b0 = image[slot, 2, g * 64 : g * 64 + 32]
            b1 = image[slot, 2, g * 64 + 32 : g * 64 + 64]
            top = halo_top[slot, g * 32 : g * 32 + 32, :]
            bot = halo_bot[slot, g * 32 : g * 32 + 32, :]
            image[slot, 0, g * 64 : g * 64 + 32] = jnp.where(half, top, swap_halves(b0))
            image[slot, 0, g * 64 + 32 : g * 64 + 64] = swap_halves(jnp.where(half, b1, top))
            image[slot, 3, g * 64 : g * 64 + 32] = swap_halves(jnp.where(half, bot, a0))
            image[slot, 3, g * 64 + 32 : g * 64 + 64] = jnp.where(half, swap_halves(a1), bot)

    place = lax.rem(lax.broadcasted_iota(jnp.int32, (256, 128), 1), 64)

    def conv(slot, weight, write):
        def tap(p, q):
            lhs = weight[p, q].reshape(256, 512)
            rhs = jnp.concatenate([image[slot, p], image[slot, p + 1]], axis=1)
            return jnp.dot(lhs, rhs, preferred_element_type=F32)

        parts = [tap(1, q) for q in range(3)]
        wait_halos(slot)
        parts = [parts[q] + tap(0, q) + tap(2, q) for q in range(3)]
        for tile in range(2):
            lanes = slice(tile * 128, (tile + 1) * 128)
            left = jnp.where(place == 0, 0.0, pltpu.roll(parts[0][:, lanes], 1, 1))
            right = jnp.where(place == 63, 0.0, pltpu.roll(parts[2][:, lanes], 127, 1))
            write(tile, lanes, parts[1][:, lanes] + left + right)

    frame_first(0)
    broadcast(1)
    send_edges(2)
    start_trades((1, 2))
    for copy in trades:
        copy.start()
    frame_second(0)
    wait_trades((1, 2))
    frame_first(1)
    send_edges(3)
    weight_copies[0].wait()
    weight_copies[1].wait()
    for copy in trades:
        copy.wait_recv()

    def write_gin(tile, lanes, value):
        for c in range(2):
            rows = slice(c * 128, (c + 1) * 128)
            gin[rows, lanes] = value[rows] + bias_col[c]

    def update(next_slot):
        def write(tile, lanes, value):
            gates = value + gin[:, lanes]
            for c in range(2):
                z = [gates[c * 128 + k * 32 : c * 128 + (k + 1) * 32] for k in range(4)]
                new = jax.nn.sigmoid(z[1] + 1.0) * cell[c, :, lanes] + jax.nn.sigmoid(z[0]) * jnp.tanh(z[2])
                cell[c, :, lanes] = new
                own[next_slot, tile, c * 32 : (c + 1) * 32] = (jax.nn.sigmoid(z[3]) * jnp.tanh(new)).astype(BF16)

        return write

    def step(t, carry):
        slot = lax.rem(t + 1, 2)
        following = lax.rem(t, 2)

        frame_wait(t)

        @pl.when(t > 1)
        def _():
            frame_edges(t)

        @pl.when((t > 0) & (t < STEPS - 1))
        def _():
            frame_second(t + 1)

        @pl.when(t < STEPS - 2)
        def _():
            frame_first(t + 2)

        conv(2 + t, wi, write_gin)

        @pl.when(t == 0)
        def _():
            frame_second(t + 1)

        @pl.when(t > 0)
        def _():
            wait_sent(following)

        wait_tiles(slot)
        conv(slot, wh, update(following))

        @pl.when(t < STEPS - 1)
        def _():
            broadcast(following)

        return carry

    lax.fori_loop(0, STEPS, step, 0)

    last = (STEPS + 1) % 2
    windows = jnp.dot(own[last, 0], spread[0:128, :], preferred_element_type=F32)
    windows = (windows + jnp.dot(own[last, 1], spread[128:256, :], preferred_element_type=F32)).astype(BF16)
    for k in range(4):
        low = windows[:32, k * 128 : (k + 1) * 128]
        high = windows[32:, k * 128 : (k + 1) * 128]
        win_out[2 * k] = jnp.where(half, low, swap_halves(high))
        win_out[2 * k + 1] = jnp.where(half, swap_halves(low), high)

    @pl.when(has_up)
    def _():
        for k in range(8):
            device = above(k)
            send(win_out.at[device[1] // 2], win_in.at[2, my_edge, :], fin_send.at[0], fin_recv.at[0], device)

    @pl.when(has_down)
    def _():
        for k in range(8):
            device = below(k)
            send(win_out.at[device[1] // 2], win_in.at[0, my_edge, :], fin_send.at[1], fin_recv.at[1], device)

    for d in FAR_FIRST:
        device = peer(d)
        send(win_out.at[device[1] // 2], win_in.at[1, my_edge, :], fin_send.at[2], fin_recv.at[2], device)
    win_in[1, my_edge, :] = win_out[grp]

    def cell_copy(c, b):
        return pltpu.make_async_remote_copy(
            src_ref=cell.at[c], dst_ref=cell_back.at[b],
            send_sem=c2_send.at[c], recv_sem=c2_recv.at[b],
            device_id=trade(c), device_id_type=MESH,
        )

    for c in range(2):
        stays = (flip == 0) & (core == c)

        @pl.when(jnp.logical_not(stays))
        def _(c=c):
            cell_copy(c, core).start()

        @pl.when(stays)
        def _(c=c):
            cell_back[core] = cell[c]

    for copy in weight_copies[2:]:
        copy.wait()
    wait_bytes(win_in.at[1, 0:224, :], fin_recv.at[2])

    @pl.when(has_down)
    def _():
        wait_bytes(win_in.at[2], fin_recv.at[0])

    @pl.when(has_up)
    def _():
        wait_bytes(win_in.at[0], fin_recv.at[1])

    unit = lax.broadcasted_iota(jnp.int32, (128, 128), 0) == lax.broadcasted_iota(jnp.int32, (128, 128), 1)
    unit = jnp.where(unit, 1.0, 0.0).astype(BF16)

    def window(k, first, stop):
        turned = lax.dot_general(unit, win_in[k], (((1,), (1,)), ((), ())), preferred_element_type=F32).astype(BF16)
        return jnp.concatenate([turned[first:stop], turned[64 + first : 64 + stop]], axis=1)

    pixels = jnp.concatenate([window(0, 32, 64), window(1, 0, 64), window(2, 0, 32)], axis=0)

    def decode(source, rows, weight):
        parts = []
        for q in range(3):
            total = None
            for p in range(3):
                term = jnp.dot(source[p * 16 : p * 16 + rows * 16], weight(p, q), preferred_element_type=F32)
                total = term if total is None else total + term
            parts.append(total)
        return parts[1] + pltpu.roll(parts[0], 1, 0) + pltpu.roll(parts[2], rows * 16 - 1, 0)

    first = decode(pixels, 6, lambda p, q: w1[p, q].reshape(512, 512)) + bias1[...]
    first = first / (1.0 + jnp.exp(-first))
    pixel = lax.broadcasted_iota(jnp.int32, (96, 512), 0)
    image_row = block * 4 - 1 + pixel // 16
    image_col = grp * 8 - 2 + lax.rem(pixel, 16)
    inside = (image_row >= 0) & (image_row < 32) & (image_col >= 0) & (image_col < 64)
    middle = jnp.where(inside, first, 0.0).astype(BF16)
    second = decode(middle, 4, lambda p, q: w2[p, q]) + bias2[...]
    shifted = second.reshape(4, 16, 512)
    for c in range(2):
        dec_out[c] = shifted[:, 2 + 4 * c : 6 + 4 * c, :].astype(BF16)

    def dec_copy(c, b):
        return pltpu.make_async_remote_copy(
            src_ref=dec_out.at[c], dst_ref=dec_in.at[b],
            send_sem=d_send.at[c], recv_sem=d_recv.at[b],
            device_id=trade(c), device_id_type=MESH,
        )

    for c in range(2):
        stays = (flip == 0) & (core == c)

        @pl.when(jnp.logical_not(stays))
        def _(c=c):
            dec_copy(c, core).start()

        @pl.when(stays)
        def _(c=c):
            dec_in[core] = dec_out[c]

    for b in range(2):
        stays = (flip == 0) & (core == b)

        @pl.when(jnp.logical_not(stays))
        def _(b=b):
            cell_copy(0, b).wait_recv()

        for r in range(4):
            start = (r % 2) * 128 + (r // 2) * 64
            cell_out[b, r] = cell_back[b, :, start : start + 64]

    for t in range(STEPS):
        wait_bytes(image.at[2 + t, 1:3, 0:192, :], x_send.at[2 + t])
        wait_bytes(image.at[2 + t, 2, 0:64, :], f_send.at[0, t])
        wait_bytes(image.at[2 + t, 2, 0:192, :], f_send.at[1, t])
        wait_bytes(image.at[2 + t, 1, 0:256, :], f_send.at[2, t])
        wait_edges_sent(2 + t)
    wait_sent(1 - last)
    wait_bytes(win_in.at[1, 0:224, :], fin_send.at[2])

    @pl.when(has_up)
    def _():
        wait_bytes(win_in.at[0], fin_send.at[0])

    @pl.when(has_down)
    def _():
        wait_bytes(win_in.at[2], fin_send.at[1])

    for copy in trades:
        copy.wait_send()

    for b in range(2):
        stays = (flip == 0) & (core == b)

        @pl.when(jnp.logical_not(stays))
        def _(b=b):
            for k in range(3):
                trade_copy(k, core, b, my_rows).wait_send()
            cell_copy(b, core).wait_send()
            dec_copy(0, b).wait_recv()
            dec_copy(b, core).wait_send()

        decoded[b] = dec_in[b]


def give_out(decoded, cell, decoded_out, cell_out, sem):
    copies = [
        pltpu.make_async_copy(decoded, decoded_out, sem.at[0]),
        pltpu.make_async_copy(cell, cell_out, sem.at[1]),
    ]
    for copy in copies:
        copy.start()
    for copy in copies:
        copy.wait()


def per_device(
    frames, hidden_start, cell_start, input_weight, hidden_weight, gate_bias,
    first_weight, first_bias, second_weight, second_bias,
):
    vmem = pl.BlockSpec(memory_space=pltpu.VMEM)
    hbm = pl.BlockSpec(memory_space=pltpu.HBM)
    dma = pltpu.SemaphoreType.DMA
    slots = STEPS + 2

    def gate_rows(weight):
        return weight.transpose(0, 1, 3, 4, 2).reshape(3, 3, 128, 512)

    operands = (
        frames.transpose(0, 1, 2, 4, 3),
        hidden_start.transpose(0, 1, 3, 2),
        cell_start.transpose(0, 1, 3, 2),
        gate_bias,
        first_bias.reshape(1, -1),
        second_bias.reshape(1, -1),
        gate_rows(input_weight),
        gate_rows(hidden_weight),
        first_weight.reshape(3, 3, 8, 2, 32, 512),
        second_weight,
    )
    decoded, cell = pl.pallas_call(
        kernel,
        name="convlstm",
        out_shape=(
            jax.ShapeDtypeStruct((2, 4, 4, 512), BF16),
            jax.ShapeDtypeStruct((2, 4, 32, 64), F32),
        ),
        in_specs=[hbm] * 10,
        out_specs=(vmem, vmem),
        scratch_shapes=[
            pltpu.VMEM((STEPS, 2, 4, 32, 64), BF16),
            pltpu.VMEM((2, 4, 32, 64), BF16),
            pltpu.VMEM((2, 4, 32, 64), F32),
            pltpu.VMEM((4, 32), F32),
            pltpu.VMEM((1, 512), F32),
            pltpu.VMEM((1, 512), F32),
            pltpu.VMEM((2, STEPS + 1, 2, 32, 128), BF16),
            pltpu.VMEM((2, 32, 256), F32),
            pltpu.VMEM((slots, 2, 64, 128), BF16),
            pltpu.VMEM((4, 32, 128), BF16),
            pltpu.VMEM((4, 32, 128), BF16),
            pltpu.VMEM((slots, 4, 512, 128), BF16),
            pltpu.VMEM((slots, 256, 128), BF16),
            pltpu.VMEM((slots, 256, 128), BF16),
            pltpu.VMEM((256, 512), BF16),
            pltpu.VMEM((8, 32, 128), BF16),
            pltpu.VMEM((3, 256, 128), BF16),
            pltpu.VMEM((STEPS, 256, 128), BF16),
            pltpu.VMEM((STEPS, 256, 128), BF16),
            pltpu.VMEM((3, 3, 2, 128, 512), BF16),
            pltpu.VMEM((3, 3, 2, 128, 512), BF16),
            pltpu.VMEM((3, 3, 2, 8, 32, 512), BF16),
            pltpu.VMEM((3, 3, 512, 512), BF16),
            pltpu.VMEM((2, 128, 128), F32),
            pltpu.VMEM((2, 32, 256), F32),
            pltpu.VMEM((256, 256), F32),
            pltpu.VMEM((2, 4, 4, 512), BF16),
            pltpu.VMEM((2, 4, 4, 512), BF16),
            pltpu.VMEM((2, 32, 256), F32),
            dma((6,)), dma((5,)), dma((3,)), dma((3,)), dma((3, 2)), dma((3, 2)), dma((3, STEPS)), dma((3, STEPS)),
            dma((slots,)), dma((slots,)), dma((slots,)), dma((slots,)), dma((slots,)), dma((slots,)),
            dma((3,)), dma((3,)), dma((2,)), dma((2,)), dma((2,)), dma((2,)),
        ],
        compiler_params=pltpu.CompilerParams(
            collective_id=0, has_side_effects=True, vmem_limit_bytes=50 << 20
        ),
    )(
        *(pltpu.with_memory_space_constraint(array, pltpu.HBM) for array in operands)
    )
    decoded, cell = pl.pallas_call(
        give_out,
        name="give_out",
        out_shape=(
            jax.ShapeDtypeStruct((2, 4, 4, 512), BF16),
            jax.ShapeDtypeStruct((2, 4, 32, 64), F32),
        ),
        in_specs=[vmem, vmem],
        out_specs=(hbm, hbm),
        scratch_shapes=[dma((2,))],
        compiler_params=pltpu.CompilerParams(vmem_limit_bytes=1 << 20),
    )(decoded, cell)
    return decoded, cell.transpose(0, 1, 3, 2)


def solution(mesh):
    return jax.shard_map(
        per_device,
        mesh=mesh,
        in_specs=(
            P(None, None, "patch", None, "hid"),
            P(None, "patch", None, "hid"),
            P(None, "patch", None, "hid"),
            P(None, None, None, None, "hid"),
            P(None, None, None, None, "hid"),
            P(None, "hid"),
            P(),
            P(),
            P(),
            P(),
        ),
        out_specs=(P(None, "patch", "hid", None), P(None, "patch", None, "hid")),
        check_vma=False,
    )
```

```python
import jax
import jax.numpy as jnp
from jax import lax
from jax.experimental import pallas as pl
from jax.experimental.pallas import tpu as pltpu
from jax.sharding import PartitionSpec as P

STEPS = 4
FAR_FIRST = (6, 5, 7, 2, 4, 1, 3)
FAR_Z = (2, 1, 3, 0)
MESH = pl.DeviceIdType.MESH
F32 = jnp.float32
BF16 = jnp.bfloat16


def swap_halves(tile):
    return jnp.concatenate([tile[..., 64:], tile[..., :64]], axis=-1)


def kernel(
    frames_hbm, hidden_hbm, cell_hbm, gate_bias_hbm, bias1_hbm, bias2_hbm, w_in, w_hid, w_first, w_second,
    decoded, cell_out,
    frames, hidden, cell_in, gate_bias, bias1, bias2,
    packed, packed_cell, own, edge_top, edge_bot, image, halo_top, halo_bot,
    spread, win_out, win_in, frame_top, frame_bot,
    wi, wh, w1, w2, bias_col, cell, gin, dec_out, dec_in, cell_back,
    in_sem, w_sem, wx_send, wx_recv, s_send, s_recv, f_send, f_recv,
    x_send, x_recv, ht_send, ht_recv, hb_send, hb_recv, fin_send, fin_recv, c2_send, c2_recv, d_send, d_recv,
):
    patch = lax.axis_index("patch")
    hid = lax.axis_index("hid")
    core = lax.rem(hid, 2)
    grp = hid // 2
    x_hi = grp // 4
    y = patch // 2
    x_lo = lax.rem(patch, 2)
    flip = lax.rem(x_hi + y, 2)
    block = y * 2 + lax.rem(x_lo + flip, 2)

    def holder(blk, g, c):
        by = blk // 2
        lo = lax.rem(lax.rem(blk, 2) + g // 4 + by, 2)
        return (by * 2 + lo, g * 2 + c)

    def trade(c):
        return (y * 2 + lax.rem(x_lo + flip, 2), grp * 2 + c)

    has_up = block > 0
    has_down = block < 7
    sibling = (patch, grp * 2 + 1 - core)
    z = lax.rem(grp, 4)
    group_patch = [holder(block, g, 0)[0] for g in (0, 4)]
    up_patch = [holder(block - 1, g, 0)[0] for g in (0, 4)]
    down_patch = [holder(block + 1, g, 0)[0] for g in (0, 4)]
    cross_patch = jnp.where(x_hi == 0, group_patch[1], group_patch[0])

    def peer(d):
        hi = 1 - x_hi if d >= 4 else x_hi
        return (cross_patch if d >= 4 else patch, (hi * 4 + lax.rem(z + d % 4, 4)) * 2 + core)

    above_same = (jnp.where(x_hi == 0, up_patch[0], up_patch[1]), hid)
    below_same = (jnp.where(x_hi == 0, down_patch[0], down_patch[1]), hid)

    def above(k):
        return (up_patch[k % 2], (k % 2 * 4 + lax.rem(z + FAR_Z[k // 2], 4)) * 2 + core)

    def below(k):
        return (down_patch[k % 2], (k % 2 * 4 + lax.rem(z + FAR_Z[k // 2], 4)) * 2 + core)

    in_copies = []
    loads = (
        (frames_hbm, frames), (hidden_hbm, hidden), (cell_hbm, cell_in),
        (gate_bias_hbm, gate_bias), (bias1_hbm, bias1), (bias2_hbm, bias2),
    )
    for k, (src, dst) in enumerate(loads):
        copy = pltpu.make_async_copy(src, dst, in_sem.at[k])
        copy.start()
        in_copies.append(copy)

    barrier = pltpu.get_barrier_semaphore()

    def greet(device):
        pl.semaphore_signal(barrier, inc=1, device_id=device, device_id_type=MESH)

    @pl.when(has_up)
    def _():
        for g in range(8):
            greet(above(g))

    @pl.when(has_down)
    def _():
        for g in range(8):
            greet(below(g))

    for d in FAR_FIRST:
        greet(peer(d))

    greet(sibling)

    @pl.when(flip == 1)
    def _():
        greet(trade(0))
        greet(trade(1))

    weight_copies = []
    for k, (src, dst) in enumerate(((w_in, wi), (w_hid, wh))):
        copy = pltpu.make_async_copy(src, dst.at[:, :, core], w_sem.at[k])
        copy.start()
        weight_copies.append(copy)
    first_parts = [(w_first.at[:, :, :, k], w1.at[:, :, k]) for k in range(2)]
    for k, (src, dst) in enumerate((*first_parts, (w_second, w2))):
        copy = pltpu.make_async_copy(src, dst, w_sem.at[2 + k])
        copy.start()
        weight_copies.append(copy)

    for copy in in_copies:
        copy.wait()
    for b in range(2):
        for i in range(2):
            packed[b, 0, i] = jnp.concatenate([hidden[b, i], hidden[b, i + 2]], axis=-1)
            for t in range(STEPS):
                packed[b, 1 + t, i] = jnp.concatenate([frames[t, b, i], frames[t, b, i + 2]], axis=-1)
        packed_cell[b] = jnp.concatenate([cell_in[b, r] for r in (0, 2, 1, 3)], axis=-1)
    eye = lax.broadcasted_iota(jnp.int32, (32, 32), 0) == lax.broadcasted_iota(jnp.int32, (32, 32), 1)
    for k in range(4):
        column = jnp.sum(jnp.where(eye, gate_bias[k : k + 1, :], 0.0), axis=1, keepdims=True)
        bias_col[core, k * 32 : (k + 1) * 32, :] = jnp.broadcast_to(column, (32, 128))

    @pl.when(block == 0)
    def _():
        halo_top[...] = jnp.zeros_like(halo_top)
        win_in[0] = jnp.zeros_like(win_in[0])

    @pl.when(block == 7)
    def _():
        halo_bot[...] = jnp.zeros_like(halo_bot)
        win_in[2] = jnp.zeros_like(win_in[2])

    lane_in = lax.broadcasted_iota(jnp.int32, (256, 512), 0)
    lane_out = lax.broadcasted_iota(jnp.int32, (256, 512), 1)
    row_in = lane_in // 128 + 2 * (lax.rem(lane_in, 128) // 64)
    row_out = lax.rem(lane_out, 64) // 16
    col_out = lane_out // 64 * 8 - 2 + lax.rem(lane_out, 16)
    taken = (row_in == row_out) & (lax.rem(lane_in, 64) == col_out)
    spread[...] = jnp.where(taken, 1.0, 0.0).astype(BF16)

    greeted = 1 + 2 * flip + 7 + jnp.where(has_up, 8, 0) + jnp.where(has_down, 8, 0)
    pl.semaphore_wait(barrier, greeted)

    my_rows = pl.ds(pl.multiple_of(core * 32, 32), 32)

    def trade_copy(k, c, b, rows):
        src, dst = (
            (lambda: (packed.at[b, 0:2], own.at[1:3, :, rows, :])),
            (lambda: (packed.at[b, 2:5], own.at[3:6, :, rows, :])),
            (lambda: (packed_cell.at[b], cell.at[c])),
        )[k]()
        return pltpu.make_async_remote_copy(
            src_ref=src, dst_ref=dst, send_sem=s_send.at[k, b], recv_sem=s_recv.at[k, c],
            device_id=trade(b), device_id_type=MESH,
        )

    def start_trades(kinds):
        for b in range(2):
            stays = (flip == 0) & (core == b)

            @pl.when(jnp.logical_not(stays))
            def _(b=b):
                for k in kinds:
                    trade_copy(k, core, b, my_rows).start()

    def wait_trades(kinds):
        for c in range(2):
            stays = (flip == 0) & (core == c)

            @pl.when(jnp.logical_not(stays))
            def _(c=c):
                for k in kinds:
                    trade_copy(k, c, 0, pl.ds(c * 32, 32)).wait_recv()

    start_trades((0,))

    @pl.when(flip == 0)
    def _():
        own[1:6, :, my_rows, :] = packed[core]
        cell[core] = packed_cell[core]

    def weight_trade(k, src, dst):
        return pltpu.make_async_remote_copy(
            src_ref=src, dst_ref=dst, send_sem=wx_send.at[k], recv_sem=wx_recv.at[k],
            device_id=sibling, device_id_type=MESH,
        )

    trades = [
        weight_trade(0, w_in, wi.at[:, :, core]),
        weight_trade(1, w_hid, wh.at[:, :, core]),
        weight_trade(2, bias_col.at[core], bias_col.at[core]),
    ]
    wait_trades((0,))

    half = lax.broadcasted_iota(jnp.int32, (32, 128), 1) < 64
    my_tile = pl.ds(pl.multiple_of(grp * 64, 64), 64)
    my_edge = pl.ds(pl.multiple_of(grp * 32, 32), 32)

    def pack_edges(slot):
        a = own[slot, 0]
        b = own[slot, 1]
        edge_top[slot] = jnp.where(half, a[:32], swap_halves(a[32:]))
        edge_bot[slot] = jnp.where(half, swap_halves(b[:32]), b[32:])

    def wait_bytes(ref, sem):
        pltpu.make_async_copy(ref, ref, sem).wait()

    def send(src, dst, send_sem, recv_sem, device):
        pltpu.make_async_remote_copy(
            src_ref=src, dst_ref=dst, send_sem=send_sem, recv_sem=recv_sem, device_id=device, device_id_type=MESH
        ).start()

    def send_tiles(slot, distances):
        for d in distances:
            send(own.at[slot], image.at[slot, 1:3, my_tile, :], x_send.at[slot], x_recv.at[slot], peer(d))
        image[slot, 1:3, my_tile, :] = own[slot]

    def send_edges(slot):
        pack_edges(slot)

        @pl.when(has_up)
        def _():
            for g in range(8):
                send(edge_top.at[slot], halo_bot.at[slot, my_edge, :], ht_send.at[slot], hb_recv.at[slot], above(g))

        @pl.when(has_down)
        def _():
            for g in range(8):
                send(edge_bot.at[slot], halo_top.at[slot, my_edge, :], hb_send.at[slot], ht_recv.at[slot], below(g))

    def broadcast(slot):
        send_edges(slot)
        send_tiles(slot, FAR_FIRST)

    def wait_tiles(slot):
        wait_bytes(image.at[slot, 1:3, 0:448, :], x_recv.at[slot])

    def wait_edges_sent(slot):
        @pl.when(has_up)
        def _():
            wait_bytes(halo_top.at[slot], ht_send.at[slot])

        @pl.when(has_down)
        def _():
            wait_bytes(halo_bot.at[slot], hb_send.at[slot])

    def wait_sent(slot):
        wait_bytes(image.at[slot, 1:3, 0:448, :], x_send.at[slot])
        wait_edges_sent(slot)

    my_half = pl.ds(pl.multiple_of(x_hi * 256, 256), 256)
    cross_tile = pl.ds(pl.multiple_of((1 - x_hi) * 256 + z * 64, 64), 64)

    def frame_first(t):
        slot = 2 + t
        send(
            own.at[slot, 1], image.at[slot, 2, my_tile, :], f_send.at[0, t], f_recv.at[0, t], peer(4)
        )
        send_tiles(slot, (2, 1, 3))

    def frame_second(t):
        slot = 2 + t
        wait_bytes(image.at[slot, 2, 0:64, :], f_recv.at[0, t])
        cross = image.at[slot, 2, cross_tile, :]
        for d in (2, 1, 3):
            send(cross, cross, f_send.at[1, t], f_recv.at[1, t], peer(d))
        wait_bytes(image.at[slot, 1:3, 0:192, :], x_recv.at[slot])
        half_ref = image.at[slot, 1, my_half, :]
        send(half_ref, half_ref, f_send.at[2, t], f_recv.at[2, t], peer(4))

    def frame_wait(t):
        slot = 2 + t
        wait_bytes(image.at[slot, 2, 0:192, :], f_recv.at[1, t])
        wait_bytes(image.at[slot, 1, 0:256, :], f_recv.at[2, t])

    def frame_edges(t):
        slot = 2 + t
        for g in range(8):
            first = slice(g * 64, g * 64 + 32)
            later = slice(g * 64 + 32, g * 64 + 64)
            rows = slice(g * 32, g * 32 + 32)
            frame_top[t, rows] = jnp.where(half, image[slot, 1, first], swap_halves(image[slot, 1, later]))
            frame_bot[t, rows] = jnp.where(half, swap_halves(image[slot, 2, first]), image[slot, 2, later])

        @pl.when(has_up)
        def _():
            send(frame_top.at[t], halo_bot.at[slot], ht_send.at[slot], hb_recv.at[slot], above_same)

        @pl.when(has_down)
        def _():
            send(frame_bot.at[t], halo_top.at[slot], hb_send.at[slot], ht_recv.at[slot], below_same)

    def wait_halos(slot):
        @pl.when(has_up)
        def _():
            wait_bytes(halo_top.at[slot], ht_recv.at[slot])

        @pl.when(has_down)
        def _():
            wait_bytes(halo_bot.at[slot], hb_recv.at[slot])

        for g in range(8):
            a0 = image[slot, 1, g * 64 : g * 64 + 32]
            a1 = image[slot, 1, g * 64 + 32 : g * 64 + 64]
            b0 = image[slot, 2, g * 64 : g * 64 + 32]
            b1 = image[slot, 2, g * 64 + 32 : g * 64 + 64]
            top = halo_top[slot, g * 32 : g * 32 + 32, :]
            bot = halo_bot[slot, g * 32 : g * 32 + 32, :]
            image[slot, 0, g * 64 : g * 64 + 32] = jnp.where(half, top, swap_halves(b0))
            image[slot, 0, g * 64 + 32 : g * 64 + 64] = swap_halves(jnp.where(half, b1, top))
            image[slot, 3, g * 64 : g * 64 + 32] = swap_halves(jnp.where(half, bot, a0))
            image[slot, 3, g * 64 + 32 : g * 64 + 64] = jnp.where(half, swap_halves(a1), bot)

    place = lax.rem(lax.broadcasted_iota(jnp.int32, (256, 128), 1), 64)

    def conv(slot, weight, write):
        def tap(p, q):
            lhs = weight[p, q].reshape(256, 512)
            rhs = jnp.concatenate([image[slot, p], image[slot, p + 1]], axis=1)
            return jnp.dot(lhs, rhs, preferred_element_type=F32)

        parts = [tap(1, q) for q in range(3)]
        wait_halos(slot)
        parts = [parts[q] + tap(0, q) + tap(2, q) for q in range(3)]
        for tile in range(2):
            lanes = slice(tile * 128, (tile + 1) * 128)
            left = jnp.where(place == 0, 0.0, pltpu.roll(parts[0][:, lanes], 1, 1))
            right = jnp.where(place == 63, 0.0, pltpu.roll(parts[2][:, lanes], 127, 1))
            write(tile, lanes, parts[1][:, lanes] + left + right)

    frame_first(0)
    broadcast(1)
    send_edges(2)
    start_trades((1, 2))
    for copy in trades:
        copy.start()
    frame_second(0)
    wait_trades((1, 2))
    frame_first(1)
    send_edges(3)
    weight_copies[0].wait()
    weight_copies[1].wait()
    for copy in trades:
        copy.wait_recv()

    def write_gin(tile, lanes, value):
        for c in range(2):
            rows = slice(c * 128, (c + 1) * 128)
            gin[rows, lanes] = value[rows] + bias_col[c]

    def update(next_slot):
        def write(tile, lanes, value):
            gates = value + gin[:, lanes]
            for c in range(2):
                z = [gates[c * 128 + k * 32 : c * 128 + (k + 1) * 32] for k in range(4)]
                new = jax.nn.sigmoid(z[1] + 1.0) * cell[c, :, lanes] + jax.nn.sigmoid(z[0]) * jnp.tanh(z[2])
                cell[c, :, lanes] = new
                own[next_slot, tile, c * 32 : (c + 1) * 32] = (jax.nn.sigmoid(z[3]) * jnp.tanh(new)).astype(BF16)

        return write

    def step(t, carry):
        slot = lax.rem(t + 1, 2)
        following = lax.rem(t, 2)

        frame_wait(t)

        @pl.when(t > 1)
        def _():
            frame_edges(t)

        @pl.when((t > 0) & (t < STEPS - 1))
        def _():
            frame_second(t + 1)

        @pl.when(t < STEPS - 2)
        def _():
            frame_first(t + 2)

        conv(2 + t, wi, write_gin)

        @pl.when(t == 0)
        def _():
            frame_second(t + 1)

        @pl.when(t > 0)
        def _():
            wait_sent(following)

        wait_tiles(slot)
        conv(slot, wh, update(following))

        @pl.when(t < STEPS - 1)
        def _():
            broadcast(following)

        return carry

    lax.fori_loop(0, STEPS, step, 0)

    last = (STEPS + 1) % 2
    windows = jnp.dot(own[last, 0], spread[0:128, :], preferred_element_type=F32)
    windows = (windows + jnp.dot(own[last, 1], spread[128:256, :], preferred_element_type=F32)).astype(BF16)
    for k in range(4):
        low = windows[:32, k * 128 : (k + 1) * 128]
        high = windows[32:, k * 128 : (k + 1) * 128]
        win_out[2 * k] = jnp.where(half, low, swap_halves(high))
        win_out[2 * k + 1] = jnp.where(half, swap_halves(low), high)

    @pl.when(has_up)
    def _():
        for k in range(8):
            device = above(k)
            send(win_out.at[device[1] // 2], win_in.at[2, my_edge, :], fin_send.at[0], fin_recv.at[0], device)

    @pl.when(has_down)
    def _():
        for k in range(8):
            device = below(k)
            send(win_out.at[device[1] // 2], win_in.at[0, my_edge, :], fin_send.at[1], fin_recv.at[1], device)

    for d in FAR_FIRST:
        device = peer(d)
        send(win_out.at[device[1] // 2], win_in.at[1, my_edge, :], fin_send.at[2], fin_recv.at[2], device)
    win_in[1, my_edge, :] = win_out[grp]

    for copy in weight_copies[2:]:
        copy.wait()
    wait_bytes(win_in.at[1, 0:224, :], fin_recv.at[2])

    @pl.when(has_down)
    def _():
        wait_bytes(win_in.at[2], fin_recv.at[0])

    @pl.when(has_up)
    def _():
        wait_bytes(win_in.at[0], fin_recv.at[1])

    def cell_copy(c, b):
        return pltpu.make_async_remote_copy(
            src_ref=cell.at[c], dst_ref=cell_back.at[b],
            send_sem=c2_send.at[c], recv_sem=c2_recv.at[b],
            device_id=trade(c), device_id_type=MESH,
        )

    for c in range(2):
        stays = (flip == 0) & (core == c)

        @pl.when(jnp.logical_not(stays))
        def _(c=c):
            cell_copy(c, core).start()

        @pl.when(stays)
        def _(c=c):
            cell_back[core] = cell[c]

    unit = lax.broadcasted_iota(jnp.int32, (128, 128), 0) == lax.broadcasted_iota(jnp.int32, (128, 128), 1)
    unit = jnp.where(unit, 1.0, 0.0).astype(BF16)

    def window(k, first, stop):
        turned = lax.dot_general(unit, win_in[k], (((1,), (1,)), ((), ())), preferred_element_type=F32).astype(BF16)
        return jnp.concatenate([turned[first:stop], turned[64 + first : 64 + stop]], axis=1)

    pixels = jnp.concatenate([window(0, 32, 64), window(1, 0, 64), window(2, 0, 32)], axis=0)

    def decode(source, rows, weight):
        parts = []
        for q in range(3):
            total = None
            for p in range(3):
                term = jnp.dot(source[p * 16 : p * 16 + rows * 16], weight(p, q), preferred_element_type=F32)
                total = term if total is None else total + term
            parts.append(total)
        return parts[1] + pltpu.roll(parts[0], 1, 0) + pltpu.roll(parts[2], rows * 16 - 1, 0)

    first = decode(pixels, 6, lambda p, q: w1[p, q].reshape(512, 512)) + bias1[...]
    first = first / (1.0 + jnp.exp(-first))
    pixel = lax.broadcasted_iota(jnp.int32, (96, 512), 0)
    image_row = block * 4 - 1 + pixel // 16
    image_col = grp * 8 - 2 + lax.rem(pixel, 16)
    inside = (image_row >= 0) & (image_row < 32) & (image_col >= 0) & (image_col < 64)
    middle = jnp.where(inside, first, 0.0).astype(BF16)
    second = decode(middle, 4, lambda p, q: w2[p, q]) + bias2[...]
    shifted = second.reshape(4, 16, 512)
    for c in range(2):
        dec_out[c] = shifted[:, 2 + 4 * c : 6 + 4 * c, :].astype(BF16)

    def dec_copy(c, b):
        return pltpu.make_async_remote_copy(
            src_ref=dec_out.at[c], dst_ref=dec_in.at[b],
            send_sem=d_send.at[c], recv_sem=d_recv.at[b],
            device_id=trade(c), device_id_type=MESH,
        )

    for c in range(2):
        stays = (flip == 0) & (core == c)

        @pl.when(jnp.logical_not(stays))
        def _(c=c):
            dec_copy(c, core).start()

        @pl.when(stays)
        def _(c=c):
            dec_in[core] = dec_out[c]

    for b in range(2):
        stays = (flip == 0) & (core == b)

        @pl.when(jnp.logical_not(stays))
        def _(b=b):
            cell_copy(0, b).wait_recv()

        for r in range(4):
            start = (r % 2) * 128 + (r // 2) * 64
            cell_out[b, r] = cell_back[b, :, start : start + 64]

    for t in range(STEPS):
        wait_bytes(image.at[2 + t, 1:3, 0:192, :], x_send.at[2 + t])
        wait_bytes(image.at[2 + t, 2, 0:64, :], f_send.at[0, t])
        wait_bytes(image.at[2 + t, 2, 0:192, :], f_send.at[1, t])
        wait_bytes(image.at[2 + t, 1, 0:256, :], f_send.at[2, t])
        wait_edges_sent(2 + t)
    wait_sent(1 - last)
    wait_bytes(win_in.at[1, 0:224, :], fin_send.at[2])

    @pl.when(has_up)
    def _():
        wait_bytes(win_in.at[0], fin_send.at[0])

    @pl.when(has_down)
    def _():
        wait_bytes(win_in.at[2], fin_send.at[1])

    for copy in trades:
        copy.wait_send()

    for b in range(2):
        stays = (flip == 0) & (core == b)

        @pl.when(jnp.logical_not(stays))
        def _(b=b):
            for k in range(3):
                trade_copy(k, core, b, my_rows).wait_send()
            cell_copy(b, core).wait_send()
            dec_copy(0, b).wait_recv()
            dec_copy(b, core).wait_send()

        decoded[b] = dec_in[b]


def give_out(decoded, cell, decoded_out, cell_out, sem):
    copies = [
        pltpu.make_async_copy(decoded, decoded_out, sem.at[0]),
        pltpu.make_async_copy(cell, cell_out, sem.at[1]),
    ]
    for copy in copies:
        copy.start()
    for copy in copies:
        copy.wait()


def per_device(
    frames, hidden_start, cell_start, input_weight, hidden_weight, gate_bias,
    first_weight, first_bias, second_weight, second_bias,
):
    vmem = pl.BlockSpec(memory_space=pltpu.VMEM)
    hbm = pl.BlockSpec(memory_space=pltpu.HBM)
    dma = pltpu.SemaphoreType.DMA
    slots = STEPS + 2

    def gate_rows(weight):
        return weight.transpose(0, 1, 3, 4, 2).reshape(3, 3, 128, 512)

    operands = (
        frames.transpose(0, 1, 2, 4, 3),
        hidden_start.transpose(0, 1, 3, 2),
        cell_start.transpose(0, 1, 3, 2),
        gate_bias,
        first_bias.reshape(1, -1),
        second_bias.reshape(1, -1),
        gate_rows(input_weight),
        gate_rows(hidden_weight),
        first_weight.reshape(3, 3, 8, 2, 32, 512),
        second_weight,
    )
    decoded, cell = pl.pallas_call(
        kernel,
        name="convlstm",
        out_shape=(
            jax.ShapeDtypeStruct((2, 4, 4, 512), BF16),
            jax.ShapeDtypeStruct((2, 4, 32, 64), F32),
        ),
        in_specs=[hbm] * 10,
        out_specs=(vmem, vmem),
        scratch_shapes=[
            pltpu.VMEM((STEPS, 2, 4, 32, 64), BF16),
            pltpu.VMEM((2, 4, 32, 64), BF16),
            pltpu.VMEM((2, 4, 32, 64), F32),
            pltpu.VMEM((4, 32), F32),
            pltpu.VMEM((1, 512), F32),
            pltpu.VMEM((1, 512), F32),
            pltpu.VMEM((2, STEPS + 1, 2, 32, 128), BF16),
            pltpu.VMEM((2, 32, 256), F32),
            pltpu.VMEM((slots, 2, 64, 128), BF16),
            pltpu.VMEM((4, 32, 128), BF16),
            pltpu.VMEM((4, 32, 128), BF16),
            pltpu.VMEM((slots, 4, 512, 128), BF16),
            pltpu.VMEM((slots, 256, 128), BF16),
            pltpu.VMEM((slots, 256, 128), BF16),
            pltpu.VMEM((256, 512), BF16),
            pltpu.VMEM((8, 32, 128), BF16),
            pltpu.VMEM((3, 256, 128), BF16),
            pltpu.VMEM((STEPS, 256, 128), BF16),
            pltpu.VMEM((STEPS, 256, 128), BF16),
            pltpu.VMEM((3, 3, 2, 128, 512), BF16),
            pltpu.VMEM((3, 3, 2, 128, 512), BF16),
            pltpu.VMEM((3, 3, 2, 8, 32, 512), BF16),
            pltpu.VMEM((3, 3, 512, 512), BF16),
            pltpu.VMEM((2, 128, 128), F32),
            pltpu.VMEM((2, 32, 256), F32),
            pltpu.VMEM((256, 256), F32),
            pltpu.VMEM((2, 4, 4, 512), BF16),
            pltpu.VMEM((2, 4, 4, 512), BF16),
            pltpu.VMEM((2, 32, 256), F32),
            dma((6,)), dma((5,)), dma((3,)), dma((3,)), dma((3, 2)), dma((3, 2)), dma((3, STEPS)), dma((3, STEPS)),
            dma((slots,)), dma((slots,)), dma((slots,)), dma((slots,)), dma((slots,)), dma((slots,)),
            dma((3,)), dma((3,)), dma((2,)), dma((2,)), dma((2,)), dma((2,)),
        ],
        compiler_params=pltpu.CompilerParams(
            collective_id=0, has_side_effects=True, vmem_limit_bytes=50 << 20
        ),
    )(
        *(pltpu.with_memory_space_constraint(array, pltpu.HBM) for array in operands)
    )
    decoded, cell = pl.pallas_call(
        give_out,
        name="give_out",
        out_shape=(
            jax.ShapeDtypeStruct((2, 4, 4, 512), BF16),
            jax.ShapeDtypeStruct((2, 4, 32, 64), F32),
        ),
        in_specs=[vmem, vmem],
        out_specs=(hbm, hbm),
        scratch_shapes=[dma((2,))],
        compiler_params=pltpu.CompilerParams(vmem_limit_bytes=1 << 20),
    )(decoded, cell)
    return decoded, cell.transpose(0, 1, 3, 2)


def solution(mesh):
    return jax.shard_map(
        per_device,
        mesh=mesh,
        in_specs=(
            P(None, None, "patch", None, "hid"),
            P(None, "patch", None, "hid"),
            P(None, "patch", None, "hid"),
            P(None, None, None, None, "hid"),
            P(None, None, None, None, "hid"),
            P(None, "hid"),
            P(),
            P(),
            P(),
            P(),
        ),
        out_specs=(P(None, "patch", "hid", None), P(None, "patch", None, "hid")),
        check_vma=False,
    )
```
